128 devices in a mesh: gx: 16 (over z, y_hi, core), gy: 8 (over x, y_lo).
Axes of the slice: x: 4, y: 4 (y_hi: 2, y_lo: 2; y = y_hi * 2 + y_lo), z: 4, core: 2. Of those that a mesh axis runs over, the one named last changes fastest.
Arguments:
- density: float32 [512, 2048], P('gx', 'gy'), may hold values from 0.5 to 2
- momentum: float32 [3, 512, 2048], P(None, 'gx', 'gy'), may hold values from -0.6 to 0.6
- magnetic: float32 [3, 512, 2048], P(None, 'gx', 'gy'), may hold values from -0.6 to 0.6
- shear_shift: int32 [8], replicated, may hold values from 0 to 2047
- shear_frac: float32 [8], replicated, may hold values from 0 to 1
Outputs:
- density_next: float32 [512, 2048], P('gx', 'gy')
- momentum_next: float32 [3, 512, 2048], P(None, 'gx', 'gy')
- magnetic_next: float32 [3, 512, 2048], P(None, 'gx', 'gy')
The draws below stay inside these ranges and needn't reach their ends.
All inputs are finite; a program needn't handle non-finite values.
Results may differ from the reference program's by a relative error of at most 0.0003.
Values sent between devices are 32-bit elements; how exact they have to be, the bound alone decides.
A program may use at most 128 MiB of HBM per device.

```python
import math
import jax
import jax.numpy as jnp

STEPS = 8
HALO = 3
NX = 512
NY = 2048


def set_ends(result, key, smallest, high):
    longest = result.shape.index(max(result.shape))
    spots = []
    for shift in (0, 1):
        where = [jax.random.randint(jax.random.fold_in(key, axis), (), 0, length) for axis, length in enumerate(result.shape)]
        where[longest] = (where[longest] + shift) % result.shape[longest]
        spots.append(tuple(where))
    return result.at[spots[0]].set(smallest).at[spots[1]].set(high)


def block_scale(own_key, extent, shards, smallest, top_value):
    factor_of, own = 1.0, jax.random.fold_in(own_key, 6)
    for dim, shards_of in shards:
        steps = jnp.exp(jax.random.uniform(jax.random.fold_in(own, dim), (shards_of,), jnp.float32, smallest / len(shards), top_value / len(shards)))
        factor_of = factor_of * jnp.repeat(steps, extent[dim] // shards_of).reshape([-1 if axis == dim else 1 for axis in range(len(extent))])
    return factor_of


def normal_values(own_key, extent, deviation, bound, cuts=(), held_as=jnp.bfloat16):
    factor_of = block_scale(own_key, extent, cuts, -0.22, 0.18) if cuts else 1.0
    result = jax.random.normal(own_key, extent, jnp.float32) * deviation * factor_of
    return jnp.minimum(jnp.maximum(result, -bound), bound).astype(held_as)


def setup_inputs(seed: int = 0) -> dict:
    arg_keys = jax.random.split(jax.random.key(seed), 6)
    return {
        "density": jnp.clip(jnp.exp(math.log(2.0) - 1.3862944 * jax.random.uniform(arg_keys[0], (NX, NY), jnp.float32) ** block_scale(arg_keys[0], (NX, NY), ((0, 16), (1, 8)), -0.2, 0.2)), 0.5, 2.0),
        "momentum": normal_values(arg_keys[1], (3, NX, NY), 0.2, 0.6, ((1, 16), (2, 8)), jnp.float32),
        "magnetic": normal_values(arg_keys[2], (3, NX, NY), 0.2, 0.6, ((1, 16), (2, 8)), jnp.float32),
        "shear_shift": set_ends(jax.random.randint(arg_keys[3], (STEPS,), 0, NY), jax.random.fold_in(arg_keys[3], 1), 0, NY - 1).astype(jnp.int32),
        "shear_frac": jnp.clip(jax.random.uniform(arg_keys[4], (STEPS,), jnp.float32, 0.0, 1.0), 0.0, 1.0),
    }


SOUND_SQ = 1.0
OMEGA = 0.5
QSHEAR = 1.5
TIMESTEP = 0.1

def displaced(values, along_x, along_y):
    return jnp.roll(values, (-along_x, -along_y), (0, 1))

def minmod(left_diff, right_diff):
    return 0.5 * (jnp.sign(left_diff) + jnp.sign(right_diff)) * jnp.minimum(jnp.abs(left_diff), jnp.abs(right_diff))

def physical(primitives, normal):
    density, vel_norm, vel_tran, vel_side, field_tran, field_side = primitives
    squared = normal * normal + field_tran * field_tran + field_side * field_side
    pressure = SOUND_SQ * density + 0.5 * squared
    conserved = (density, density * vel_norm, density * vel_tran, density * vel_side, field_tran, field_side)
    fluxes = (density * vel_norm, density * vel_norm * vel_norm + pressure - normal * normal, density * vel_norm * vel_tran - normal * field_tran, density * vel_norm * vel_side - normal * field_side, field_tran * vel_norm - normal * vel_tran, field_side * vel_norm - normal * vel_side)
    signal = jnp.abs(vel_norm) + jnp.sqrt(SOUND_SQ + squared / density)
    return (conserved, fluxes, signal)

def riemann(left_state, right_state, normal):
    cons_left, flux_left, signal_left = physical(left_state, normal)
    cons_right, flux_right, signal_right = physical(right_state, normal)
    fastest = jnp.maximum(signal_left, signal_right)
    return tuple((0.5 * (first_flux + second_flux) - 0.5 * fastest * (upper_cons - lower_cons) for first_flux, second_flux, lower_cons, upper_cons in zip(flux_left, flux_right, cons_left, cons_right)))

def face_states(primitives, along_x, along_y, accuracy):
    behind = tuple((displaced(quantity, -along_x, -along_y) for quantity in primitives))
    if accuracy == 1:
        return (behind, primitives)
    beyond = tuple((displaced(quantity, along_x, along_y) for quantity in primitives))
    gradients = tuple((minmod(quantity - minus_one, plus_one - quantity) for quantity, minus_one, plus_one in zip(primitives, behind, beyond)))
    left_state = tuple((displaced(quantity + 0.5 * gradient, -along_x, -along_y) for quantity, gradient in zip(primitives, gradients)))
    right_state = tuple((quantity - 0.5 * gradient for quantity, gradient in zip(primitives, gradients)))
    return (left_state, right_state)

def unchanged(corner):
    return corner

def evaluate(initial, current, factor, accuracy, repair):
    density, momentum_x, momentum_y, momentum_z, field_z, field_x, field_y = current
    velocity_x = momentum_x / density
    velocity_y = momentum_y / density
    velocity_z = momentum_z / density
    centre_x = 0.5 * (field_x + displaced(field_x, 1, 0))
    centre_y = 0.5 * (field_y + displaced(field_y, 0, 1))
    left_state, right_state = face_states((density, velocity_x, velocity_y, velocity_z, centre_y, field_z), 1, 0, accuracy)
    flux_x = riemann(left_state, right_state, field_x)
    left_state, right_state = face_states((density, velocity_y, velocity_x, velocity_z, centre_x, field_z), 0, 1, accuracy)
    flux_y = riemann(left_state, right_state, field_y)
    corner = 0.25 * (flux_y[4] + displaced(flux_y[4], -1, 0) - flux_x[4] - displaced(flux_x[4], 0, -1))
    corner = repair(corner)
    stride = factor * TIMESTEP

    def update(previous, along_x, along_y, source):
        return previous - stride * (displaced(along_x, 1, 0) - along_x + (displaced(along_y, 0, 1) - along_y)) + stride * source
    return (update(initial[0], flux_x[0], flux_y[0], 0.0), update(initial[1], flux_x[1], flux_y[2], 2.0 * OMEGA * momentum_y), update(initial[2], flux_x[2], flux_y[1], -(2.0 - QSHEAR) * OMEGA * momentum_x), update(initial[3], flux_x[3], flux_y[3], 0.0), update(initial[4], flux_x[5], flux_y[5], 0.0), initial[5] - stride * (displaced(corner, 0, 1) - corner), initial[6] + stride * (displaced(corner, 1, 0) - corner))

def extend(field, offset_cells, fraction):
    inner_rows = field[NX - HALO:]
    outer_rows = field[:HALO]
    inner = (1.0 - fraction) * jnp.roll(inner_rows, offset_cells, 1) + fraction * jnp.roll(inner_rows, offset_cells + 1, 1)
    outer = (1.0 - fraction) * jnp.roll(outer_rows, -offset_cells, 1) + fraction * jnp.roll(outer_rows, -offset_cells - 1, 1)
    radial = jnp.concatenate([inner, field, outer], 0)
    return jnp.concatenate([radial[:, NY - HALO:], radial, radial[:, :HALO]], 1)

def boundary(corner, offset_cells, fraction):
    columns = jnp.arange(NY + 1, dtype=jnp.int32)
    low_row = corner[HALO, HALO:HALO + NY + 1]
    high_row = corner[HALO + NX, HALO:HALO + NY + 1]
    from_high = high_row[:NY]
    from_low = low_row[:NY]
    remote_low = (1.0 - fraction) * from_high[(columns - offset_cells) % NY] + fraction * from_high[(columns - offset_cells - 1) % NY]
    remote_high = (1.0 - fraction) * from_low[(columns + offset_cells) % NY] + fraction * from_low[(columns + offset_cells + 1) % NY]
    corner = corner.at[HALO, HALO:HALO + NY + 1].set(0.5 * (low_row + remote_low))
    corner = corner.at[HALO + NX, HALO:HALO + NY + 1].set(0.5 * (high_row + remote_high))
    return corner

def reference(density, momentum, magnetic, shear_shift, shear_frac):
    fields = (density, momentum[0], momentum[1], momentum[2], magnetic[2], magnetic[0], magnetic[1])
    for step_index in range(STEPS):
        offset_cells = shear_shift[step_index]
        fraction = shear_frac[step_index]
        padded = tuple((extend(field, offset_cells, fraction) for field in fields))
        predicted = evaluate(padded, padded, 0.5, 1, unchanged)
        corrected = evaluate(padded, predicted, 1.0, 2, lambda corner: boundary(corner, offset_cells, fraction))
        fields = tuple((field[HALO:HALO + NX, HALO:HALO + NY] for field in corrected))
    return (fields[0], jnp.stack([fields[1], fields[2], fields[3]]), jnp.stack([fields[5], fields[6], fields[4]]))
```

```python
import functools

import jax
import jax.numpy as jnp
from jax import lax
from jax.experimental import pallas as pl
from jax.experimental.pallas import tpu as pltpu
from jax.sharding import PartitionSpec as P

STEPS = 8
OMEGA = 0.5
QSHEAR = 1.5
TIMESTEP = 0.1
MESH = pl.DeviceIdType.MESH

D, MX, MY, MZ, BZ, BX, BY = range(7)
VX, VY, VZ, CY, CX, QBZ = 1, 2, 3, 4, 5, 6
OWN = 4
GHOST = OWN
STRIP = OWN + 1
TILES = OWN + 2
LANES = 384


def roll(x, shift, axis):
    return pltpu.roll(x, shift % x.shape[axis], axis)


def row_iota(shape):
    return lax.broadcasted_iota(jnp.int32, shape, len(shape) - 2)


def lane_iota(shape):
    return lax.broadcasted_iota(jnp.int32, shape, len(shape) - 1)


def kernel(
    gxn, gyn, shift_ref, frac_ref, den, mom, mag, den_out, mom_out, mag_out,
    U, Q, M, QL, QR, FX, PART, FY4, SX4, EZ, NBX, NBY,
    pack_lo, pack_hi, recv_lo, recv_hi, circ, ring, far, col_r, col_l,
    col_send, col_recv, row_send, row_recv, circ_send, circ_recv,
):
    gx = lax.axis_index("gx")
    gy = lax.axis_index("gy")
    at_low = gx == 0
    at_high = gx == gxn - 1
    at_end = jnp.logical_or(at_low, at_high)
    not_low = gx > 0
    not_high = gx < gxn - 1
    east = lax.rem(gy + 1, gyn)
    west = lax.rem(gy + gyn - 1, gyn)
    circle = 2 * gyn

    rows8 = row_iota((8, LANES))
    lanes8 = lane_iota((8, LANES))
    first_row = rows8 == 0
    last_row = rows8 == 7

    def previous(k):
        return STRIP if k == STRIP else (k + STRIP - 1) % STRIP

    def following(k):
        return STRIP if k == STRIP else (k + 1) % STRIP

    def row_before(before, here):
        return roll(jnp.where(last_row, before, here), 1, 0)

    def row_after(here, after):
        return roll(jnp.where(first_row, after, here), -1, 0)

    def lane_before(x):
        return roll(x, 1, 1)

    def lane_after(x):
        return roll(x, -1, 1)

    barrier = pltpu.get_barrier_semaphore()
    for partner in (east, west):
        pl.semaphore_signal(barrier, inc=1, device_id=(gx, partner), device_id_type=MESH)

    @pl.when(not_low)
    def _():
        pl.semaphore_signal(barrier, inc=1, device_id=(gx - 1, gy), device_id_type=MESH)

    @pl.when(not_high)
    def _():
        pl.semaphore_signal(barrier, inc=1, device_id=(gx + 1, gy), device_id_type=MESH)

    @pl.when(at_end)
    def _():
        other = gxn - 1 - gx
        for g in range(gyn):
            pl.semaphore_signal(barrier, inc=1, device_id=(other, g), device_id_type=MESH)

    def source_rows(field, k):
        rows = pl.ds(8 * k, 8)
        if field == D:
            return den[rows, :]
        if field in (MX, MY, MZ):
            return mom[field - MX, rows, :]
        return mag[{BX: 0, BY: 1, BZ: 2}[field], rows, :]

    for field in range(7):
        for k in range(OWN):
            U[field, k, :, 0:256] = source_rows(field, k)

    pl.semaphore_wait(barrier, jnp.where(at_end, 3 + gyn, 4))

    to_west = pltpu.make_async_remote_copy(
        src_ref=U.at[:, 0:OWN, :, 0:128], dst_ref=col_r, send_sem=col_send.at[0], recv_sem=col_recv.at[0],
        device_id=(gx, west), device_id_type=MESH,
    )
    to_east = pltpu.make_async_remote_copy(
        src_ref=U.at[:, 0:OWN, :, 128:256], dst_ref=col_l, send_sem=col_send.at[1], recv_sem=col_recv.at[1],
        device_id=(gx, east), device_id_type=MESH,
    )
    to_west.start()
    to_east.start()
    to_west.wait()
    to_east.wait()
    near = lane_iota((8, 128)) < 64
    for field in range(7):
        for k in range(OWN):
            U[field, k, :, 256:384] = jnp.where(near, col_r[field, k], col_l[field, k])
        for k in (GHOST, STRIP):
            U[field, k] = U[field, 0]

    def packed(tiles, first):
        def at(field, row):
            return tiles[field] if row == first else roll(tiles[field], row - first, 0)

        return (
            jnp.where(rows8 < 3, at(0, 0), jnp.where(rows8 < 6, at(1, 3), at(6, 6))),
            jnp.where(rows8 < 3, at(2, 0), jnp.where(rows8 < 6, at(3, 3), at(6, 4))),
            jnp.where(rows8 < 3, at(4, 0), at(5, 3)),
        )

    def unpacked(tiles, first):
        def move(x, row):
            return x if row == first else roll(x, first - row, 0)

        sixth = jnp.where(rows8 < first + 2, move(tiles[0], 6), move(tiles[1], 4))
        return (
            move(tiles[0], 0), move(tiles[0], 3), move(tiles[1], 0), move(tiles[1], 3),
            move(tiles[2], 0), move(tiles[2], 3), sixth,
        )

    def store_pack(ref, slot, tiles):
        for part in range(3):
            for lane in range(3):
                ref[slot, lane, part] = tiles[part][:, 128 * lane : 128 * (lane + 1)]

    def load_pack(ref, slot):
        return [jnp.concatenate([ref[slot, lane, part] for lane in range(3)], axis=1) for part in range(3)]

    ghost_above = rows8 < 3
    ghost_below = rows8 >= 5

    def minmod(a, b):
        return jnp.maximum(jnp.minimum(a, b), 0.0) + jnp.minimum(jnp.maximum(a, b), 0.0)

    def signal(density, speed, squared):
        total = density + squared
        return jnp.abs(speed) + jnp.abs(total) * lax.rsqrt(total * density)

    def riemann(left, right, normal, wanted):
        dl, vnl, vtl, vsl, btl, bsl = left
        dr, vnr, vtr, vsr, btr, bsr = right
        n2 = normal * normal
        tl = btl * btl + bsl * bsl
        tr = btr * btr + bsr * bsr
        fastest = jnp.maximum(signal(dl, vnl, n2 + tl), signal(dr, vnr, n2 + tr))
        out = {}
        if 0 in wanted or 1 in wanted or 2 in wanted or 3 in wanted:
            ml = dl * vnl
            mr = dr * vnr
        if 0 in wanted:
            out[0] = ml + mr - fastest * (dr - dl)
        if 1 in wanted:
            out[1] = (ml * vnl + mr * vnr) + (dl + dr) + 0.5 * (tl + tr) - n2 - fastest * (mr - ml)
        if 2 in wanted:
            out[2] = (ml * vtl + mr * vtr) - normal * (btl + btr) - fastest * (dr * vtr - dl * vtl)
        if 3 in wanted:
            out[3] = (ml * vsl + mr * vsr) - normal * (bsl + bsr) - fastest * (dr * vsr - dl * vsl)
        if 4 in wanted:
            out[4] = (btl * vnl + btr * vnr) - normal * (vtl + vtr) - fastest * (btr - btl)
        if 5 in wanted:
            out[5] = (bsl * vnl + bsr * vnr) - normal * (vsl + vsr) - fastest * (bsr - bsl)
        return out

    def primitives(k, density, mx, my, mz, bz, bx, bx_after, by):
        inverse = 1.0 / density
        Q[0, k] = density
        Q[VX, k] = mx * inverse
        Q[VY, k] = my * inverse
        Q[VZ, k] = mz * inverse
        Q[CX, k] = 0.5 * (bx + row_after(bx, bx_after))
        Q[CY, k] = 0.5 * (by + lane_after(by))
        Q[QBZ, k] = bz

    def initial_primitives(k):
        primitives(k, *(U[f, k] for f in (D, MX, MY, MZ, BZ, BX)), U[BX, following(k)], U[BY, k])

    X_STATE = (0, VX, VY, VZ, CY, QBZ)
    Y_STATE = (0, VY, VX, VZ, CX, QBZ)

    def finish_fluxes(k, fx, fy, stride, mx, my, cells):
        half = 0.5 * stride
        if 0 in fx:
            for spot, part in enumerate((0, 1, 2, 3, 5)):
                FX[spot, k] = fx[part]
        FY4[k] = fy[4]
        SX4[k] = fx[4] + lane_before(fx[4])
        if cells:
            for spot, (field, px, py) in enumerate(((D, 0, 0), (MX, 1, 2), (MY, 2, 1), (MZ, 3, 3), (BZ, 5, 5))):
                value = U[field, k] - half * ((lane_after(fy[py]) - fy[py]) - fx[px])
                if field == MX:
                    value += (stride * 2.0 * OMEGA) * my
                if field == MY:
                    value -= (stride * (2.0 - QSHEAR) * OMEGA) * mx
                PART[spot, k] = value

    ALL = (0, 1, 2, 3, 4, 5)

    def first_order(k, stride):
        left = [row_before(Q[i, previous(k)], Q[i, k]) for i in X_STATE]
        fx = riemann(left, [Q[i, k] for i in X_STATE], U[BX, k], ALL)
        right = [Q[i, k] for i in Y_STATE]
        fy = riemann([lane_before(q) for q in right], right, U[BY, k], ALL)
        finish_fluxes(k, fx, fy, stride, U[MX, k], U[MY, k], True)

    def slopes(k):
        for spot, i in enumerate(X_STATE):
            here = Q[i, k]
            gradient = 0.5 * minmod(here - row_before(Q[i, previous(k)], here), row_after(here, Q[i, following(k)]) - here)
            QL[spot, k] = here + gradient
            QR[spot, k] = here - gradient

    def second_order(k, stride):
        cells = k < OWN
        x_wanted = ALL if k < STRIP else (4,)
        y_wanted = ALL if cells else (4,)
        left = [row_before(QL[i, previous(k)], QL[i, k]) for i in range(6)]
        fx = riemann(left, [QR[i, k] for i in range(6)], NBX[k], x_wanted)
        left, right = [], []
        for i in Y_STATE:
            here = Q[i, k]
            behind = here - lane_before(here)
            gradient = 0.5 * minmod(behind, lane_after(behind))
            left.append(lane_before(here + gradient))
            right.append(here - gradient)
        fy = riemann(left, right, NBY[k], y_wanted)
        finish_fluxes(k, fx, fy, stride, M[0, k], M[1, k], cells)

    def corner(k):
        return 0.125 * (FY4[k] + row_before(FY4[previous(k)], FY4[k]) - SX4[k])

    def face_x(k, emf, stride):
        EZ[k] = emf
        return U[BX, k] - stride * (lane_after(emf) - emf)

    def face_y(k, stride):
        emf = EZ[k]
        return U[BY, k] + stride * (row_after(emf, EZ[following(k)]) - emf)

    def cells_of(k, stride):
        return [PART[i, k] - (0.5 * stride) * row_after(FX[i, k], FX[i, following(k)]) for i in range(5)]

    def tiles(run, *ends):
        for k in range(STRIP):
            run(k)
        if ends:

            @pl.when(at_end)
            def _():
                run(STRIP)

    def step(n, carry):
        slot = lax.rem(n, 2)
        fraction = frac_ref[n]
        shift = shift_ref[n]

        store_pack(pack_lo, slot, packed([U[f, 0] for f in range(7)], 0))
        store_pack(pack_hi, slot, packed([U[f, OWN - 1] for f in range(7)], 5))

        def to_far(pack, g):
            return pltpu.make_async_remote_copy(
                src_ref=pack.at[slot, 0:2], dst_ref=circ.at[slot, pl.ds(2 * gy, 2)],
                send_sem=circ_send.at[g], recv_sem=circ_recv.at[slot, gy],
                device_id=(gxn - 1 - gx, g), device_id_type=MESH,
            )

        def from_far(g):
            return pltpu.make_async_remote_copy(
                src_ref=pack_lo.at[slot, 0:2], dst_ref=circ.at[slot, pl.ds(2 * g, 2)],
                send_sem=circ_send.at[g], recv_sem=circ_recv.at[slot, g],
                device_id=(gxn - 1 - gx, g), device_id_type=MESH,
            )

        down = pltpu.make_async_remote_copy(
            src_ref=pack_lo.at[slot], dst_ref=recv_hi.at[slot], send_sem=row_send.at[0], recv_sem=row_recv.at[slot, 0],
            device_id=(lax.max(gx - 1, 0), gy), device_id_type=MESH,
        )
        up = pltpu.make_async_remote_copy(
            src_ref=pack_hi.at[slot], dst_ref=recv_lo.at[slot], send_sem=row_send.at[1], recv_sem=row_recv.at[slot, 1],
            device_id=(lax.min(gx + 1, gxn - 1), gy), device_id_type=MESH,
        )

        @pl.when(at_low)
        def _():
            for g in range(gyn):
                to_far(pack_lo, g).start()

        @pl.when(at_high)
        def _():
            for g in range(gyn):
                to_far(pack_hi, g).start()

        @pl.when(not_low)
        def _():
            down.start()

        @pl.when(not_high)
        def _():
            up.start()

        @pl.when(not_high)
        def _():
            down.wait_recv()
            for f, tile in enumerate(unpacked(load_pack(recv_hi, slot), 0)):
                U[f, GHOST] = jnp.where(ghost_above, tile, U[f, GHOST])

        @pl.when(not_low)
        def _():
            up.wait_recv()
            for f, tile in enumerate(unpacked(load_pack(recv_lo, slot), 5)):
                U[f, GHOST] = jnp.where(ghost_below, tile, U[f, GHOST])

        @pl.when(at_end)
        def _():
            for g in range(gyn):
                from_far(g).wait_recv()
            for place in range(circle):
                for part in range(3):
                    ring[place, part] = circ[slot, place, part]
            moved = jnp.where(at_low, -shift, shift)
            origin = lax.rem(gy * 256 + moved + 256 * gyn, 256 * gyn)
            lane_tile = lax.div(origin, 128)
            offset = lax.rem(origin, 128)
            turn = lax.rem(128 - offset, 128)
            inside = lane_iota((8, 128)) < 128 - offset
            for part in range(3):
                turned = []
                for i in range(5):
                    place = lax.rem(lane_tile + (circle - 1 + i), circle)
                    turned.append(pltpu.roll(ring[place, part], turn, 1))
                spans = [jnp.where(inside, a, b) for a, b in zip(turned[:-1], turned[1:])]
                far[part, :, 0:128] = spans[1]
                far[part, :, 128:256] = spans[2]
                far[part, :, 256:384] = jnp.where(near, spans[3], spans[0])

        def blended(x, towards):
            return (1.0 - fraction) * x + fraction * roll(x, -towards, 1)

        @pl.when(at_low)
        def _():
            raw = [far[part] for part in range(3)]
            for f, tile in enumerate(unpacked([blended(x, -1) for x in raw], 5)):
                U[f, GHOST] = jnp.where(ghost_below, tile, U[f, GHOST])
            for f, tile in enumerate(unpacked(raw, 0)):
                own = roll(blended(U[f, 0], 1), 3, 0)
                U[f, STRIP] = jnp.where(ghost_above, tile, own)

        @pl.when(at_high)
        def _():
            raw = [far[part] for part in range(3)]
            for f, tile in enumerate(unpacked([blended(x, 1) for x in raw], 0)):
                U[f, GHOST] = jnp.where(ghost_above, tile, U[f, GHOST])
            for f, tile in enumerate(unpacked(raw, 3)):
                own = roll(blended(U[f, OWN - 1], -1), 3, 0)
                U[f, STRIP] = jnp.where(ghost_above, own, tile)

        stride = 0.5 * TIMESTEP
        tiles(initial_primitives, True)
        tiles(lambda k: first_order(k, stride), True)

        def predicted_x(k):
            NBX[k] = face_x(k, corner(k), stride)

        tiles(predicted_x, True)

        def predicted_cells(k):
            density, mx, my, mz, bz = cells_of(k, stride)
            by = face_y(k, stride)
            NBY[k] = by
            M[0, k] = mx
            M[1, k] = my
            primitives(k, density, mx, my, mz, bz, NBX[k], NBX[following(k)], by)

        tiles(predicted_cells, True)

        tiles(slopes, True)
        tiles(lambda k: second_order(k, TIMESTEP), True)

        @pl.when(at_end)
        def _():
            EZ[STRIP] = corner(STRIP)

        emf_strip = EZ[STRIP]
        towards = jnp.where(at_low, lane_before(emf_strip), lane_after(emf_strip))
        remote = (1.0 - fraction) * emf_strip + fraction * towards
        remote = roll(remote, -3, 0)
        for k in range(STRIP):
            emf = corner(k)
            if k in (0, GHOST):
                ours = at_low if k == 0 else at_high
                fixed = jnp.where(first_row, 0.5 * (emf + remote), emf)
                emf = jnp.where(ours, fixed, emf)
            new_bx = face_x(k, emf, TIMESTEP)
            if k < OWN:
                U[BX, k] = new_bx
        for k in range(OWN):
            for field, value in zip((D, MX, MY, MZ, BZ), cells_of(k, TIMESTEP)):
                U[field, k] = value
            U[BY, k] = face_y(k, TIMESTEP)

        @pl.when(at_low)
        def _():
            for g in range(gyn):
                to_far(pack_lo, g).wait_send()

        @pl.when(at_high)
        def _():
            for g in range(gyn):
                to_far(pack_hi, g).wait_send()

        @pl.when(not_low)
        def _():
            down.wait_send()

        @pl.when(not_high)
        def _():
            up.wait_send()

        return carry

    EZ[STRIP] = jnp.zeros((8, LANES), jnp.float32)
    lax.fori_loop(0, STEPS, step, 0)

    for k in range(OWN):
        rows = pl.ds(8 * k, 8)
        den_out[rows, :] = U[D, k, :, 0:256]
        for i, field in enumerate((MX, MY, MZ)):
            mom_out[i, rows, :] = U[field, k, :, 0:256]
        for i, field in enumerate((BX, BY, BZ)):
            mag_out[i, rows, :] = U[field, k, :, 0:256]


def scratch(gyn):
    tile = (TILES, 8, LANES)
    f32 = jnp.float32
    vmem = lambda *shape: pltpu.VMEM(shape, f32)
    dma = pltpu.SemaphoreType.DMA
    return [
        vmem(7, *tile), vmem(7, *tile), vmem(2, *tile), vmem(6, *tile), vmem(6, *tile), vmem(5, *tile), vmem(5, *tile),
        vmem(*tile), vmem(*tile), vmem(*tile), vmem(*tile), vmem(*tile),
        vmem(2, 3, 3, 8, 128), vmem(2, 3, 3, 8, 128), vmem(2, 3, 3, 8, 128), vmem(2, 3, 3, 8, 128),
        vmem(2, 2 * gyn, 3, 8, 128), vmem(2 * gyn, 3, 8, 128), vmem(3, 8, LANES), vmem(7, OWN, 8, 128), vmem(7, OWN, 8, 128),
        dma((2,)), dma((2,)), dma((2,)), dma((2, 2)), dma((gyn,)), dma((2, gyn)),
    ]


def solution(mesh):
    gxn, gyn = mesh.shape["gx"], mesh.shape["gy"]

    def per_device(density, momentum, magnetic, shear_shift, shear_frac):
        return pl.pallas_call(
            functools.partial(kernel, gxn, gyn),
            name="shearing_box",
            out_shape=tuple(jax.ShapeDtypeStruct(a.shape, jnp.float32) for a in (density, momentum, magnetic)),
            in_specs=[pl.BlockSpec(memory_space=pltpu.SMEM)] * 2 + [pl.BlockSpec(memory_space=pltpu.VMEM)] * 3,
            out_specs=tuple(pl.BlockSpec(memory_space=pltpu.VMEM) for _ in range(3)),
            scratch_shapes=scratch(gyn),
            compiler_params=pltpu.CompilerParams(
                collective_id=0, has_side_effects=True, vmem_limit_bytes=32 * 1024 * 1024
            ),
        )(shear_shift, shear_frac, density, momentum, magnetic)

    return jax.shard_map(
        per_device,
        mesh=mesh,
        in_specs=(P("gx", "gy"), P(None, "gx", "gy"), P(None, "gx", "gy"), P(), P()),
        out_specs=(P("gx", "gy"), P(None, "gx", "gy"), P(None, "gx", "gy")),
        check_vma=False,
    )
```

```python
import functools

import jax
import jax.numpy as jnp
from jax import lax
from jax.experimental import pallas as pl
from jax.experimental.pallas import tpu as pltpu
from jax.sharding import PartitionSpec as P

STEPS = 8
OMEGA = 0.5
QSHEAR = 1.5
TIMESTEP = 0.1
MESH = pl.DeviceIdType.MESH

D, MX, MY, MZ, BX, BY, BZ = range(7)
VX, VY, VZ, CY, CX, QBZ = 1, 2, 3, 4, 5, 6
OWN = 4
ABOVE, BELOW = OWN, OWN + 1
RING = OWN + 2
AHEAD = (RING, RING + 1)
TILES = RING + 2
LANES = 384
PARTS = 6


def roll(x, shift, axis):
    return pltpu.roll(x, shift % x.shape[axis], axis)


def row_iota(shape):
    return lax.broadcasted_iota(jnp.int32, shape, len(shape) - 2)


def lane_iota(shape):
    return lax.broadcasted_iota(jnp.int32, shape, len(shape) - 1)


def kernel(
    gxn, gyn, shift_in, frac_in, den, mom, mag, den_out, mom_out, mag_out,
    U, Q, M, QL, QR, FX, PART, FY4, SX4, EZ, NBX, NBY,
    pack_lo, pack_hi, recv_lo, recv_hi, diagonal, circ_far, circ_near, ring_far, ring_near, col_r, col_l,
    shift_ref, frac_ref, load_sem,
    col_send, col_recv, row_send, row_recv, dia_send, dia_recv, far_send, far_recv, near_send, near_recv,
):
    gx = lax.axis_index("gx")
    gy = lax.axis_index("gy")
    at_low = gx == 0
    at_high = gx == gxn - 1
    at_end = jnp.logical_or(at_low, at_high)
    not_low = gx > 0
    not_high = gx < gxn - 1
    below_gx = lax.max(gx - 1, 0)
    above_gx = lax.min(gx + 1, gxn - 1)
    other_end = gxn - 1 - gx
    east = lax.rem(gy + 1, gyn)
    west = lax.rem(gy + gyn - 1, gyn)
    circle = 2 * gyn

    rows8 = row_iota((8, LANES))
    first_row = rows8 == 0
    last_row = rows8 == 7
    near = lane_iota((8, 128)) < 64

    def previous(k):
        return sum(AHEAD) - k if k in AHEAD else (k + RING - 1) % RING

    def following(k):
        return sum(AHEAD) - k if k in AHEAD else (k + 1) % RING

    def row_before(before, here):
        return roll(jnp.where(last_row, before, here), 1, 0)

    def row_after(here, after):
        return roll(jnp.where(first_row, after, here), -1, 0)

    def lane_before(x):
        return roll(x, 1, 1)

    def lane_after(x):
        return roll(x, -1, 1)

    loads = [
        pltpu.make_async_copy(den, U.at[D, 0:OWN, :, 0:256], load_sem.at[0]),
        pltpu.make_async_copy(mom, U.at[MX : MZ + 1, 0:OWN, :, 0:256], load_sem.at[1]),
        pltpu.make_async_copy(mag, U.at[BX : BZ + 1, 0:OWN, :, 0:256], load_sem.at[2]),
        pltpu.make_async_copy(shift_in, shift_ref, load_sem.at[3]),
        pltpu.make_async_copy(frac_in, frac_ref, load_sem.at[4]),
    ]
    for load in loads:
        load.start()

    barrier = pltpu.get_barrier_semaphore()

    def greet(to_gx, to_gy):
        pl.semaphore_signal(barrier, inc=1, device_id=(to_gx, to_gy), device_id_type=MESH)

    @pl.when(at_end)
    def _():
        for g in range(gyn):
            greet(other_end, g)
        for i in range(1, gyn):
            greet(gx, lax.rem(gy + i, gyn))

    @pl.when(jnp.logical_not(at_end))
    def _():
        greet(gx, east)
        greet(gx, west)

    @pl.when(not_low)
    def _():
        for g in (west, gy, east):
            greet(below_gx, g)

    @pl.when(not_high)
    def _():
        for g in (west, gy, east):
            greet(above_gx, g)

    for load in loads:
        load.wait()

    def packed(tiles, first):
        def at(field, row):
            return tiles[field] if row == first else roll(tiles[field], row - first, 0)

        return [
            jnp.where(rows8 < 3, at(0, 0), jnp.where(rows8 < 6, at(1, 3), at(6, 6))),
            jnp.where(rows8 < 3, at(2, 0), jnp.where(rows8 < 6, at(3, 3), at(6, 4))),
            jnp.where(rows8 < 3, at(4, 0), at(5, 3)),
        ]

    def unpacked(tiles, first):
        def move(x, row):
            return x if row == first else roll(x, first - row, 0)

        sixth = jnp.where(((rows8 - first) & 7) < 2, move(tiles[0], 6), move(tiles[1], 4))
        return (
            move(tiles[0], 0), move(tiles[0], 3), move(tiles[1], 0), move(tiles[1], 3),
            move(tiles[2], 0), move(tiles[2], 3), sixth,
        )

    def pack_edge(ref, slot, k, outer, inner):
        tiles = [U[f, k] for f in range(7)]
        for part, tile in enumerate(packed(tiles, outer) + packed(tiles, inner)):
            for lane in range(3):
                ref[slot, lane, part] = tile[:, 128 * lane : 128 * (lane + 1)]

    def load_pack(ref, slot, parts):
        return [jnp.concatenate([ref[slot, lane, part] for lane in range(3)], axis=1) for part in parts]

    def pack_edges(slot):
        pack_edge(pack_lo, slot, 0, 0, 3)
        pack_edge(pack_hi, slot, OWN - 1, 5, 2)

    def to_far(pack, slot, g):
        return pltpu.make_async_remote_copy(
            src_ref=pack.at[slot, 0:2], dst_ref=circ_far.at[slot, pl.ds(2 * gy, 2)],
            send_sem=far_send.at[g], recv_sem=far_recv.at[slot, gy],
            device_id=(other_end, g), device_id_type=MESH,
        )

    def from_far(slot, g):
        return pltpu.make_async_remote_copy(
            src_ref=pack_lo.at[slot, 0:2], dst_ref=circ_far.at[slot, pl.ds(2 * g, 2)],
            send_sem=far_send.at[g], recv_sem=far_recv.at[slot, g],
            device_id=(other_end, g), device_id_type=MESH,
        )

    def to_near(pack, slot, i):
        return pltpu.make_async_remote_copy(
            src_ref=pack.at[slot, 0:2, 0:3], dst_ref=circ_near.at[slot, pl.ds(2 * gy, 2)],
            send_sem=near_send.at[i], recv_sem=near_recv.at[slot, i],
            device_id=(gx, lax.rem(gy + i, gyn)), device_id_type=MESH,
        )

    def from_near(slot, i):
        sender = lax.rem(gy + gyn - i, gyn)
        return pltpu.make_async_remote_copy(
            src_ref=pack_lo.at[slot, 0:2, 0:3], dst_ref=circ_near.at[slot, pl.ds(2 * sender, 2)],
            send_sem=near_send.at[i], recv_sem=near_recv.at[slot, i],
            device_id=(gx, sender), device_id_type=MESH,
        )

    def down(slot):
        return pltpu.make_async_remote_copy(
            src_ref=pack_lo.at[slot], dst_ref=recv_hi.at[slot], send_sem=row_send.at[0], recv_sem=row_recv.at[slot, 0],
            device_id=(below_gx, gy), device_id_type=MESH,
        )

    def up(slot):
        return pltpu.make_async_remote_copy(
            src_ref=pack_hi.at[slot], dst_ref=recv_lo.at[slot], send_sem=row_send.at[1], recv_sem=row_recv.at[slot, 1],
            device_id=(above_gx, gy), device_id_type=MESH,
        )

    def diagonals(pack, side, to_gx):
        return [
            pltpu.make_async_remote_copy(
                src_ref=pack.at[0, lane], dst_ref=diagonal.at[side, lane],
                send_sem=dia_send.at[side, lane], recv_sem=dia_recv.at[side, lane],
                device_id=(to_gx, g), device_id_type=MESH,
            )
            for lane, g in ((0, west), (1, east))
        ]

    def start_sends(slot):
        for end, pack in ((at_low, pack_lo), (at_high, pack_hi)):

            @pl.when(end)
            def _(pack=pack):
                for g in range(gyn):
                    to_far(pack, slot, g).start()
                for i in range(1, gyn):
                    to_near(pack, slot, i).start()

        @pl.when(not_low)
        def _():
            down(slot).start()

        @pl.when(not_high)
        def _():
            up(slot).start()

    def finish_sends(slot):
        @pl.when(at_end)
        def _():
            for g in range(gyn):
                to_far(pack_lo, slot, g).wait_send()
            for i in range(1, gyn):
                to_near(pack_lo, slot, i).wait_send()

        @pl.when(not_low)
        def _():
            down(slot).wait_send()

        @pl.when(not_high)
        def _():
            up(slot).wait_send()

    to_west = pltpu.make_async_remote_copy(
        src_ref=U.at[:, 0:OWN, :, 0:128], dst_ref=col_r, send_sem=col_send.at[0], recv_sem=col_recv.at[0],
        device_id=(gx, west), device_id_type=MESH,
    )
    to_east = pltpu.make_async_remote_copy(
        src_ref=U.at[:, 0:OWN, :, 128:256], dst_ref=col_l, send_sem=col_send.at[1], recv_sem=col_recv.at[1],
        device_id=(gx, east), device_id_type=MESH,
    )

    for field in range(7):
        for k in range(OWN):
            U[field, k, :, 256:384] = U[field, k, :, 0:128]
        for k in (ABOVE, BELOW) + AHEAD:
            U[field, k] = U[field, 0]
    pack_edges(0)
    pl.semaphore_wait(barrier, jnp.where(at_end, 2 * gyn + 2, 8))

    start_sends(0)

    @pl.when(not_low)
    def _():
        for copy in diagonals(pack_lo, 0, below_gx):
            copy.start()

    @pl.when(not_high)
    def _():
        for copy in diagonals(pack_hi, 1, above_gx):
            copy.start()

    to_west.start()
    to_east.start()

    def first_columns():
        to_west.wait()
        to_east.wait()
        for field in range(7):
            for k in range(OWN):
                U[field, k, :, 256:384] = jnp.where(near, col_r[field, k], col_l[field, k])
        for partner, side, pack, ref, sent_to in ((not_high, 0, pack_lo, recv_hi, not_low), (not_low, 1, pack_hi, recv_lo, not_high)):

            @pl.when(sent_to)
            def _(side=side, pack=pack):
                for copy in diagonals(pack, side, gx):
                    copy.wait_send()

            @pl.when(partner)
            def _(side=side, pack=pack, ref=ref):
                for copy in diagonals(pack, side, gx):
                    copy.wait_recv()
                for part in range(PARTS):
                    ref[0, 2, part] = jnp.where(near, diagonal[side, 0, part], diagonal[side, 1, part])

    def ghosts_of_neighbours(slot):
        @pl.when(not_high)
        def _():
            outer = unpacked(load_pack(recv_hi, slot, (0, 1, 2)), 0)
            inner = unpacked(load_pack(recv_hi, slot, (3, 4, 5)), 3)
            for f in range(7):
                U[f, ABOVE] = jnp.where(rows8 < 3, outer[f], inner[f])

        @pl.when(not_low)
        def _():
            outer = unpacked(load_pack(recv_lo, slot, (0, 1, 2)), 5)
            inner = unpacked(load_pack(recv_lo, slot, (3, 4, 5)), 2)
            for f in range(7):
                U[f, BELOW] = jnp.where(rows8 >= 5, outer[f], inner[f])

    def window(ring, parts, moved):
        origin = lax.rem(gy * 256 + moved + 512 * gyn, 256 * gyn)
        lane_tile = lax.div(origin, 128)
        offset = lax.rem(origin, 128)
        turn = lax.rem(128 - offset, 128)
        inside = lane_iota((8, 128)) < 128 - offset
        out = []
        for part in parts:
            turned = [
                pltpu.roll(ring[lax.rem(lane_tile + (circle - 1 + i), circle), part], turn, 1) for i in range(5)
            ]
            spans = [jnp.where(inside, a, b) for a, b in zip(turned[:-1], turned[1:])]
            out.append(jnp.concatenate([spans[1], spans[2], jnp.where(near, spans[3], spans[0])], axis=1))
        return out

    def blended(x, fraction, towards):
        return (1.0 - fraction) * x + fraction * roll(x, -towards, 1)

    def low_ghosts(f, raw, fraction):
        ghost = blended(raw, fraction, -1)
        far_rows = roll(raw, 1, 0)
        own = roll(blended(U[f, 0], fraction, 1), 1, 0)
        U[f, BELOW] = jnp.where(rows8 >= 5, ghost, jnp.where(first_row, far_rows, own))
        U[f, ABOVE] = jnp.where(rows8 >= 6, far_rows, U[f, ABOVE])

    def high_ghosts(f, raw, fraction):
        ghost = blended(raw, fraction, 1)
        far_rows = roll(raw, 6, 0)
        own = roll(blended(U[f, OWN - 1], fraction, -1), -2, 0)
        U[f, ABOVE] = jnp.where(rows8 < 3, ghost, jnp.where(rows8 < 6, own, far_rows))
        U[f, BELOW] = jnp.where(rows8 < 2, far_rows, U[f, BELOW])

    def ghosts_of_far_end(slot, n):
        @pl.when(at_end)
        def _():
            for i in range(1, gyn):
                from_near(slot, i).wait_recv()
            for g in range(gyn):
                from_far(slot, g).wait_recv()
            for place in range(circle):
                for part in range(PARTS):
                    ring_far[place, part] = circ_far[slot, place, part]

        shift, shift_next = shift_ref[n], shift_ref[n + 1]
        fraction = frac_ref[n]
        A, B = (0, 1, 2), (3, 4, 5)
        left, right = AHEAD

        def near_ring(pack):
            for place in range(circle):
                mine = lax.div(place + 0 * gy, 2) == gy
                for part in range(3):
                    ring_near[place, part] = jnp.where(mine, pack[slot, place % 2, part], circ_near[slot, place, part])

        @pl.when(at_low)
        def _():
            near_ring(pack_lo)
            for f, raw in enumerate(unpacked(window(ring_far, A, -shift), 5)):
                low_ghosts(f, raw, fraction)
            outer = window(ring_far, A, -shift_next)
            inner = unpacked(window(ring_far, B, -shift_next), 2)
            beyond = window(ring_near, A, shift - shift_next)
            rows_a = unpacked(outer, 5)
            ghost = unpacked([blended(x, fraction, 1) for x in beyond], 0)
            mirror = unpacked([blended(x, fraction, -1) for x in outer], 3)
            raw = unpacked(beyond, 6)
            for f in range(7):
                U[f, left] = jnp.where(first_row, raw[f], jnp.where(rows8 < 5, inner[f], rows_a[f]))
                U[f, right] = jnp.where(rows8 < 3, ghost[f], jnp.where(rows8 < 6, mirror[f], raw[f]))

        @pl.when(at_high)
        def _():
            near_ring(pack_hi)
            for f, raw in enumerate(unpacked(window(ring_far, A, shift), 0)):
                high_ghosts(f, raw, fraction)
            outer = window(ring_far, A, shift_next)
            inner = unpacked(window(ring_far, B, shift_next), 3)
            beyond = window(ring_near, A, shift_next - shift)
            rows_a = unpacked(outer, 0)
            ghost = unpacked([blended(x, fraction, -1) for x in beyond], 5)
            mirror = unpacked([blended(x, fraction, 1) for x in outer], 2)
            raw = unpacked(beyond, 7)
            for f in range(7):
                U[f, left] = jnp.where(rows8 < 2, raw[f], jnp.where(rows8 < 5, mirror[f], ghost[f]))
                U[f, right] = jnp.where(rows8 < 3, rows_a[f], jnp.where(last_row, raw[f], inner[f]))

    def ghosts_from_ahead(n):
        fraction = frac_ref[n]

        @pl.when(at_low)
        def _():
            for f in range(7):
                low_ghosts(f, U[f, AHEAD[0]], fraction)

        @pl.when(at_high)
        def _():
            for f in range(7):
                high_ghosts(f, U[f, AHEAD[1]], fraction)

    def minmod(a, b):
        return jnp.maximum(jnp.minimum(a, b), 0.0) + jnp.minimum(jnp.maximum(a, b), 0.0)

    def signal(density, speed, squared):
        total = density + squared
        return jnp.abs(speed) + jnp.abs(total) * lax.rsqrt(total * density)

    def riemann(left, right, normal, wanted):
        dl, vnl, vtl, vsl, btl, bsl = left
        dr, vnr, vtr, vsr, btr, bsr = right
        n2 = normal * normal
        tl = btl * btl + bsl * bsl
        tr = btr * btr + bsr * bsr
        fastest = jnp.maximum(signal(dl, vnl, n2 + tl), signal(dr, vnr, n2 + tr))
        ul = vnl + fastest
        ur = vnr - fastest
        out = {}
        if wanted != (4,):
            al = dl * ul
            ar = dr * ur
        if 0 in wanted:
            out[0] = al + ar
        if 1 in wanted:
            out[1] = (al * vnl + ar * vnr) + ((dl + dr) + (0.5 * (tl + tr) - n2))
        if 2 in wanted:
            out[2] = (al * vtl + ar * vtr) - normal * (btl + btr)
        if 3 in wanted:
            out[3] = (al * vsl + ar * vsr) - normal * (bsl + bsr)
        if 4 in wanted:
            out[4] = (btl * ul + btr * ur) - normal * (vtl + vtr)
        if 5 in wanted:
            out[5] = (bsl * ul + bsr * ur) - normal * (vsl + vsr)
        return out

    def primitives(k, density, mx, my, mz, bz, bx, bx_after, by):
        inverse = 1.0 / density
        Q[0, k] = density
        Q[VX, k] = mx * inverse
        Q[VY, k] = my * inverse
        Q[VZ, k] = mz * inverse
        Q[CX, k] = 0.5 * (bx + row_after(bx, bx_after))
        Q[CY, k] = 0.5 * (by + lane_after(by))
        Q[QBZ, k] = bz

    def initial_primitives(k):
        primitives(k, *(U[f, k] for f in (D, MX, MY, MZ, BZ, BX)), U[BX, following(k)], U[BY, k])

    X_STATE = (0, VX, VY, VZ, CY, QBZ)
    Y_STATE = (0, VY, VX, VZ, CX, QBZ)

    def finish_fluxes(k, fx, fy, stride, mx, my, cells):
        half = 0.5 * stride
        if 0 in fx:
            for spot, part in enumerate((0, 1, 2, 3, 5)):
                FX[spot, k] = fx[part]
        FY4[k] = fy[4]
        SX4[k] = fx[4] + lane_before(fx[4])
        if cells:
            for spot, (field, px, py) in enumerate(((D, 0, 0), (MX, 1, 2), (MY, 2, 1), (MZ, 3, 3), (BZ, 5, 5))):
                value = U[field, k] - half * ((lane_after(fy[py]) - fy[py]) - fx[px])
                if field == MX:
                    value += (stride * 2.0 * OMEGA) * my
                if field == MY:
                    value -= (stride * (2.0 - QSHEAR) * OMEGA) * mx
                PART[spot, k] = value

    ALL = (0, 1, 2, 3, 4, 5)

    def first_order(k, stride):
        left = [row_before(Q[i, previous(k)], Q[i, k]) for i in X_STATE]
        fx = riemann(left, [Q[i, k] for i in X_STATE], U[BX, k], ALL)
        right = [Q[i, k] for i in Y_STATE]
        fy = riemann([lane_before(q) for q in right], right, U[BY, k], ALL)
        finish_fluxes(k, fx, fy, stride, U[MX, k], U[MY, k], True)

    def slopes(k):
        for spot, i in enumerate(X_STATE):
            here = Q[i, k]
            gradient = 0.5 * minmod(here - row_before(Q[i, previous(k)], here), row_after(here, Q[i, following(k)]) - here)
            QL[spot, k] = here + gradient
            QR[spot, k] = here - gradient

    def second_order(k, stride, last):
        cells = k < OWN or not last
        x_wanted = ALL if cells or k == ABOVE else (4,)
        y_wanted = ALL if cells else (4,)
        left = [row_before(QL[i, previous(k)], QL[i, k]) for i in range(6)]
        fx = riemann(left, [QR[i, k] for i in range(6)], NBX[k], x_wanted)
        left, right = [], []
        for i in Y_STATE:
            here = Q[i, k]
            behind = here - lane_before(here)
            gradient = 0.5 * minmod(behind, lane_after(behind))
            left.append(lane_before(here + gradient))
            right.append(here - gradient)
        fy = riemann(left, right, NBY[k], y_wanted)
        finish_fluxes(k, fx, fy, stride, M[0, k], M[1, k], cells)

    def corner(k):
        return 0.125 * (FY4[k] + row_before(FY4[previous(k)], FY4[k]) - SX4[k])

    def face_x(k, emf, stride):
        EZ[k] = emf
        return U[BX, k] - stride * (lane_after(emf) - emf)

    def face_y(k, stride):
        emf = EZ[k]
        return U[BY, k] + stride * (row_after(emf, EZ[following(k)]) - emf)

    def cells_of(k, stride):
        return [PART[i, k] - (0.5 * stride) * row_after(FX[i, k], FX[i, following(k)]) for i in range(5)]

    def advance(n, last):
        fraction = frac_ref[n]

        def tiles(run):
            for k in range(RING):
                run(k)
            if not last:

                @pl.when(at_end)
                def _():
                    for k in AHEAD:
                        run(k)

        stride = 0.5 * TIMESTEP
        tiles(initial_primitives)
        tiles(lambda k: first_order(k, stride))

        def predicted_x(k):
            NBX[k] = face_x(k, corner(k), stride)

        tiles(predicted_x)

        def predicted_cells(k):
            density, mx, my, mz, bz = cells_of(k, stride)
            by = face_y(k, stride)
            NBY[k] = by
            M[0, k] = mx
            M[1, k] = my
            primitives(k, density, mx, my, mz, bz, NBX[k], NBX[following(k)], by)

        tiles(predicted_cells)

        tiles(slopes)
        tiles(lambda k: second_order(k, TIMESTEP, last))
        kept = range(OWN) if last else range(RING)

        def mended(emf, remote_row, towards, ours):
            remote = blended(remote_row, fraction, towards)
            return jnp.where(jnp.logical_and(first_row, ours), 0.5 * (emf + remote), emf)

        emfs = [corner(k) for k in range(RING)]
        low_fix = mended(emfs[0], roll(emfs[BELOW], -1, 0), -1, at_low)
        high_fix = mended(emfs[ABOVE], roll(emfs[ABOVE], -6, 0), 1, at_high)
        emfs[0], emfs[ABOVE] = low_fix, high_fix
        for k in range(RING):
            new_bx = face_x(k, emfs[k], TIMESTEP)
            if k in kept:
                U[BX, k] = new_bx

        def new_cells(k):
            for field, value in zip((D, MX, MY, MZ, BZ), cells_of(k, TIMESTEP)):
                U[field, k] = value
            U[BY, k] = face_y(k, TIMESTEP)

        for k in kept:
            new_cells(k)
        if not last:

            @pl.when(at_end)
            def _():
                left, right = AHEAD
                emf_l, emf_r = corner(left), corner(right)
                from_low = blended(roll(emf_r, -6, 0), fraction, 1)
                from_high = blended(roll(emf_l, -2, 0), fraction, -1)
                remote = jnp.where(at_low, from_low, from_high)
                emf_r = jnp.where(first_row, 0.5 * (emf_r + remote), emf_r)
                U[BX, left] = face_x(left, emf_l, TIMESTEP)
                U[BX, right] = face_x(right, emf_r, TIMESTEP)
                for k in AHEAD:
                    new_cells(k)

    rounds = STEPS // 2

    def two_steps(r, carry):
        slot = lax.rem(r, 2)

        @pl.when(not_high)
        def _():
            down(slot).wait_recv()

        @pl.when(not_low)
        def _():
            up(slot).wait_recv()

        @pl.when(r == 0)
        def _():
            first_columns()

        ghosts_of_neighbours(slot)
        ghosts_of_far_end(slot, 2 * r)
        advance(2 * r, False)
        ghosts_from_ahead(2 * r + 1)
        advance(2 * r + 1, True)
        finish_sends(slot)

        @pl.when(r < rounds - 1)
        def _():
            pack_edges(1 - slot)
            start_sends(1 - slot)

        return carry

    lax.fori_loop(0, rounds, two_steps, 0)

    for k in range(OWN):
        rows = pl.ds(8 * k, 8)
        den_out[rows, :] = U[D, k, :, 0:256]
        for i, field in enumerate((MX, MY, MZ)):
            mom_out[i, rows, :] = U[field, k, :, 0:256]
        for i, field in enumerate((BX, BY, BZ)):
            mag_out[i, rows, :] = U[field, k, :, 0:256]


def scratch(gyn):
    tile = (TILES, 8, LANES)
    f32 = jnp.float32
    vmem = lambda *shape: pltpu.VMEM(shape, f32)
    dma = pltpu.SemaphoreType.DMA
    return [
        vmem(7, *tile), vmem(7, *tile), vmem(2, *tile), vmem(6, *tile), vmem(6, *tile), vmem(5, *tile), vmem(5, *tile),
        vmem(*tile), vmem(*tile), vmem(*tile), vmem(*tile), vmem(*tile),
        *(vmem(2, 3, PARTS, 8, 128) for _ in range(4)), vmem(2, 2, PARTS, 8, 128),
        vmem(2, 2 * gyn, PARTS, 8, 128), vmem(2, 2 * gyn, 3, 8, 128),
        vmem(2 * gyn, PARTS, 8, 128), vmem(2 * gyn, 3, 8, 128), vmem(7, OWN, 8, 128), vmem(7, OWN, 8, 128),
        pltpu.SMEM((STEPS,), jnp.int32), pltpu.SMEM((STEPS,), f32), dma((5,)),
        dma((2,)), dma((2,)), dma((2,)), dma((2, 2)), dma((2, 2)), dma((2, 2)),
        dma((gyn,)), dma((2, gyn)), dma((gyn,)), dma((2, gyn)),
    ]


def solution(mesh):
    gxn, gyn = mesh.shape["gx"], mesh.shape["gy"]

    def per_device(density, momentum, magnetic, shear_shift, shear_frac):
        return pl.pallas_call(
            functools.partial(kernel, gxn, gyn),
            name="shearing_box",
            out_shape=tuple(jax.ShapeDtypeStruct(a.shape, jnp.float32) for a in (density, momentum, magnetic)),
            in_specs=[pl.BlockSpec(memory_space=pl.ANY)] * 5,
            out_specs=tuple(pl.BlockSpec(memory_space=pltpu.VMEM) for _ in range(3)),
            scratch_shapes=scratch(gyn),
            compiler_params=pltpu.CompilerParams(
                collective_id=0, has_side_effects=True, vmem_limit_bytes=48 * 1024 * 1024
            ),
        )(
            shear_shift,
            shear_frac,
            density.reshape(OWN, 8, 256),
            momentum.reshape(3, OWN, 8, 256),
            magnetic.reshape(3, OWN, 8, 256),
        )

    return jax.shard_map(
        per_device,
        mesh=mesh,
        in_specs=(P("gx", "gy"), P(None, "gx", "gy"), P(None, "gx", "gy"), P(), P()),
        out_specs=(P("gx", "gy"), P(None, "gx", "gy"), P(None, "gx", "gy")),
        check_vma=False,
    )
```

```python
import functools

import jax
import jax.numpy as jnp
from jax import lax
from jax.experimental import pallas as pl
from jax.experimental.pallas import tpu as pltpu
from jax.sharding import PartitionSpec as P

STEPS = 8
OMEGA = 0.5
QSHEAR = 1.5
TIMESTEP = 0.1
MESH = pl.DeviceIdType.MESH

D, MX, MY, MZ, BX, BY, BZ = range(7)
VX, VY, VZ, CY, CX, QBZ = 1, 2, 3, 4, 5, 6
OWN = 4
ABOVE, BELOW = OWN, OWN + 1
RING = OWN + 2
AHEAD = (RING, RING + 1)
TILES = RING + 2
LANES = 384
PARTS = 6


def roll(x, shift, axis):
    return pltpu.roll(x, shift % x.shape[axis], axis)


def row_iota(shape):
    return lax.broadcasted_iota(jnp.int32, shape, len(shape) - 2)


def lane_iota(shape):
    return lax.broadcasted_iota(jnp.int32, shape, len(shape) - 1)


def kernel(
    gxn, gyn, shift_in, frac_in, den, mom, mag, den_out, mom_out, mag_out,
    U, Q, M, QL, QR, FX, PART, FY4, SX4, EZ, NBX, NBY,
    pack_lo, pack_hi, recv_lo, recv_hi, block, circ_far, circ_near, ring_far, ring_near, col_r, col_l,
    shift_ref, frac_ref, load_sem,
    col_send, col_recv, row_send, row_recv, far_send, far_recv, near_send, near_recv,
):
    gx = lax.axis_index("gx")
    gy = lax.axis_index("gy")
    at_low = gx == 0
    at_high = gx == gxn - 1
    at_end = jnp.logical_or(at_low, at_high)
    not_low = gx > 0
    not_high = gx < gxn - 1
    below_gx = lax.max(gx - 1, 0)
    above_gx = lax.min(gx + 1, gxn - 1)
    other_end = gxn - 1 - gx
    east = lax.rem(gy + 1, gyn)
    west = lax.rem(gy + gyn - 1, gyn)

    rows8 = row_iota((8, LANES))
    first_row = rows8 == 0
    last_row = rows8 == 7
    near = lane_iota((8, 128)) < 64

    def previous(k):
        return sum(AHEAD) - k if k in AHEAD else (k + RING - 1) % RING

    def following(k):
        return sum(AHEAD) - k if k in AHEAD else (k + 1) % RING

    def row_before(before, here):
        return roll(jnp.where(last_row, before, here), 1, 0)

    def row_after(here, after):
        return roll(jnp.where(first_row, after, here), -1, 0)

    def lane_before(x):
        return jnp.concatenate([roll(x[:, 256:384], 1, 1), x[:, 0:128], x[:, 128:256]], axis=1)

    def lane_after(x):
        return jnp.concatenate([x[:, 128:256], x[:, 256:384], roll(x[:, 0:128], -1, 1)], axis=1)

    spots = lane_iota((8, LANES))
    columns = 3 * (spots & 127) + (spots >> 7)
    spot_of_row = lane_iota((LANES, LANES))
    permutation = jnp.where(row_iota((LANES, LANES)) == 3 * (spot_of_row & 127) + (spot_of_row >> 7), 1.0, 0.0)

    loads = [
        pltpu.make_async_copy(den, block.at[D], load_sem.at[0]),
        pltpu.make_async_copy(mom, block.at[MX : MZ + 1], load_sem.at[1]),
        pltpu.make_async_copy(mag, block.at[BX : BZ + 1], load_sem.at[2]),
        pltpu.make_async_copy(shift_in, shift_ref, load_sem.at[3]),
        pltpu.make_async_copy(frac_in, frac_ref, load_sem.at[4]),
    ]
    for load in loads:
        load.start()

    barrier = pltpu.get_barrier_semaphore()

    def greet(to_gx, to_gy):
        pl.semaphore_signal(barrier, inc=1, device_id=(to_gx, to_gy), device_id_type=MESH)

    @pl.when(at_end)
    def _():
        for g in range(gyn):
            greet(other_end, g)
        for i in range(1, gyn):
            greet(gx, lax.rem(gy + i, gyn))

    @pl.when(jnp.logical_not(at_end))
    def _():
        greet(gx, east)
        greet(gx, west)

    @pl.when(not_low)
    def _():
        greet(below_gx, gy)

    @pl.when(not_high)
    def _():
        greet(above_gx, gy)

    for load in loads:
        load.wait()

    def packed(tiles, first):
        def at(field, row):
            return tiles[field] if row == first else roll(tiles[field], row - first, 0)

        return [
            jnp.where(rows8 < 3, at(0, 0), jnp.where(rows8 < 6, at(1, 3), at(6, 6))),
            jnp.where(rows8 < 3, at(2, 0), jnp.where(rows8 < 6, at(3, 3), at(6, 4))),
            jnp.where(rows8 < 3, at(4, 0), at(5, 3)),
        ]

    def unpacked(tiles, first):
        def move(x, row):
            return x if row == first else roll(x, first - row, 0)

        sixth = jnp.where(((rows8 - first) & 7) < 2, move(tiles[0], 6), move(tiles[1], 4))
        return (
            move(tiles[0], 0), move(tiles[0], 3), move(tiles[1], 0), move(tiles[1], 3),
            move(tiles[2], 0), move(tiles[2], 3), sixth,
        )

    def pack_edge(ref, slot, k, outer, inner):
        tiles = [U[f, k] for f in range(7)]
        for part, tile in enumerate(packed(tiles, outer) + packed(tiles, inner)):
            for lane in range(3):
                ref[slot, lane, part] = tile[:, 128 * lane : 128 * (lane + 1)]

    def load_pack(ref, slot, parts):
        return [jnp.concatenate([ref[slot, lane, part] for lane in range(3)], axis=1) for part in parts]

    def pack_edges(slot):
        pack_edge(pack_lo, slot, 0, 0, 3)
        pack_edge(pack_hi, slot, OWN - 1, 5, 2)

    def to_far(pack, source, slot, g):
        return pltpu.make_async_remote_copy(
            src_ref=pack.at[source], dst_ref=circ_far.at[slot, gy],
            send_sem=far_send.at[g], recv_sem=far_recv.at[slot, gy],
            device_id=(other_end, g), device_id_type=MESH,
        )

    def from_far(slot, g):
        return pltpu.make_async_remote_copy(
            src_ref=pack_lo.at[slot], dst_ref=circ_far.at[slot, g],
            send_sem=far_send.at[g], recv_sem=far_recv.at[slot, g],
            device_id=(other_end, g), device_id_type=MESH,
        )

    def to_near(pack, source, slot, i):
        return pltpu.make_async_remote_copy(
            src_ref=pack.at[source, :, 0:3], dst_ref=circ_near.at[slot, gy],
            send_sem=near_send.at[i], recv_sem=near_recv.at[slot, i],
            device_id=(gx, lax.rem(gy + i, gyn)), device_id_type=MESH,
        )

    def from_near(slot, i):
        sender = lax.rem(gy + gyn - i, gyn)
        return pltpu.make_async_remote_copy(
            src_ref=pack_lo.at[slot, :, 0:3], dst_ref=circ_near.at[slot, sender],
            send_sem=near_send.at[i], recv_sem=near_recv.at[slot, i],
            device_id=(gx, sender), device_id_type=MESH,
        )

    def down(slot):
        return pltpu.make_async_remote_copy(
            src_ref=pack_lo.at[slot], dst_ref=recv_hi.at[slot], send_sem=row_send.at[0], recv_sem=row_recv.at[slot, 0],
            device_id=(below_gx, gy), device_id_type=MESH,
        )

    def up(slot):
        return pltpu.make_async_remote_copy(
            src_ref=pack_hi.at[slot], dst_ref=recv_lo.at[slot], send_sem=row_send.at[1], recv_sem=row_recv.at[slot, 1],
            device_id=(above_gx, gy), device_id_type=MESH,
        )

    def start_far(source, slot):
        for end, pack in ((at_low, pack_lo), (at_high, pack_hi)):

            @pl.when(end)
            def _(pack=pack):
                for g in range(gyn):
                    to_far(pack, source, slot, g).start()
                for i in range(1, gyn):
                    to_near(pack, source, slot, i).start()

    def start_rows(slot):
        @pl.when(not_low)
        def _():
            down(slot).start()

        @pl.when(not_high)
        def _():
            up(slot).start()

    def finish_sends(slot):
        @pl.when(at_end)
        def _():
            for g in range(gyn):
                to_far(pack_lo, slot, slot, g).wait_send()
            for i in range(1, gyn):
                to_near(pack_lo, slot, slot, i).wait_send()

        @pl.when(not_low)
        def _():
            down(slot).wait_send()

        @pl.when(not_high)
        def _():
            up(slot).wait_send()

    to_west = pltpu.make_async_remote_copy(
        src_ref=block.at[:, :, :, 0:128], dst_ref=col_r, send_sem=col_send.at[0], recv_sem=col_recv.at[0],
        device_id=(gx, west), device_id_type=MESH,
    )
    to_east = pltpu.make_async_remote_copy(
        src_ref=block.at[:, :, :, 128:256], dst_ref=col_l, send_sem=col_send.at[1], recv_sem=col_recv.at[1],
        device_id=(gx, east), device_id_type=MESH,
    )

    def interleaved(x, start, stop):
        flat = x.reshape(7 * OWN * 8, stop - start)
        out = jnp.dot(
            flat, permutation[start:stop], precision=lax.Precision.HIGHEST, preferred_element_type=jnp.float32
        )
        return out.reshape(7, OWN, 8, LANES)

    own_columns = interleaved(block[...], 0, 256)
    U[:, 0:OWN] = own_columns
    pack_edges(1)
    pl.semaphore_wait(barrier, jnp.where(at_end, 2 * gyn, 4))

    start_far(1, 0)
    to_west.start()
    to_east.start()
    to_west.wait()
    to_east.wait()

    near = lane_iota((7, OWN, 8, 128)) < 64
    halo = interleaved(jnp.where(near, col_r[...], col_l[...]), 256, 384)
    U[:, 0:OWN] = U[:, 0:OWN] + halo
    for field in range(7):
        for k in (ABOVE, BELOW) + AHEAD:
            U[field, k] = U[field, 0]
    pack_edges(0)
    start_rows(0)

    def ghosts_of_neighbours(slot):
        @pl.when(not_high)
        def _():
            outer = unpacked(load_pack(recv_hi, slot, (0, 1, 2)), 0)
            inner = unpacked(load_pack(recv_hi, slot, (3, 4, 5)), 3)
            for f in range(7):
                U[f, ABOVE] = jnp.where(rows8 < 3, outer[f], inner[f])

        @pl.when(not_low)
        def _():
            outer = unpacked(load_pack(recv_lo, slot, (0, 1, 2)), 5)
            inner = unpacked(load_pack(recv_lo, slot, (3, 4, 5)), 2)
            for f in range(7):
                U[f, BELOW] = jnp.where(rows8 >= 5, outer[f], inner[f])

    wrapped = jnp.where(columns < 320, columns, columns - LANES)

    def window(ring, parts, moved):
        origin = lax.rem(gy * 256 + moved + 512 * gyn, 256 * gyn)
        first_block = lax.div(origin, 256)
        offset = lax.rem(origin, 256)
        sources = []
        for i in (0, 1, jnp.where(offset < 128, -1, 2)):
            ahead = offset - 256 * i
            whole = lax.div(ahead + 2 * LANES, 3)
            phase = lax.rem(ahead + 2 * LANES, 3)
            place = lax.rem(first_block + i + gyn, gyn)
            picks = []
            for j in range(3):
                vector = lax.rem(phase + j, 3)
                turn = lax.rem(4 * 128 - whole - lax.div(phase + j, 3), 128)
                picks.append((vector, turn))
            at = wrapped + ahead
            sources.append((place, picks, jnp.logical_and(at >= 0, at < 256)))
        out = []
        for part in parts:
            spans = [
                jnp.concatenate([pltpu.roll(ring[place, vector, part], turn, 1) for vector, turn in picks], axis=1)
                for place, picks, _ in sources
            ]
            out.append(jnp.where(sources[0][2], spans[0], jnp.where(sources[1][2], spans[1], spans[2])))
        return out

    def blended(x, fraction, towards):
        return (1.0 - fraction) * x + fraction * (lane_after(x) if towards == 1 else lane_before(x))

    def low_ghosts(f, raw, fraction):
        ghost = blended(raw, fraction, -1)
        far_rows = roll(raw, 1, 0)
        own = roll(blended(U[f, 0], fraction, 1), 1, 0)
        U[f, BELOW] = jnp.where(rows8 >= 5, ghost, jnp.where(first_row, far_rows, own))
        U[f, ABOVE] = jnp.where(rows8 >= 6, far_rows, U[f, ABOVE])

    def high_ghosts(f, raw, fraction):
        ghost = blended(raw, fraction, 1)
        far_rows = roll(raw, 6, 0)
        own = roll(blended(U[f, OWN - 1], fraction, -1), -2, 0)
        U[f, ABOVE] = jnp.where(rows8 < 3, ghost, jnp.where(rows8 < 6, own, far_rows))
        U[f, BELOW] = jnp.where(rows8 < 2, far_rows, U[f, BELOW])

    def ghosts_of_far_end(slot, n):
        @pl.when(at_end)
        def _():
            for i in range(1, gyn):
                from_near(slot, i).wait_recv()
            for g in range(gyn):
                from_far(slot, g).wait_recv()
            for place in range(gyn):
                ring_far[place] = circ_far[slot, place]
                ring_near[place] = circ_near[slot, place]

        shift, shift_next = shift_ref[n], shift_ref[n + 1]
        fraction = frac_ref[n]
        A, B = (0, 1, 2), (3, 4, 5)
        left, right = AHEAD

        @pl.when(at_low)
        def _():
            ring_near[gy] = pack_lo[slot, :, 0:3]
            for f, raw in enumerate(unpacked(window(ring_far, A, -shift), 5)):
                low_ghosts(f, raw, fraction)
            outer = window(ring_far, A, -shift_next)
            inner = unpacked(window(ring_far, B, -shift_next), 2)
            beyond = window(ring_near, A, shift - shift_next)
            rows_a = unpacked(outer, 5)
            ghost = unpacked([blended(x, fraction, 1) for x in beyond], 0)
            mirror = unpacked([blended(x, fraction, -1) for x in outer], 3)
            raw = unpacked(beyond, 6)
            for f in range(7):
                U[f, left] = jnp.where(first_row, raw[f], jnp.where(rows8 < 5, inner[f], rows_a[f]))
                U[f, right] = jnp.where(rows8 < 3, ghost[f], jnp.where(rows8 < 6, mirror[f], raw[f]))

        @pl.when(at_high)
        def _():
            ring_near[gy] = pack_hi[slot, :, 0:3]
            for f, raw in enumerate(unpacked(window(ring_far, A, shift), 0)):
                high_ghosts(f, raw, fraction)
            outer = window(ring_far, A, shift_next)
            inner = unpacked(window(ring_far, B, shift_next), 3)
            beyond = window(ring_near, A, shift_next - shift)
            rows_a = unpacked(outer, 0)
            ghost = unpacked([blended(x, fraction, -1) for x in beyond], 5)
            mirror = unpacked([blended(x, fraction, 1) for x in outer], 2)
            raw = unpacked(beyond, 7)
            for f in range(7):
                U[f, left] = jnp.where(rows8 < 2, raw[f], jnp.where(rows8 < 5, mirror[f], ghost[f]))
                U[f, right] = jnp.where(rows8 < 3, rows_a[f], jnp.where(last_row, raw[f], inner[f]))

    def ghosts_from_ahead(n):
        fraction = frac_ref[n]

        @pl.when(at_low)
        def _():
            for f in range(7):
                low_ghosts(f, U[f, AHEAD[0]], fraction)

        @pl.when(at_high)
        def _():
            for f in range(7):
                high_ghosts(f, U[f, AHEAD[1]], fraction)

    def minmod(a, b):
        return jnp.maximum(jnp.minimum(a, b), 0.0) + jnp.minimum(jnp.maximum(a, b), 0.0)

    def signal(density, speed, squared):
        total = density + squared
        return jnp.abs(speed) + jnp.abs(total) * lax.rsqrt(total * density)

    def riemann(left, right, normal, wanted):
        dl, vnl, vtl, vsl, btl, bsl = left
        dr, vnr, vtr, vsr, btr, bsr = right
        n2 = normal * normal
        tl = btl * btl + bsl * bsl
        tr = btr * btr + bsr * bsr
        fastest = jnp.maximum(signal(dl, vnl, n2 + tl), signal(dr, vnr, n2 + tr))
        ul = vnl + fastest
        ur = vnr - fastest
        out = {}
        if wanted != (4,):
            al = dl * ul
            ar = dr * ur
        if 0 in wanted:
            out[0] = al + ar
        if 1 in wanted:
            out[1] = (al * vnl + ar * vnr) + ((dl + dr) + (0.5 * (tl + tr) - n2))
        if 2 in wanted:
            out[2] = (al * vtl + ar * vtr) - normal * (btl + btr)
        if 3 in wanted:
            out[3] = (al * vsl + ar * vsr) - normal * (bsl + bsr)
        if 4 in wanted:
            out[4] = (btl * ul + btr * ur) - normal * (vtl + vtr)
        if 5 in wanted:
            out[5] = (bsl * ul + bsr * ur) - normal * (vsl + vsr)
        return out

    def primitives(k, density, mx, my, mz, bz, bx, bx_after, by):
        inverse = 1.0 / density
        Q[0, k] = density
        Q[VX, k] = mx * inverse
        Q[VY, k] = my * inverse
        Q[VZ, k] = mz * inverse
        Q[CX, k] = 0.5 * (bx + row_after(bx, bx_after))
        Q[CY, k] = 0.5 * (by + lane_after(by))
        Q[QBZ, k] = bz

    def initial_primitives(k):
        primitives(k, *(U[f, k] for f in (D, MX, MY, MZ, BZ, BX)), U[BX, following(k)], U[BY, k])

    X_STATE = (0, VX, VY, VZ, CY, QBZ)
    Y_STATE = (0, VY, VX, VZ, CX, QBZ)

    def finish_fluxes(k, fx, fy, stride, mx, my, cells):
        half = 0.5 * stride
        if 0 in fx:
            for spot, part in enumerate((0, 1, 2, 3, 5)):
                FX[spot, k] = fx[part]
        FY4[k] = fy[4]
        SX4[k] = fx[4] + lane_before(fx[4])
        if cells:
            for spot, (field, px, py) in enumerate(((D, 0, 0), (MX, 1, 2), (MY, 2, 1), (MZ, 3, 3), (BZ, 5, 5))):
                value = U[field, k] - half * ((lane_after(fy[py]) - fy[py]) - fx[px])
                if field == MX:
                    value += (stride * 2.0 * OMEGA) * my
                if field == MY:
                    value -= (stride * (2.0 - QSHEAR) * OMEGA) * mx
                PART[spot, k] = value

    ALL = (0, 1, 2, 3, 4, 5)

    def first_order(k, stride):
        left = [row_before(Q[i, previous(k)], Q[i, k]) for i in X_STATE]
        fx = riemann(left, [Q[i, k] for i in X_STATE], U[BX, k], ALL)
        right = [Q[i, k] for i in Y_STATE]
        fy = riemann([lane_before(q) for q in right], right, U[BY, k], ALL)
        finish_fluxes(k, fx, fy, stride, U[MX, k], U[MY, k], True)

    def slopes(k):
        for spot, i in enumerate(X_STATE):
            here = Q[i, k]
            gradient = 0.5 * minmod(here - row_before(Q[i, previous(k)], here), row_after(here, Q[i, following(k)]) - here)
            QL[spot, k] = here + gradient
            QR[spot, k] = here - gradient

    def second_order(k, stride, last):
        cells = k < OWN or not last
        x_wanted = ALL if cells or k == ABOVE else (4,)
        y_wanted = ALL if cells else (4,)
        left = [row_before(QL[i, previous(k)], QL[i, k]) for i in range(6)]
        fx = riemann(left, [QR[i, k] for i in range(6)], NBX[k], x_wanted)
        left, right = [], []
        for i in Y_STATE:
            here = Q[i, k]
            behind = here - lane_before(here)
            gradient = 0.5 * minmod(behind, lane_after(behind))
            left.append(lane_before(here + gradient))
            right.append(here - gradient)
        fy = riemann(left, right, NBY[k], y_wanted)
        finish_fluxes(k, fx, fy, stride, M[0, k], M[1, k], cells)

    def corner(k):
        return 0.125 * (FY4[k] + row_before(FY4[previous(k)], FY4[k]) - SX4[k])

    def face_x(k, emf, stride):
        EZ[k] = emf
        return U[BX, k] - stride * (lane_after(emf) - emf)

    def face_y(k, stride):
        emf = EZ[k]
        return U[BY, k] + stride * (row_after(emf, EZ[following(k)]) - emf)

    def cells_of(k, stride):
        return [PART[i, k] - (0.5 * stride) * row_after(FX[i, k], FX[i, following(k)]) for i in range(5)]

    def advance(n, last):
        fraction = frac_ref[n]

        def tiles(run):
            for k in range(RING):
                run(k)
            if not last:

                @pl.when(at_end)
                def _():
                    for k in AHEAD:
                        run(k)

        stride = 0.5 * TIMESTEP
        tiles(initial_primitives)
        tiles(lambda k: first_order(k, stride))

        def predicted_x(k):
            NBX[k] = face_x(k, corner(k), stride)

        tiles(predicted_x)

        def predicted_cells(k):
            density, mx, my, mz, bz = cells_of(k, stride)
            by = face_y(k, stride)
            NBY[k] = by
            M[0, k] = mx
            M[1, k] = my
            primitives(k, density, mx, my, mz, bz, NBX[k], NBX[following(k)], by)

        tiles(predicted_cells)

        tiles(slopes)
        tiles(lambda k: second_order(k, TIMESTEP, last))
        kept = range(OWN) if last else range(RING)

        def mended(emf, remote_row, towards, ours):
            remote = blended(remote_row, fraction, towards)
            return jnp.where(jnp.logical_and(first_row, ours), 0.5 * (emf + remote), emf)

        emfs = [corner(k) for k in range(RING)]
        low_fix = mended(emfs[0], roll(emfs[BELOW], -1, 0), -1, at_low)
        high_fix = mended(emfs[ABOVE], roll(emfs[ABOVE], -6, 0), 1, at_high)
        emfs[0], emfs[ABOVE] = low_fix, high_fix
        for k in range(RING):
            new_bx = face_x(k, emfs[k], TIMESTEP)
            if k in kept:
                U[BX, k] = new_bx

        def new_cells(k):
            for field, value in zip((D, MX, MY, MZ, BZ), cells_of(k, TIMESTEP)):
                U[field, k] = value
            U[BY, k] = face_y(k, TIMESTEP)

        for k in kept:
            new_cells(k)
        if not last:

            @pl.when(at_end)
            def _():
                left, right = AHEAD
                emf_l, emf_r = corner(left), corner(right)
                from_low = blended(roll(emf_r, -6, 0), fraction, 1)
                from_high = blended(roll(emf_l, -2, 0), fraction, -1)
                remote = jnp.where(at_low, from_low, from_high)
                emf_r = jnp.where(first_row, 0.5 * (emf_r + remote), emf_r)
                U[BX, left] = face_x(left, emf_l, TIMESTEP)
                U[BX, right] = face_x(right, emf_r, TIMESTEP)
                for k in AHEAD:
                    new_cells(k)

    rounds = STEPS // 2

    def two_steps(r, carry):
        slot = lax.rem(r, 2)

        @pl.when(not_high)
        def _():
            down(slot).wait_recv()

        @pl.when(not_low)
        def _():
            up(slot).wait_recv()

        ghosts_of_neighbours(slot)
        ghosts_of_far_end(slot, 2 * r)
        advance(2 * r, False)
        ghosts_from_ahead(2 * r + 1)
        advance(2 * r + 1, True)
        finish_sends(slot)

        @pl.when(r < rounds - 1)
        def _():
            pack_edges(1 - slot)
            start_far(1 - slot, 1 - slot)
            start_rows(1 - slot)

        return carry

    lax.fori_loop(0, rounds, two_steps, 0)

    flat = U[:, 0:OWN].reshape(7 * OWN * 8, LANES)
    out = lax.dot_general(
        flat, permutation[0:256], (((1,), (1,)), ((), ())),
        precision=lax.Precision.HIGHEST, preferred_element_type=jnp.float32,
    ).reshape(7, 8 * OWN, 256)
    den_out[...] = out[D]
    mom_out[...] = out[MX : MZ + 1]
    mag_out[...] = out[BX : BZ + 1]


def scratch(gyn):
    tile = (TILES, 8, LANES)
    f32 = jnp.float32
    vmem = lambda *shape: pltpu.VMEM(shape, f32)
    dma = pltpu.SemaphoreType.DMA
    return [
        vmem(7, *tile), vmem(7, *tile), vmem(2, *tile), vmem(6, *tile), vmem(6, *tile), vmem(5, *tile), vmem(5, *tile),
        vmem(*tile), vmem(*tile), vmem(*tile), vmem(*tile), vmem(*tile),
        *(vmem(2, 3, PARTS, 8, 128) for _ in range(4)), vmem(7, OWN, 8, 256),
        vmem(2, gyn, 3, PARTS, 8, 128), vmem(2, gyn, 3, 3, 8, 128),
        vmem(gyn, 3, PARTS, 8, 128), vmem(gyn, 3, 3, 8, 128), vmem(7, OWN, 8, 128), vmem(7, OWN, 8, 128),
        pltpu.SMEM((STEPS,), jnp.int32), pltpu.SMEM((STEPS,), f32), dma((5,)),
        dma((2,)), dma((2,)), dma((2,)), dma((2, 2)),
        dma((gyn,)), dma((2, gyn)), dma((gyn,)), dma((2, gyn)),
    ]


def solution(mesh):
    gxn, gyn = mesh.shape["gx"], mesh.shape["gy"]

    def per_device(density, momentum, magnetic, shear_shift, shear_frac):
        return pl.pallas_call(
            functools.partial(kernel, gxn, gyn),
            name="shearing_box",
            out_shape=tuple(jax.ShapeDtypeStruct(a.shape, jnp.float32) for a in (density, momentum, magnetic)),
            in_specs=[pl.BlockSpec(memory_space=pl.ANY)] * 5,
            out_specs=tuple(pl.BlockSpec(memory_space=pltpu.VMEM) for _ in range(3)),
            scratch_shapes=scratch(gyn),
            compiler_params=pltpu.CompilerParams(
                collective_id=0, has_side_effects=True, vmem_limit_bytes=48 * 1024 * 1024
            ),
        )(
            shear_shift,
            shear_frac,
            density.reshape(OWN, 8, 256),
            momentum.reshape(3, OWN, 8, 256),
            magnetic.reshape(3, OWN, 8, 256),
        )

    return jax.shard_map(
        per_device,
        mesh=mesh,
        in_specs=(P("gx", "gy"), P(None, "gx", "gy"), P(None, "gx", "gy"), P(), P()),
        out_specs=(P("gx", "gy"), P(None, "gx", "gy"), P(None, "gx", "gy")),
        check_vma=False,
    )
```

```python
import functools

import jax
import jax.numpy as jnp
from jax import lax
from jax.experimental import pallas as pl
from jax.experimental.pallas import tpu as pltpu
from jax.sharding import PartitionSpec as P

STEPS = 8
OMEGA = 0.5
QSHEAR = 1.5
TIMESTEP = 0.1
MESH = pl.DeviceIdType.MESH

D, MX, MY, MZ, BX, BY, BZ = range(7)
VX, VY, VZ, CY, CX, QBZ = 1, 2, 3, 4, 5, 6
OWN = 4
ABOVE, BELOW = OWN, OWN + 1
RING = OWN + 2
AHEAD = (RING, RING + 1)
MAIN = tuple(range(RING))
TILES = RING + 2
LANES = 384
GROUPS = 2


def roll(x, shift, axis):
    return pltpu.roll(x, shift % x.shape[axis], axis)


def row_iota(shape):
    return lax.broadcasted_iota(jnp.int32, shape, len(shape) - 2)


def lane_iota(shape):
    return lax.broadcasted_iota(jnp.int32, shape, len(shape) - 1)


def kernel(
    gxn, gyn, shift_in, frac_in, den, mom, mag, den_out, mom_out, mag_out,
    U, Q, M, QL, QR, FX, PART, FY4, SX4, EZ, NBX, NBY,
    pack_lo, pack_hi, recv_lo, recv_hi, block, circ_far, circ_near, ring_far, ring_near, col_r, col_l,
    shift_ref, frac_ref, load_sem,
    col_send, col_recv, row_send, row_recv, far_send, far_recv, near_send, near_recv,
):
    gx = lax.axis_index("gx")
    gy = lax.axis_index("gy")
    at_low = gx == 0
    at_high = gx == gxn - 1
    at_end = jnp.logical_or(at_low, at_high)
    not_low = gx > 0
    not_high = gx < gxn - 1
    below_gx = lax.max(gx - 1, 0)
    above_gx = lax.min(gx + 1, gxn - 1)
    other_end = gxn - 1 - gx
    east = lax.rem(gy + 1, gyn)
    west = lax.rem(gy + gyn - 1, gyn)

    rows8 = row_iota((8, LANES))
    first_row = rows8 == 0
    last_row = rows8 == 7
    near = lane_iota((8, 128)) < 64

    def previous(k):
        return sum(AHEAD) - k if k in AHEAD else (k + RING - 1) % RING

    def following(k):
        return sum(AHEAD) - k if k in AHEAD else (k + 1) % RING

    def row_before(before, here):
        return roll(jnp.where(last_row, before, here), 1, 0)

    def row_after(here, after):
        return roll(jnp.where(first_row, after, here), -1, 0)

    def lane_before(x):
        return jnp.concatenate([roll(x[:, 256:384], 1, 1), x[:, 0:128], x[:, 128:256]], axis=1)

    def lane_after(x):
        return jnp.concatenate([x[:, 128:256], x[:, 256:384], roll(x[:, 0:128], -1, 1)], axis=1)

    spots = lane_iota((8, LANES))
    columns = 3 * (spots & 127) + (spots >> 7)
    spot_of_row = lane_iota((LANES, LANES))
    permutation = jnp.where(row_iota((LANES, LANES)) == 3 * (spot_of_row & 127) + (spot_of_row >> 7), 1.0, 0.0)

    loads = [
        pltpu.make_async_copy(den, block.at[D], load_sem.at[0]),
        pltpu.make_async_copy(mom, block.at[MX : MZ + 1], load_sem.at[1]),
        pltpu.make_async_copy(mag, block.at[BX : BZ + 1], load_sem.at[2]),
        pltpu.make_async_copy(shift_in, shift_ref, load_sem.at[3]),
        pltpu.make_async_copy(frac_in, frac_ref, load_sem.at[4]),
    ]
    for load in loads:
        load.start()

    barrier = pltpu.get_barrier_semaphore()

    def greet(to_gx, to_gy):
        pl.semaphore_signal(barrier, inc=1, device_id=(to_gx, to_gy), device_id_type=MESH)

    @pl.when(at_end)
    def _():
        for g in range(gyn):
            greet(other_end, g)
        for i in range(1, gyn):
            greet(gx, lax.rem(gy + i, gyn))

    @pl.when(jnp.logical_not(at_end))
    def _():
        greet(gx, east)
        greet(gx, west)

    @pl.when(not_low)
    def _():
        greet(below_gx, gy)

    @pl.when(not_high)
    def _():
        greet(above_gx, gy)

    for load in loads:
        load.wait()

    def packed(tiles, first):
        def at(field, row):
            return tiles[field] if row == first else roll(tiles[field], row - first, 0)

        return [
            jnp.where(rows8 < 3, at(0, 0), jnp.where(rows8 < 6, at(1, 3), at(6, 6))),
            jnp.where(rows8 < 3, at(2, 0), jnp.where(rows8 < 6, at(3, 3), at(6, 4))),
            jnp.where(rows8 < 3, at(4, 0), at(5, 3)),
        ]

    def unpacked(tiles, first):
        def move(x, row):
            return x if row == first else roll(x, first - row, 0)

        sixth = jnp.where(((rows8 - first) & 7) < 2, move(tiles[0], 6), move(tiles[1], 4))
        return (
            move(tiles[0], 0), move(tiles[0], 3), move(tiles[1], 0), move(tiles[1], 3),
            move(tiles[2], 0), move(tiles[2], 3), sixth,
        )

    def pack_edge(ref, slot, k, outer, inner):
        tiles = [U[f, k] for f in range(7)]
        for group, first in enumerate((outer, inner)):
            for part, tile in enumerate(packed(tiles, first)):
                for lane in range(3):
                    ref[slot, group, lane, part] = tile[:, 128 * lane : 128 * (lane + 1)]

    def load_pack(ref, slot, group):
        return [jnp.concatenate([ref[slot, group, lane, part] for lane in range(3)], axis=1) for part in range(3)]

    def pack_edges(slot):
        pack_edge(pack_lo, slot, 0, 0, 3)
        pack_edge(pack_hi, slot, OWN - 1, 5, 2)

    def to_far(pack, source, slot, group, g):
        return pltpu.make_async_remote_copy(
            src_ref=pack.at[source, group], dst_ref=circ_far.at[slot, group, gy],
            send_sem=far_send.at[group, g], recv_sem=far_recv.at[slot, group, gy],
            device_id=(other_end, g), device_id_type=MESH,
        )

    def from_far(slot, group, g):
        return pltpu.make_async_remote_copy(
            src_ref=pack_lo.at[slot, group], dst_ref=circ_far.at[slot, group, g],
            send_sem=far_send.at[group, g], recv_sem=far_recv.at[slot, group, g],
            device_id=(other_end, g), device_id_type=MESH,
        )

    def to_near(pack, source, slot, i):
        return pltpu.make_async_remote_copy(
            src_ref=pack.at[source, 0], dst_ref=circ_near.at[slot, gy],
            send_sem=near_send.at[i], recv_sem=near_recv.at[slot, i],
            device_id=(gx, lax.rem(gy + i, gyn)), device_id_type=MESH,
        )

    def from_near(slot, i):
        sender = lax.rem(gy + gyn - i, gyn)
        return pltpu.make_async_remote_copy(
            src_ref=pack_lo.at[slot, 0], dst_ref=circ_near.at[slot, sender],
            send_sem=near_send.at[i], recv_sem=near_recv.at[slot, i],
            device_id=(gx, sender), device_id_type=MESH,
        )

    def down(slot):
        return pltpu.make_async_remote_copy(
            src_ref=pack_lo.at[slot], dst_ref=recv_hi.at[slot], send_sem=row_send.at[0], recv_sem=row_recv.at[slot, 0],
            device_id=(below_gx, gy), device_id_type=MESH,
        )

    def up(slot):
        return pltpu.make_async_remote_copy(
            src_ref=pack_hi.at[slot], dst_ref=recv_lo.at[slot], send_sem=row_send.at[1], recv_sem=row_recv.at[slot, 1],
            device_id=(above_gx, gy), device_id_type=MESH,
        )

    def at_ends(run):
        for end, pack in ((at_low, pack_lo), (at_high, pack_hi)):

            @pl.when(end)
            def _(pack=pack):
                run(pack)

    def start_far(source, slot):
        def run(pack):
            for g in range(gyn):
                to_far(pack, source, slot, 0, g).start()

        at_ends(run)

    def start_ahead(source, slot):
        def run(pack):
            for i in range(1, gyn):
                to_near(pack, source, slot, i).start()
            for g in range(gyn):
                to_far(pack, source, slot, 1, g).start()

        at_ends(run)

    def start_rows(slot):
        @pl.when(not_low)
        def _():
            down(slot).start()

        @pl.when(not_high)
        def _():
            up(slot).start()

    def finish_sends(slot):
        @pl.when(at_end)
        def _():
            for group in range(2):
                for g in range(gyn):
                    to_far(pack_lo, slot, slot, group, g).wait_send()
            for i in range(1, gyn):
                to_near(pack_lo, slot, slot, i).wait_send()

        @pl.when(not_low)
        def _():
            down(slot).wait_send()

        @pl.when(not_high)
        def _():
            up(slot).wait_send()

    to_west = pltpu.make_async_remote_copy(
        src_ref=block.at[:, :, :, 0:128], dst_ref=col_r, send_sem=col_send.at[0], recv_sem=col_recv.at[0],
        device_id=(gx, west), device_id_type=MESH,
    )
    to_east = pltpu.make_async_remote_copy(
        src_ref=block.at[:, :, :, 128:256], dst_ref=col_l, send_sem=col_send.at[1], recv_sem=col_recv.at[1],
        device_id=(gx, east), device_id_type=MESH,
    )

    def interleaved(x, start, stop):
        flat = x.reshape(7 * OWN * 8, stop - start)
        out = jnp.dot(
            flat, permutation[start:stop], precision=lax.Precision.HIGHEST, preferred_element_type=jnp.float32
        )
        return out.reshape(7, OWN, 8, LANES)

    own_columns = interleaved(block[...], 0, 256)
    U[:, 0:OWN] = own_columns
    pack_edges(1)
    pl.semaphore_wait(barrier, jnp.where(at_end, 2 * gyn, 4))

    start_far(1, 0)
    to_west.start()
    to_east.start()
    start_ahead(1, 0)
    to_west.wait()
    to_east.wait()

    near = lane_iota((7, OWN, 8, 128)) < 64
    halo = interleaved(jnp.where(near, col_r[...], col_l[...]), 256, 384)
    U[:, 0:OWN] = U[:, 0:OWN] + halo
    for field in range(7):
        for k in (ABOVE, BELOW) + AHEAD:
            U[field, k] = U[field, 0]
    pack_edges(0)
    start_rows(0)

    def ghosts_of_neighbours(slot):
        @pl.when(not_high)
        def _():
            outer = unpacked(load_pack(recv_hi, slot, 0), 0)
            inner = unpacked(load_pack(recv_hi, slot, 1), 3)
            for f in range(7):
                U[f, ABOVE] = jnp.where(rows8 < 3, outer[f], inner[f])

        @pl.when(not_low)
        def _():
            outer = unpacked(load_pack(recv_lo, slot, 0), 5)
            inner = unpacked(load_pack(recv_lo, slot, 1), 2)
            for f in range(7):
                U[f, BELOW] = jnp.where(rows8 >= 5, outer[f], inner[f])

    wrapped = jnp.where(columns < 320, columns, columns - LANES)

    def window(ring, moved):
        origin = lax.rem(gy * 256 + moved + 512 * gyn, 256 * gyn)
        first_block = lax.div(origin, 256)
        offset = lax.rem(origin, 256)
        sources = []
        for i in (0, 1, jnp.where(offset < 128, -1, 2)):
            ahead = offset - 256 * i
            whole = lax.div(ahead + 2 * LANES, 3)
            phase = lax.rem(ahead + 2 * LANES, 3)
            place = lax.rem(first_block + i + gyn, gyn)
            picks = []
            for j in range(3):
                vector = lax.rem(phase + j, 3)
                turn = lax.rem(4 * 128 - whole - lax.div(phase + j, 3), 128)
                picks.append((vector, turn))
            at = wrapped + ahead
            sources.append((place, picks, jnp.logical_and(at >= 0, at < 256)))
        out = []
        for part in range(3):
            spans = [
                jnp.concatenate([pltpu.roll(ring[place, vector, part], turn, 1) for vector, turn in picks], axis=1)
                for place, picks, _ in sources
            ]
            out.append(jnp.where(sources[0][2], spans[0], jnp.where(sources[1][2], spans[1], spans[2])))
        return out

    def blended(x, fraction, towards):
        return (1.0 - fraction) * x + fraction * (lane_after(x) if towards == 1 else lane_before(x))

    def low_ghosts(f, raw, fraction):
        ghost = blended(raw, fraction, -1)
        far_rows = roll(raw, 1, 0)
        own = roll(blended(U[f, 0], fraction, 1), 1, 0)
        U[f, BELOW] = jnp.where(rows8 >= 5, ghost, jnp.where(first_row, far_rows, own))
        U[f, ABOVE] = jnp.where(rows8 >= 6, far_rows, U[f, ABOVE])

    def high_ghosts(f, raw, fraction):
        ghost = blended(raw, fraction, 1)
        far_rows = roll(raw, 6, 0)
        own = roll(blended(U[f, OWN - 1], fraction, -1), -2, 0)
        U[f, ABOVE] = jnp.where(rows8 < 3, ghost, jnp.where(rows8 < 6, own, far_rows))
        U[f, BELOW] = jnp.where(rows8 < 2, far_rows, U[f, BELOW])

    def ghosts_of_far_end(slot, n):
        shift = shift_ref[n]
        fraction = frac_ref[n]

        @pl.when(at_end)
        def _():
            for g in range(gyn):
                from_far(slot, 0, g).wait_recv()
            ring_far[0] = circ_far[slot, 0]

        @pl.when(at_low)
        def _():
            for f, raw in enumerate(unpacked(window(ring_far.at[0], -shift), 5)):
                low_ghosts(f, raw, fraction)

        @pl.when(at_high)
        def _():
            for f, raw in enumerate(unpacked(window(ring_far.at[0], shift), 0)):
                high_ghosts(f, raw, fraction)

    def rows_ahead(slot, n):
        shift, shift_next = shift_ref[n], shift_ref[n + 1]
        fraction = frac_ref[n]
        left, right = AHEAD

        @pl.when(at_end)
        def _():
            for i in range(1, gyn):
                from_near(slot, i).wait_recv()
            for g in range(gyn):
                from_far(slot, 1, g).wait_recv()
            ring_far[1] = circ_far[slot, 1]
            ring_near[...] = circ_near[slot]

        @pl.when(at_low)
        def _():
            ring_near[gy] = pack_lo[slot, 0]
            outer = window(ring_far.at[0], -shift_next)
            inner = unpacked(window(ring_far.at[1], -shift_next), 2)
            beyond = window(ring_near, shift - shift_next)
            rows_a = unpacked(outer, 5)
            ghost = unpacked([blended(x, fraction, 1) for x in beyond], 0)
            mirror = unpacked([blended(x, fraction, -1) for x in outer], 3)
            raw = unpacked(beyond, 6)
            for f in range(7):
                U[f, left] = jnp.where(first_row, raw[f], jnp.where(rows8 < 5, inner[f], rows_a[f]))
                U[f, right] = jnp.where(rows8 < 3, ghost[f], jnp.where(rows8 < 6, mirror[f], raw[f]))

        @pl.when(at_high)
        def _():
            ring_near[gy] = pack_hi[slot, 0]
            outer = window(ring_far.at[0], shift_next)
            inner = unpacked(window(ring_far.at[1], shift_next), 3)
            beyond = window(ring_near, shift_next - shift)
            rows_a = unpacked(outer, 0)
            ghost = unpacked([blended(x, fraction, -1) for x in beyond], 5)
            mirror = unpacked([blended(x, fraction, 1) for x in outer], 2)
            raw = unpacked(beyond, 7)
            for f in range(7):
                U[f, left] = jnp.where(rows8 < 2, raw[f], jnp.where(rows8 < 5, mirror[f], ghost[f]))
                U[f, right] = jnp.where(rows8 < 3, rows_a[f], jnp.where(last_row, raw[f], inner[f]))

    def ghosts_from_ahead(n):
        fraction = frac_ref[n]

        @pl.when(at_low)
        def _():
            for f in range(7):
                low_ghosts(f, U[f, AHEAD[0]], fraction)

        @pl.when(at_high)
        def _():
            for f in range(7):
                high_ghosts(f, U[f, AHEAD[1]], fraction)

    def minmod(a, b):
        return jnp.maximum(jnp.minimum(a, b), 0.0) + jnp.minimum(jnp.maximum(a, b), 0.0)

    def signal(density, speed, squared):
        total = density + squared
        return jnp.abs(speed) + jnp.abs(total) * lax.rsqrt(total * density)

    def riemann(left, right, normal, wanted):
        dl, vnl, vtl, vsl, btl, bsl = left
        dr, vnr, vtr, vsr, btr, bsr = right
        n2 = normal * normal
        tl = btl * btl + bsl * bsl
        tr = btr * btr + bsr * bsr
        fastest = jnp.maximum(signal(dl, vnl, n2 + tl), signal(dr, vnr, n2 + tr))
        ul = vnl + fastest
        ur = vnr - fastest
        out = {}
        if wanted != (4,):
            al = dl * ul
            ar = dr * ur
        if 0 in wanted:
            out[0] = al + ar
        if 1 in wanted:
            out[1] = (al * vnl + ar * vnr) + ((dl + dr) + (0.5 * (tl + tr) - n2))
        if 2 in wanted:
            out[2] = (al * vtl + ar * vtr) - normal * (btl + btr)
        if 3 in wanted:
            out[3] = (al * vsl + ar * vsr) - normal * (bsl + bsr)
        if 4 in wanted:
            out[4] = (btl * ul + btr * ur) - normal * (vtl + vtr)
        if 5 in wanted:
            out[5] = (bsl * ul + bsr * ur) - normal * (vsl + vsr)
        return out

    def primitives(k, density, mx, my, mz, bz, bx, bx_after, by):
        inverse = 1.0 / density
        Q[0, k] = density
        Q[VX, k] = mx * inverse
        Q[VY, k] = my * inverse
        Q[VZ, k] = mz * inverse
        Q[CX, k] = 0.5 * (bx + row_after(bx, bx_after))
        Q[CY, k] = 0.5 * (by + lane_after(by))
        Q[QBZ, k] = bz

    def initial_primitives(k):
        primitives(k, *(U[f, k] for f in (D, MX, MY, MZ, BZ, BX)), U[BX, following(k)], U[BY, k])

    X_STATE = (0, VX, VY, VZ, CY, QBZ)
    Y_STATE = (0, VY, VX, VZ, CX, QBZ)

    def finish_fluxes(k, fx, fy, stride, mx, my, cells):
        half = 0.5 * stride
        if 0 in fx:
            for spot, part in enumerate((0, 1, 2, 3, 5)):
                FX[spot, k] = fx[part]
        FY4[k] = fy[4]
        SX4[k] = fx[4] + lane_before(fx[4])
        if cells:
            for spot, (field, px, py) in enumerate(((D, 0, 0), (MX, 1, 2), (MY, 2, 1), (MZ, 3, 3), (BZ, 5, 5))):
                value = U[field, k] - half * ((lane_after(fy[py]) - fy[py]) - fx[px])
                if field == MX:
                    value += (stride * 2.0 * OMEGA) * my
                if field == MY:
                    value -= (stride * (2.0 - QSHEAR) * OMEGA) * mx
                PART[spot, k] = value

    ALL = (0, 1, 2, 3, 4, 5)

    def first_order(k, stride):
        left = [row_before(Q[i, previous(k)], Q[i, k]) for i in X_STATE]
        fx = riemann(left, [Q[i, k] for i in X_STATE], U[BX, k], ALL)
        right = [Q[i, k] for i in Y_STATE]
        fy = riemann([lane_before(q) for q in right], right, U[BY, k], ALL)
        finish_fluxes(k, fx, fy, stride, U[MX, k], U[MY, k], True)

    def slopes(k):
        for spot, i in enumerate(X_STATE):
            here = Q[i, k]
            gradient = 0.5 * minmod(here - row_before(Q[i, previous(k)], here), row_after(here, Q[i, following(k)]) - here)
            QL[spot, k] = here + gradient
            QR[spot, k] = here - gradient

    def second_order(k, stride, last):
        cells = k < OWN or not last
        x_wanted = ALL if cells or k == ABOVE else (4,)
        y_wanted = ALL if cells else (4,)
        left = [row_before(QL[i, previous(k)], QL[i, k]) for i in range(6)]
        fx = riemann(left, [QR[i, k] for i in range(6)], NBX[k], x_wanted)
        left, right = [], []
        for i in Y_STATE:
            here = Q[i, k]
            behind = here - lane_before(here)
            gradient = 0.5 * minmod(behind, lane_after(behind))
            left.append(lane_before(here + gradient))
            right.append(here - gradient)
        fy = riemann(left, right, NBY[k], y_wanted)
        finish_fluxes(k, fx, fy, stride, M[0, k], M[1, k], cells)

    def corner(k):
        return 0.125 * (FY4[k] + row_before(FY4[previous(k)], FY4[k]) - SX4[k])

    def face_x(k, emf, stride):
        EZ[k] = emf
        return U[BX, k] - stride * (lane_after(emf) - emf)

    def face_y(k, stride):
        emf = EZ[k]
        return U[BY, k] + stride * (row_after(emf, EZ[following(k)]) - emf)

    def cells_of(k, stride):
        return [PART[i, k] - (0.5 * stride) * row_after(FX[i, k], FX[i, following(k)]) for i in range(5)]

    def advance(n, last, ring):
        fraction = frac_ref[n]

        def tiles(run):
            for k in ring:
                run(k)

        stride = 0.5 * TIMESTEP
        tiles(initial_primitives)
        tiles(lambda k: first_order(k, stride))

        def predicted_x(k):
            NBX[k] = face_x(k, corner(k), stride)

        tiles(predicted_x)

        def predicted_cells(k):
            density, mx, my, mz, bz = cells_of(k, stride)
            by = face_y(k, stride)
            NBY[k] = by
            M[0, k] = mx
            M[1, k] = my
            primitives(k, density, mx, my, mz, bz, NBX[k], NBX[following(k)], by)

        tiles(predicted_cells)

        tiles(slopes)
        tiles(lambda k: second_order(k, TIMESTEP, last))
        def new_cells(k):
            for field, value in zip((D, MX, MY, MZ, BZ), cells_of(k, TIMESTEP)):
                U[field, k] = value
            U[BY, k] = face_y(k, TIMESTEP)

        if ring == AHEAD:
            left, right = AHEAD
            emf_l, emf_r = corner(left), corner(right)
            from_low = blended(roll(emf_r, -6, 0), fraction, 1)
            from_high = blended(roll(emf_l, -2, 0), fraction, -1)
            remote = jnp.where(at_low, from_low, from_high)
            emf_r = jnp.where(first_row, 0.5 * (emf_r + remote), emf_r)
            U[BX, left] = face_x(left, emf_l, TIMESTEP)
            U[BX, right] = face_x(right, emf_r, TIMESTEP)
            tiles(new_cells)
            return
        kept = range(OWN) if last else ring

        def mended(emf, remote_row, towards, ours):
            remote = blended(remote_row, fraction, towards)
            return jnp.where(jnp.logical_and(first_row, ours), 0.5 * (emf + remote), emf)

        emfs = [corner(k) for k in ring]
        low_fix = mended(emfs[0], roll(emfs[BELOW], -1, 0), -1, at_low)
        high_fix = mended(emfs[ABOVE], roll(emfs[ABOVE], -6, 0), 1, at_high)
        emfs[0], emfs[ABOVE] = low_fix, high_fix
        for k in ring:
            new_bx = face_x(k, emfs[k], TIMESTEP)
            if k in kept:
                U[BX, k] = new_bx
        for k in kept:
            new_cells(k)

    rounds = STEPS // 2

    def two_steps(r, carry):
        slot = lax.rem(r, 2)

        @pl.when(not_high)
        def _():
            down(slot).wait_recv()

        @pl.when(not_low)
        def _():
            up(slot).wait_recv()

        ghosts_of_neighbours(slot)
        ghosts_of_far_end(slot, 2 * r)
        advance(2 * r, False, MAIN)
        rows_ahead(slot, 2 * r)

        @pl.when(at_end)
        def _():
            advance(2 * r, False, AHEAD)

        ghosts_from_ahead(2 * r + 1)
        advance(2 * r + 1, True, MAIN)
        finish_sends(slot)

        @pl.when(r < rounds - 1)
        def _():
            pack_edges(1 - slot)
            start_far(1 - slot, 1 - slot)
            start_rows(1 - slot)
            start_ahead(1 - slot, 1 - slot)

        return carry

    lax.fori_loop(0, rounds, two_steps, 0)

    flat = U[:, 0:OWN].reshape(7 * OWN * 8, LANES)
    out = lax.dot_general(
        flat, permutation[0:256], (((1,), (1,)), ((), ())),
        precision=lax.Precision.HIGHEST, preferred_element_type=jnp.float32,
    ).reshape(7, 8 * OWN, 256)
    den_out[...] = out[D]
    mom_out[...] = out[MX : MZ + 1]
    mag_out[...] = out[BX : BZ + 1]


def scratch(gyn):
    tile = (TILES, 8, LANES)
    f32 = jnp.float32
    vmem = lambda *shape: pltpu.VMEM(shape, f32)
    dma = pltpu.SemaphoreType.DMA
    return [
        vmem(7, *tile), vmem(7, *tile), vmem(2, *tile), vmem(6, *tile), vmem(6, *tile), vmem(5, *tile), vmem(5, *tile),
        vmem(*tile), vmem(*tile), vmem(*tile), vmem(*tile), vmem(*tile),
        *(vmem(2, GROUPS, 3, 3, 8, 128) for _ in range(4)), vmem(7, OWN, 8, 256),
        vmem(2, GROUPS, gyn, 3, 3, 8, 128), vmem(2, gyn, 3, 3, 8, 128),
        vmem(GROUPS, gyn, 3, 3, 8, 128), vmem(gyn, 3, 3, 8, 128), vmem(7, OWN, 8, 128), vmem(7, OWN, 8, 128),
        pltpu.SMEM((STEPS,), jnp.int32), pltpu.SMEM((STEPS,), f32), dma((5,)),
        dma((2,)), dma((2,)), dma((2,)), dma((2, 2)),
        dma((GROUPS, gyn)), dma((2, GROUPS, gyn)), dma((gyn,)), dma((2, gyn)),
    ]


def solution(mesh):
    gxn, gyn = mesh.shape["gx"], mesh.shape["gy"]

    def per_device(density, momentum, magnetic, shear_shift, shear_frac):
        return pl.pallas_call(
            functools.partial(kernel, gxn, gyn),
            name="shearing_box",
            out_shape=tuple(jax.ShapeDtypeStruct(a.shape, jnp.float32) for a in (density, momentum, magnetic)),
            in_specs=[pl.BlockSpec(memory_space=pl.ANY)] * 5,
            out_specs=tuple(pl.BlockSpec(memory_space=pltpu.VMEM) for _ in range(3)),
            scratch_shapes=scratch(gyn),
            compiler_params=pltpu.CompilerParams(
                collective_id=0, has_side_effects=True, vmem_limit_bytes=48 * 1024 * 1024
            ),
        )(
            shear_shift,
            shear_frac,
            density.reshape(OWN, 8, 256),
            momentum.reshape(3, OWN, 8, 256),
            magnetic.reshape(3, OWN, 8, 256),
        )

    return jax.shard_map(
        per_device,
        mesh=mesh,
        in_specs=(P("gx", "gy"), P(None, "gx", "gy"), P(None, "gx", "gy"), P(), P()),
        out_specs=(P("gx", "gy"), P(None, "gx", "gy"), P(None, "gx", "gy")),
        check_vma=False,
    )
```

```python
import functools

import jax
import jax.numpy as jnp
from jax import lax
from jax.experimental import pallas as pl
from jax.experimental.pallas import tpu as pltpu
from jax.sharding import PartitionSpec as P

STEPS = 8
OMEGA = 0.5
QSHEAR = 1.5
TIMESTEP = 0.1
MESH = pl.DeviceIdType.MESH

D, MX, MY, MZ, BX, BY, BZ = range(7)
VX, VY, VZ, CY, CX, QBZ = 1, 2, 3, 4, 5, 6
OWN = 4
ABOVE, BELOW = OWN, OWN + 1
RING = OWN + 2
AHEAD = (RING, RING + 1)
MAIN = tuple(range(RING))
TILES = RING + 2
LANES = 384
GROUPS = 2


def roll(x, shift, axis):
    return pltpu.roll(x, shift % x.shape[axis], axis)


def row_iota(shape):
    return lax.broadcasted_iota(jnp.int32, shape, len(shape) - 2)


def lane_iota(shape):
    return lax.broadcasted_iota(jnp.int32, shape, len(shape) - 1)


def kernel(
    gxn, gyn, shift_in, frac_in, den, mom, mag, den_out, mom_out, mag_out,
    U, Q, M, QL, QR, FX, PART, FY4, SX4, EZ, NBX, NBY,
    pack_lo, pack_hi, recv_lo, recv_hi, fold, block, circ_far, circ_near, ring_far, ring_near, col_r, col_l,
    shift_ref, frac_ref, load_sem,
    col_send, col_recv, row_send, row_recv, far_send, far_recv, near_send, near_recv,
):
    gx = lax.axis_index("gx")
    gy = lax.axis_index("gy")
    at_low = gx == 0
    at_high = gx == gxn - 1
    at_end = jnp.logical_or(at_low, at_high)
    not_low = gx > 0
    not_high = gx < gxn - 1
    below_gx = lax.max(gx - 1, 0)
    above_gx = lax.min(gx + 1, gxn - 1)
    other_end = gxn - 1 - gx
    east = lax.rem(gy + 1, gyn)
    west = lax.rem(gy + gyn - 1, gyn)

    rows8 = row_iota((8, LANES))
    first_row = rows8 == 0
    last_row = rows8 == 7
    near = lane_iota((8, 128)) < 64

    def previous(k):
        return sum(AHEAD) - k if k in AHEAD else (k + RING - 1) % RING

    def following(k):
        return sum(AHEAD) - k if k in AHEAD else (k + 1) % RING

    def row_before(before, here):
        return roll(jnp.where(last_row, before, here), 1, 0)

    def row_after(here, after):
        return roll(jnp.where(first_row, after, here), -1, 0)

    def lane_before(x):
        return jnp.concatenate([roll(x[:, 256:384], 1, 1), x[:, 0:128], x[:, 128:256]], axis=1)

    def lane_after(x):
        return jnp.concatenate([x[:, 128:256], x[:, 256:384], roll(x[:, 0:128], -1, 1)], axis=1)

    spots = lane_iota((8, LANES))
    columns = 3 * (spots & 127) + (spots >> 7)
    spot_of_row = lane_iota((LANES, LANES))
    permutation = jnp.where(row_iota((LANES, LANES)) == 3 * (spot_of_row & 127) + (spot_of_row >> 7), 1.0, 0.0)

    loads = [
        pltpu.make_async_copy(den, block.at[D], load_sem.at[0]),
        pltpu.make_async_copy(mom, block.at[MX : MZ + 1], load_sem.at[1]),
        pltpu.make_async_copy(mag, block.at[BX : BZ + 1], load_sem.at[2]),
        pltpu.make_async_copy(shift_in, shift_ref, load_sem.at[3]),
        pltpu.make_async_copy(frac_in, frac_ref, load_sem.at[4]),
    ]
    for load in loads:
        load.start()

    barrier = pltpu.get_barrier_semaphore()

    def greet(to_gx, to_gy):
        pl.semaphore_signal(barrier, inc=1, device_id=(to_gx, to_gy), device_id_type=MESH)

    @pl.when(at_end)
    def _():
        for g in range(gyn):
            greet(other_end, g)
        for i in range(1, gyn):
            greet(gx, lax.rem(gy + i, gyn))

    @pl.when(jnp.logical_not(at_end))
    def _():
        greet(gx, east)
        greet(gx, west)

    @pl.when(not_low)
    def _():
        greet(below_gx, gy)

    @pl.when(not_high)
    def _():
        greet(above_gx, gy)

    for load in loads:
        load.wait()

    def packed(tiles, first):
        def at(field, row):
            return tiles[field] if row == first else roll(tiles[field], row - first, 0)

        return [
            jnp.where(rows8 < 3, at(0, 0), jnp.where(rows8 < 6, at(1, 3), at(6, 6))),
            jnp.where(rows8 < 3, at(2, 0), jnp.where(rows8 < 6, at(3, 3), at(6, 4))),
            jnp.where(rows8 < 3, at(4, 0), at(5, 3)),
        ]

    def unpacked(tiles, first):
        def move(x, row):
            return x if row == first else roll(x, first - row, 0)

        sixth = jnp.where(((rows8 - first) & 7) < 2, move(tiles[0], 6), move(tiles[1], 4))
        return (
            move(tiles[0], 0), move(tiles[0], 3), move(tiles[1], 0), move(tiles[1], 3),
            move(tiles[2], 0), move(tiles[2], 3), sixth,
        )

    def pack_edge(ref, slot, tiles, outer, inner):
        for group, first in enumerate((outer, inner)):
            for part, tile in enumerate(packed(tiles, first)):
                for lane in range(3):
                    ref[slot, group, lane, part] = tile[:, 128 * lane : 128 * (lane + 1)]

    def load_pack(ref, slot, group):
        return [jnp.concatenate([ref[slot, group, lane, part] for lane in range(3)], axis=1) for part in range(3)]

    def pack_edges(slot, low_tiles, high_tiles):
        pack_edge(pack_lo, slot, low_tiles, 0, 3)
        pack_edge(pack_hi, slot, high_tiles, 5, 2)

    def edges_of_block(slot):
        pack_edges(slot, [U[f, 0] for f in range(7)], [U[f, OWN - 1] for f in range(7)])

    lane = lane_iota((8, 128))

    def at_ends(run):
        for end, pack in ((at_low, pack_lo), (at_high, pack_hi)):

            @pl.when(end)
            def _(pack=pack):
                run(pack)

    def fold_edge(slot):
        def run(pack):
            for group in range(GROUPS):
                for part in range(3):
                    third = pack[slot, group, 2, part]
                    fold[slot, group, 0, part] = jnp.where(lane < 86, pack[slot, group, 0, part], roll(third, 86, 1))
                    fold[slot, group, 1, part] = jnp.where(lane < 85, pack[slot, group, 1, part], roll(third, 43, 1))

        at_ends(run)

    def to_far(slot, group, g):
        return pltpu.make_async_remote_copy(
            src_ref=fold.at[slot, group], dst_ref=circ_far.at[slot, group, gy],
            send_sem=far_send.at[group, g], recv_sem=far_recv.at[slot, group, gy],
            device_id=(other_end, g), device_id_type=MESH,
        )

    def from_far(slot, group, g):
        return pltpu.make_async_remote_copy(
            src_ref=fold.at[slot, group], dst_ref=circ_far.at[slot, group, g],
            send_sem=far_send.at[group, g], recv_sem=far_recv.at[slot, group, g],
            device_id=(other_end, g), device_id_type=MESH,
        )

    def to_near(slot, i):
        return pltpu.make_async_remote_copy(
            src_ref=fold.at[slot, 0], dst_ref=circ_near.at[slot, gy],
            send_sem=near_send.at[i], recv_sem=near_recv.at[slot, i],
            device_id=(gx, lax.rem(gy + i, gyn)), device_id_type=MESH,
        )

    def from_near(slot, i):
        sender = lax.rem(gy + gyn - i, gyn)
        return pltpu.make_async_remote_copy(
            src_ref=fold.at[slot, 0], dst_ref=circ_near.at[slot, sender],
            send_sem=near_send.at[i], recv_sem=near_recv.at[slot, i],
            device_id=(gx, sender), device_id_type=MESH,
        )

    def down(slot):
        return pltpu.make_async_remote_copy(
            src_ref=pack_lo.at[slot], dst_ref=recv_hi.at[slot], send_sem=row_send.at[0], recv_sem=row_recv.at[slot, 0],
            device_id=(below_gx, gy), device_id_type=MESH,
        )

    def up(slot):
        return pltpu.make_async_remote_copy(
            src_ref=pack_hi.at[slot], dst_ref=recv_lo.at[slot], send_sem=row_send.at[1], recv_sem=row_recv.at[slot, 1],
            device_id=(above_gx, gy), device_id_type=MESH,
        )

    def start_far(slot):
        @pl.when(at_end)
        def _():
            for g in range(gyn):
                to_far(slot, 0, g).start()

    def start_ahead(slot):
        @pl.when(at_end)
        def _():
            for i in range(1, gyn):
                to_near(slot, i).start()
            for g in range(gyn):
                to_far(slot, 1, g).start()

    def start_rows(slot):
        @pl.when(not_low)
        def _():
            down(slot).start()

        @pl.when(not_high)
        def _():
            up(slot).start()

    def finish_sends(slot):
        @pl.when(at_end)
        def _():
            for group in range(2):
                for g in range(gyn):
                    to_far(slot, group, g).wait_send()
            for i in range(1, gyn):
                to_near(slot, i).wait_send()

        @pl.when(not_low)
        def _():
            down(slot).wait_send()

        @pl.when(not_high)
        def _():
            up(slot).wait_send()

    to_west = pltpu.make_async_remote_copy(
        src_ref=block.at[:, :, :, 0:128], dst_ref=col_r, send_sem=col_send.at[0], recv_sem=col_recv.at[0],
        device_id=(gx, west), device_id_type=MESH,
    )
    to_east = pltpu.make_async_remote_copy(
        src_ref=block.at[:, :, :, 128:256], dst_ref=col_l, send_sem=col_send.at[1], recv_sem=col_recv.at[1],
        device_id=(gx, east), device_id_type=MESH,
    )

    def interleaved(x, start, stop):
        flat = x.reshape(7 * OWN * 8, stop - start)
        out = jnp.dot(
            flat, permutation[start:stop], precision=lax.Precision.HIGHEST, preferred_element_type=jnp.float32
        )
        return out.reshape(7, OWN, 8, LANES)

    own_columns = interleaved(block[...], 0, 256)
    U[:, 0:OWN] = own_columns
    edges_of_block(0)
    fold_edge(0)
    pl.semaphore_wait(barrier, jnp.where(at_end, 2 * gyn, 4))

    start_far(0)
    to_west.start()
    to_east.start()
    start_ahead(0)
    to_west.wait()
    to_east.wait()

    near = lane_iota((7, OWN, 8, 128)) < 64
    halo = interleaved(jnp.where(near, col_r[...], col_l[...]), 256, 384)
    U[:, 0:OWN] = U[:, 0:OWN] + halo
    for field in range(7):
        for k in (ABOVE, BELOW) + AHEAD:
            U[field, k] = U[field, 0]
    edges_of_block(0)
    start_rows(0)

    def ghosts_of_neighbours(slot):
        @pl.when(not_high)
        def _():
            outer = unpacked(load_pack(recv_hi, slot, 0), 0)
            inner = unpacked(load_pack(recv_hi, slot, 1), 3)
            for f in range(7):
                U[f, ABOVE] = jnp.where(rows8 < 3, outer[f], inner[f])

        @pl.when(not_low)
        def _():
            outer = unpacked(load_pack(recv_lo, slot, 0), 5)
            inner = unpacked(load_pack(recv_lo, slot, 1), 2)
            for f in range(7):
                U[f, BELOW] = jnp.where(rows8 >= 5, outer[f], inner[f])

    wrapped = jnp.where(columns < 320, columns, columns - LANES)

    def window(ring, moved):
        origin = lax.rem(gy * 256 + moved + 512 * gyn, 256 * gyn)
        first_block = lax.div(origin, 256)
        offset = lax.rem(origin, 256)
        sources = []
        for i in (0, 1, jnp.where(offset < 128, -1, 2)):
            ahead = offset - 256 * i
            whole = lax.div(ahead + 2 * LANES, 3)
            phase = lax.rem(ahead + 2 * LANES, 3)
            place = lax.rem(first_block + i + gyn, gyn)
            turns = []
            for j in range(3):
                turns.append(lax.rem(4 * 128 - whole - lax.div(phase + j, 3), 128))
            at = wrapped + ahead
            sources.append((place, phase, turns, jnp.logical_and(at >= 0, at < 256)))
        out = []
        for part in range(3):
            spans = []
            for place, phase, turns, _ in sources:
                one, two = ring[place, 0, part], ring[place, 1, part]
                three = jnp.where(lane < 42, roll(one, -86, 1), roll(two, -43, 1))
                vectors = (one, two, three)
                picked = [
                    jnp.where(phase == 0, vectors[j], jnp.where(phase == 1, vectors[(j + 1) % 3], vectors[(j + 2) % 3]))
                    for j in range(3)
                ]
                spans.append(jnp.concatenate([pltpu.roll(x, turn, 1) for x, turn in zip(picked, turns)], axis=1))
            out.append(jnp.where(sources[0][3], spans[0], jnp.where(sources[1][3], spans[1], spans[2])))
        return out

    def blended(x, fraction, towards):
        return (1.0 - fraction) * x + fraction * (lane_after(x) if towards == 1 else lane_before(x))

    def low_ghosts(f, raw, fraction):
        ghost = blended(raw, fraction, -1)
        far_rows = roll(raw, 1, 0)
        own = roll(blended(U[f, 0], fraction, 1), 1, 0)
        U[f, BELOW] = jnp.where(rows8 >= 5, ghost, jnp.where(first_row, far_rows, own))
        U[f, ABOVE] = jnp.where(rows8 >= 6, far_rows, U[f, ABOVE])

    def high_ghosts(f, raw, fraction):
        ghost = blended(raw, fraction, 1)
        far_rows = roll(raw, 6, 0)
        own = roll(blended(U[f, OWN - 1], fraction, -1), -2, 0)
        U[f, ABOVE] = jnp.where(rows8 < 3, ghost, jnp.where(rows8 < 6, own, far_rows))
        U[f, BELOW] = jnp.where(rows8 < 2, far_rows, U[f, BELOW])

    def ghosts_of_far_end(slot, n):
        shift = shift_ref[n]
        fraction = frac_ref[n]

        @pl.when(at_end)
        def _():
            for g in range(gyn):
                from_far(slot, 0, g).wait_recv()
            ring_far[0] = circ_far[slot, 0]

        @pl.when(at_low)
        def _():
            for f, raw in enumerate(unpacked(window(ring_far.at[0], -shift), 5)):
                low_ghosts(f, raw, fraction)

        @pl.when(at_high)
        def _():
            for f, raw in enumerate(unpacked(window(ring_far.at[0], shift), 0)):
                high_ghosts(f, raw, fraction)

    def rows_ahead(slot, n):
        shift, shift_next = shift_ref[n], shift_ref[n + 1]
        fraction = frac_ref[n]
        left, right = AHEAD

        @pl.when(at_end)
        def _():
            for i in range(1, gyn):
                from_near(slot, i).wait_recv()
            for g in range(gyn):
                from_far(slot, 1, g).wait_recv()
            ring_far[1] = circ_far[slot, 1]
            ring_near[...] = circ_near[slot]

        @pl.when(at_low)
        def _():
            ring_near[gy] = fold[slot, 0]
            outer = window(ring_far.at[0], -shift_next)
            inner = unpacked(window(ring_far.at[1], -shift_next), 2)
            beyond = window(ring_near, shift - shift_next)
            rows_a = unpacked(outer, 5)
            ghost = unpacked([blended(x, fraction, 1) for x in beyond], 0)
            mirror = unpacked([blended(x, fraction, -1) for x in outer], 3)
            raw = unpacked(beyond, 6)
            for f in range(7):
                U[f, left] = jnp.where(first_row, raw[f], jnp.where(rows8 < 5, inner[f], rows_a[f]))
                U[f, right] = jnp.where(rows8 < 3, ghost[f], jnp.where(rows8 < 6, mirror[f], raw[f]))

        @pl.when(at_high)
        def _():
            ring_near[gy] = fold[slot, 0]
            outer = window(ring_far.at[0], shift_next)
            inner = unpacked(window(ring_far.at[1], shift_next), 3)
            beyond = window(ring_near, shift_next - shift)
            rows_a = unpacked(outer, 0)
            ghost = unpacked([blended(x, fraction, -1) for x in beyond], 5)
            mirror = unpacked([blended(x, fraction, 1) for x in outer], 2)
            raw = unpacked(beyond, 7)
            for f in range(7):
                U[f, left] = jnp.where(rows8 < 2, raw[f], jnp.where(rows8 < 5, mirror[f], ghost[f]))
                U[f, right] = jnp.where(rows8 < 3, rows_a[f], jnp.where(last_row, raw[f], inner[f]))

    def ghosts_from_ahead(n):
        fraction = frac_ref[n]

        @pl.when(at_low)
        def _():
            for f in range(7):
                low_ghosts(f, U[f, AHEAD[0]], fraction)

        @pl.when(at_high)
        def _():
            for f in range(7):
                high_ghosts(f, U[f, AHEAD[1]], fraction)

    def minmod(a, b):
        return jnp.maximum(jnp.minimum(a, b), 0.0) + jnp.minimum(jnp.maximum(a, b), 0.0)

    def signal(density, speed, squared):
        total = density + squared
        return jnp.abs(speed) + jnp.abs(total) * lax.rsqrt(total * density)

    def riemann(left, right, normal, wanted):
        dl, vnl, vtl, vsl, btl, bsl = left
        dr, vnr, vtr, vsr, btr, bsr = right
        n2 = normal * normal
        tl = btl * btl + bsl * bsl
        tr = btr * btr + bsr * bsr
        fastest = jnp.maximum(signal(dl, vnl, n2 + tl), signal(dr, vnr, n2 + tr))
        ul = vnl + fastest
        ur = vnr - fastest
        out = {}
        if wanted != (4,):
            al = dl * ul
            ar = dr * ur
        if 0 in wanted:
            out[0] = al + ar
        if 1 in wanted:
            out[1] = (al * vnl + ar * vnr) + ((dl + dr) + (0.5 * (tl + tr) - n2))
        if 2 in wanted:
            out[2] = (al * vtl + ar * vtr) - normal * (btl + btr)
        if 3 in wanted:
            out[3] = (al * vsl + ar * vsr) - normal * (bsl + bsr)
        if 4 in wanted:
            out[4] = (btl * ul + btr * ur) - normal * (vtl + vtr)
        if 5 in wanted:
            out[5] = (bsl * ul + bsr * ur) - normal * (vsl + vsr)
        return out

    def primitives(k, density, mx, my, mz, bz, bx, bx_after, by):
        inverse = 1.0 / density
        Q[0, k] = density
        Q[VX, k] = mx * inverse
        Q[VY, k] = my * inverse
        Q[VZ, k] = mz * inverse
        Q[CX, k] = 0.5 * (bx + row_after(bx, bx_after))
        Q[CY, k] = 0.5 * (by + lane_after(by))
        Q[QBZ, k] = bz

    def initial_primitives(k):
        primitives(k, *(U[f, k] for f in (D, MX, MY, MZ, BZ, BX)), U[BX, following(k)], U[BY, k])

    X_STATE = (0, VX, VY, VZ, CY, QBZ)
    Y_STATE = (0, VY, VX, VZ, CX, QBZ)

    def finish_fluxes(k, fx, fy, stride, mx, my, cells):
        half = 0.5 * stride
        if 0 in fx:
            for spot, part in enumerate((0, 1, 2, 3, 5)):
                FX[spot, k] = fx[part]
        FY4[k] = fy[4]
        SX4[k] = fx[4] + lane_before(fx[4])
        if cells:
            for spot, (field, px, py) in enumerate(((D, 0, 0), (MX, 1, 2), (MY, 2, 1), (MZ, 3, 3), (BZ, 5, 5))):
                value = U[field, k] - half * ((lane_after(fy[py]) - fy[py]) - fx[px])
                if field == MX:
                    value += (stride * 2.0 * OMEGA) * my
                if field == MY:
                    value -= (stride * (2.0 - QSHEAR) * OMEGA) * mx
                PART[spot, k] = value

    ALL = (0, 1, 2, 3, 4, 5)

    def first_order(k, stride):
        left = [row_before(Q[i, previous(k)], Q[i, k]) for i in X_STATE]
        fx = riemann(left, [Q[i, k] for i in X_STATE], U[BX, k], ALL)
        right = [Q[i, k] for i in Y_STATE]
        fy = riemann([lane_before(q) for q in right], right, U[BY, k], ALL)
        finish_fluxes(k, fx, fy, stride, U[MX, k], U[MY, k], True)

    def slopes(k):
        for spot, i in enumerate(X_STATE):
            here = Q[i, k]
            gradient = 0.5 * minmod(here - row_before(Q[i, previous(k)], here), row_after(here, Q[i, following(k)]) - here)
            QL[spot, k] = here + gradient
            QR[spot, k] = here - gradient

    def second_order(k, stride, last):
        cells = k < OWN or not last
        x_wanted = ALL if cells or k == ABOVE else (4,)
        y_wanted = ALL if cells else (4,)
        left = [row_before(QL[i, previous(k)], QL[i, k]) for i in range(6)]
        fx = riemann(left, [QR[i, k] for i in range(6)], NBX[k], x_wanted)
        left, right = [], []
        for i in Y_STATE:
            here = Q[i, k]
            behind = here - lane_before(here)
            gradient = 0.5 * minmod(behind, lane_after(behind))
            left.append(lane_before(here + gradient))
            right.append(here - gradient)
        fy = riemann(left, right, NBY[k], y_wanted)
        finish_fluxes(k, fx, fy, stride, M[0, k], M[1, k], cells)

    def corner(k):
        return 0.125 * (FY4[k] + row_before(FY4[previous(k)], FY4[k]) - SX4[k])

    def face_x(k, emf, stride):
        EZ[k] = emf
        return U[BX, k] - stride * (lane_after(emf) - emf)

    def face_y(k, stride):
        emf = EZ[k]
        return U[BY, k] + stride * (row_after(emf, EZ[following(k)]) - emf)

    def cells_of(k, stride):
        return [PART[i, k] - (0.5 * stride) * row_after(FX[i, k], FX[i, following(k)]) for i in range(5)]

    def advance(n, last, ring, ready_primitives=(), ready_fluxes=(), send_edges=None):
        fraction = frac_ref[n]

        def tiles(run):
            for k in ring:
                run(k)

        stride = 0.5 * TIMESTEP
        for k in ring:
            if k not in ready_primitives:
                initial_primitives(k)
        for k in ring:
            if k not in ready_fluxes:
                first_order(k, stride)

        def predicted_x(k):
            NBX[k] = face_x(k, corner(k), stride)

        tiles(predicted_x)

        def predicted_cells(k):
            density, mx, my, mz, bz = cells_of(k, stride)
            by = face_y(k, stride)
            NBY[k] = by
            M[0, k] = mx
            M[1, k] = my
            primitives(k, density, mx, my, mz, bz, NBX[k], NBX[following(k)], by)

        tiles(predicted_cells)

        tiles(slopes)
        if not last:
            tiles(lambda k: second_order(k, TIMESTEP, False))
        def new_cells(k):
            for field, value in zip((D, MX, MY, MZ, BZ), cells_of(k, TIMESTEP)):
                U[field, k] = value
            U[BY, k] = face_y(k, TIMESTEP)

        if ring == AHEAD:
            left, right = AHEAD
            emf_l, emf_r = corner(left), corner(right)
            from_low = blended(roll(emf_r, -6, 0), fraction, 1)
            from_high = blended(roll(emf_l, -2, 0), fraction, -1)
            remote = jnp.where(at_low, from_low, from_high)
            emf_r = jnp.where(first_row, 0.5 * (emf_r + remote), emf_r)
            U[BX, left] = face_x(left, emf_l, TIMESTEP)
            U[BX, right] = face_x(right, emf_r, TIMESTEP)
            tiles(new_cells)
            return
        kept = range(OWN) if last else ring

        def mended(emf, remote_row, towards, ours):
            remote = blended(remote_row, fraction, towards)
            return jnp.where(jnp.logical_and(first_row, ours), 0.5 * (emf + remote), emf)

        def fixed_corners(ks):
            emfs = {k: corner(k) for k in ks}
            if 0 in ks:
                emfs[0] = mended(emfs[0], roll(emfs[BELOW], -1, 0), -1, at_low)
                emfs[ABOVE] = mended(emfs[ABOVE], roll(emfs[ABOVE], -6, 0), 1, at_high)
            return emfs

        if not last:
            emfs = fixed_corners(ring)
        else:
            early, late = (0, OWN - 1, ABOVE, BELOW), range(1, OWN - 1)
            for k in early:
                second_order(k, TIMESTEP, True)
            emfs = fixed_corners(early)
            new_bx = {k: face_x(k, emfs[k], TIMESTEP) for k in early}

            def edge_tiles(k):
                density, mx, my, mz, bz = cells_of(k, TIMESTEP)
                return [density, mx, my, mz, new_bx[k], face_y(k, TIMESTEP), bz]

            send_edges(edge_tiles)
            for k in late:
                second_order(k, TIMESTEP, True)
            emfs.update({k: corner(k) for k in (*late, OWN - 1)})
        for k in kept:
            U[BX, k] = face_x(k, emfs[k], TIMESTEP)
        for k in ring:
            if k not in kept:
                EZ[k] = emfs[k]
        for k in kept:
            new_cells(k)

    rounds = STEPS // 2

    def two_steps(r, carry):
        slot = lax.rem(r, 2)

        for k in range(OWN - 1):
            initial_primitives(k)
        for k in range(1, OWN - 1):
            first_order(k, 0.5 * TIMESTEP)

        @pl.when(not_high)
        def _():
            down(slot).wait_recv()

        @pl.when(not_low)
        def _():
            up(slot).wait_recv()

        ghosts_of_neighbours(slot)
        ghosts_of_far_end(slot, 2 * r)
        advance(2 * r, False, MAIN, tuple(range(OWN - 1)), tuple(range(1, OWN - 1)))
        rows_ahead(slot, 2 * r)

        @pl.when(at_end)
        def _():
            advance(2 * r, False, AHEAD)

        ghosts_from_ahead(2 * r + 1)
        finish_sends(slot)

        def send_edges(edge_tiles):
            @pl.when(r < rounds - 1)
            def _():
                pack_edges(1 - slot, edge_tiles(0), edge_tiles(OWN - 1))
                fold_edge(1 - slot)
                start_far(1 - slot)
                start_rows(1 - slot)
                start_ahead(1 - slot)

        advance(2 * r + 1, True, MAIN, send_edges=send_edges)
        return carry

    lax.fori_loop(0, rounds, two_steps, 0)

    flat = U[:, 0:OWN].reshape(7 * OWN * 8, LANES)
    out = lax.dot_general(
        flat, permutation[0:256], (((1,), (1,)), ((), ())),
        precision=lax.Precision.HIGHEST, preferred_element_type=jnp.float32,
    ).reshape(7, 8 * OWN, 256)
    den_out[...] = out[D]
    mom_out[...] = out[MX : MZ + 1]
    mag_out[...] = out[BX : BZ + 1]


def scratch(gyn):
    tile = (TILES, 8, LANES)
    f32 = jnp.float32
    vmem = lambda *shape: pltpu.VMEM(shape, f32)
    dma = pltpu.SemaphoreType.DMA
    return [
        vmem(7, *tile), vmem(7, *tile), vmem(2, *tile), vmem(6, *tile), vmem(6, *tile), vmem(5, *tile), vmem(5, *tile),
        vmem(*tile), vmem(*tile), vmem(*tile), vmem(*tile), vmem(*tile),
        *(vmem(2, GROUPS, 3, 3, 8, 128) for _ in range(4)), vmem(2, GROUPS, 2, 3, 8, 128),
        vmem(7, OWN, 8, 256), vmem(2, GROUPS, gyn, 2, 3, 8, 128), vmem(2, gyn, 2, 3, 8, 128),
        vmem(GROUPS, gyn, 2, 3, 8, 128), vmem(gyn, 2, 3, 8, 128), vmem(7, OWN, 8, 128), vmem(7, OWN, 8, 128),
        pltpu.SMEM((STEPS,), jnp.int32), pltpu.SMEM((STEPS,), f32), dma((5,)),
        dma((2,)), dma((2,)), dma((2,)), dma((2, 2)),
        dma((GROUPS, gyn)), dma((2, GROUPS, gyn)), dma((gyn,)), dma((2, gyn)),
    ]


def solution(mesh):
    gxn, gyn = mesh.shape["gx"], mesh.shape["gy"]

    def per_device(density, momentum, magnetic, shear_shift, shear_frac):
        return pl.pallas_call(
            functools.partial(kernel, gxn, gyn),
            name="shearing_box",
            out_shape=tuple(jax.ShapeDtypeStruct(a.shape, jnp.float32) for a in (density, momentum, magnetic)),
            in_specs=[pl.BlockSpec(memory_space=pl.ANY)] * 5,
            out_specs=tuple(pl.BlockSpec(memory_space=pltpu.VMEM) for _ in range(3)),
            scratch_shapes=scratch(gyn),
            compiler_params=pltpu.CompilerParams(
                collective_id=0, has_side_effects=True, vmem_limit_bytes=48 * 1024 * 1024
            ),
        )(
            shear_shift,
            shear_frac,
            density.reshape(OWN, 8, 256),
            momentum.reshape(3, OWN, 8, 256),
            magnetic.reshape(3, OWN, 8, 256),
        )

    return jax.shard_map(
        per_device,
        mesh=mesh,
        in_specs=(P("gx", "gy"), P(None, "gx", "gy"), P(None, "gx", "gy"), P(), P()),
        out_specs=(P("gx", "gy"), P(None, "gx", "gy"), P(None, "gx", "gy")),
        check_vma=False,
    )
```

```python
import functools

import jax
import jax.numpy as jnp
from jax import lax
from jax.experimental import pallas as pl
from jax.experimental.pallas import tpu as pltpu
from jax.sharding import PartitionSpec as P

STEPS = 8
OMEGA = 0.5
QSHEAR = 1.5
TIMESTEP = 0.1
MESH = pl.DeviceIdType.MESH

D, MX, MY, MZ, BX, BY, BZ = range(7)
VX, VY, VZ, CY, CX, QBZ = 1, 2, 3, 4, 5, 6
OWN = 4
ABOVE, BELOW = OWN, OWN + 1
RING = OWN + 2
AHEAD = (RING, RING + 1)
MAIN = tuple(range(RING))
TILES = RING + 2
LANES = 384
GROUPS = 2


def roll(x, shift, axis):
    return pltpu.roll(x, shift % x.shape[axis], axis)


def row_iota(shape):
    return lax.broadcasted_iota(jnp.int32, shape, len(shape) - 2)


def lane_iota(shape):
    return lax.broadcasted_iota(jnp.int32, shape, len(shape) - 1)


def kernel(
    gxn, gyn, shift_in, frac_in, den, mom, mag, den_out, mom_out, mag_out,
    U, Q, M, QL, QR, FX, PART, FY4, SX4, EZ, NBX, NBY,
    pack_lo, pack_hi, recv_lo, recv_hi, fold, block, circ_far, circ_near, ring_far, ring_near, col_r, col_l,
    shift_ref, frac_ref, load_sem,
    col_send, col_recv, row_send, row_recv, far_send, far_recv, near_send, near_recv,
):
    gx = lax.axis_index("gx")
    gy = lax.axis_index("gy")
    at_low = gx == 0
    at_high = gx == gxn - 1
    at_end = jnp.logical_or(at_low, at_high)
    not_low = gx > 0
    not_high = gx < gxn - 1
    below_gx = lax.max(gx - 1, 0)
    above_gx = lax.min(gx + 1, gxn - 1)
    other_end = gxn - 1 - gx
    east = lax.rem(gy + 1, gyn)
    west = lax.rem(gy + gyn - 1, gyn)
    far_order = sorted(range(gyn), key=lambda i: -min(i, gyn - i))

    rows8 = row_iota((8, LANES))
    first_row = rows8 == 0
    last_row = rows8 == 7
    near = lane_iota((8, 128)) < 64

    def previous(k):
        return sum(AHEAD) - k if k in AHEAD else (k + RING - 1) % RING

    def following(k):
        return sum(AHEAD) - k if k in AHEAD else (k + 1) % RING

    def row_before(before, here):
        return roll(jnp.where(last_row, before, here), 1, 0)

    def row_after(here, after):
        return roll(jnp.where(first_row, after, here), -1, 0)

    def lane_before(x):
        return jnp.concatenate([roll(x[:, 256:384], 1, 1), x[:, 0:128], x[:, 128:256]], axis=1)

    def lane_after(x):
        return jnp.concatenate([x[:, 128:256], x[:, 256:384], roll(x[:, 0:128], -1, 1)], axis=1)

    spots = lane_iota((8, LANES))
    columns = 3 * (spots & 127) + (spots >> 7)
    spot_of_row = lane_iota((LANES, LANES))
    permutation = jnp.where(row_iota((LANES, LANES)) == 3 * (spot_of_row & 127) + (spot_of_row >> 7), 1.0, 0.0)

    loads = [
        pltpu.make_async_copy(den, block.at[D], load_sem.at[0]),
        pltpu.make_async_copy(mom, block.at[MX : MZ + 1], load_sem.at[1]),
        pltpu.make_async_copy(mag, block.at[BX : BZ + 1], load_sem.at[2]),
        pltpu.make_async_copy(shift_in, shift_ref, load_sem.at[3]),
        pltpu.make_async_copy(frac_in, frac_ref, load_sem.at[4]),
    ]
    for load in loads:
        load.start()

    barrier = pltpu.get_barrier_semaphore()

    def greet(to_gx, to_gy):
        pl.semaphore_signal(barrier, inc=1, device_id=(to_gx, to_gy), device_id_type=MESH)

    @pl.when(at_end)
    def _():
        for i in far_order:
            greet(other_end, lax.rem(gy + i, gyn))
        for i in range(1, gyn):
            greet(gx, lax.rem(gy + i, gyn))

    @pl.when(jnp.logical_not(at_end))
    def _():
        greet(gx, east)
        greet(gx, west)

    @pl.when(not_low)
    def _():
        greet(below_gx, gy)

    @pl.when(not_high)
    def _():
        greet(above_gx, gy)

    for load in loads:
        load.wait()

    def packed(tiles, first):
        def at(field, row):
            return tiles[field] if row == first else roll(tiles[field], row - first, 0)

        return [
            jnp.where(rows8 < 3, at(0, 0), jnp.where(rows8 < 6, at(1, 3), at(6, 6))),
            jnp.where(rows8 < 3, at(2, 0), jnp.where(rows8 < 6, at(3, 3), at(6, 4))),
            jnp.where(rows8 < 3, at(4, 0), at(5, 3)),
        ]

    def unpacked(tiles, first):
        def move(x, row):
            return x if row == first else roll(x, first - row, 0)

        sixth = jnp.where(((rows8 - first) & 7) < 2, move(tiles[0], 6), move(tiles[1], 4))
        return (
            move(tiles[0], 0), move(tiles[0], 3), move(tiles[1], 0), move(tiles[1], 3),
            move(tiles[2], 0), move(tiles[2], 3), sixth,
        )

    def pack_edge(ref, slot, tiles, outer, inner):
        for group, first in enumerate((outer, inner)):
            for part, tile in enumerate(packed(tiles, first)):
                for lane in range(3):
                    ref[slot, group, lane, part] = tile[:, 128 * lane : 128 * (lane + 1)]

    def load_pack(ref, slot, group):
        return [jnp.concatenate([ref[slot, group, lane, part] for lane in range(3)], axis=1) for part in range(3)]

    def pack_edges(slot, low_tiles, high_tiles):
        pack_edge(pack_lo, slot, low_tiles, 0, 3)
        pack_edge(pack_hi, slot, high_tiles, 5, 2)

    def edges_of_block(slot):
        pack_edges(slot, [U[f, 0] for f in range(7)], [U[f, OWN - 1] for f in range(7)])

    lane = lane_iota((8, 128))

    def at_ends(run):
        for end, pack in ((at_low, pack_lo), (at_high, pack_hi)):

            @pl.when(end)
            def _(pack=pack):
                run(pack)

    def fold_edge(slot):
        def run(pack):
            for group in range(GROUPS):
                for part in range(3):
                    third = pack[slot, group, 2, part]
                    fold[slot, group, 0, part] = jnp.where(lane < 86, pack[slot, group, 0, part], roll(third, 86, 1))
                    fold[slot, group, 1, part] = jnp.where(lane < 85, pack[slot, group, 1, part], roll(third, 43, 1))

        at_ends(run)

    def to_far(slot, group, i):
        return pltpu.make_async_remote_copy(
            src_ref=fold.at[slot, group], dst_ref=circ_far.at[slot, group, gy],
            send_sem=far_send.at[group, i], recv_sem=far_recv.at[slot, group, gy],
            device_id=(other_end, lax.rem(gy + i, gyn)), device_id_type=MESH,
        )

    def from_far(slot, group, g):
        return pltpu.make_async_remote_copy(
            src_ref=fold.at[slot, group], dst_ref=circ_far.at[slot, group, g],
            send_sem=far_send.at[group, g], recv_sem=far_recv.at[slot, group, g],
            device_id=(other_end, g), device_id_type=MESH,
        )

    def to_near(slot, i):
        return pltpu.make_async_remote_copy(
            src_ref=fold.at[slot, 0], dst_ref=circ_near.at[slot, gy],
            send_sem=near_send.at[i], recv_sem=near_recv.at[slot, i],
            device_id=(gx, lax.rem(gy + i, gyn)), device_id_type=MESH,
        )

    def from_near(slot, i):
        sender = lax.rem(gy + gyn - i, gyn)
        return pltpu.make_async_remote_copy(
            src_ref=fold.at[slot, 0], dst_ref=circ_near.at[slot, sender],
            send_sem=near_send.at[i], recv_sem=near_recv.at[slot, i],
            device_id=(gx, sender), device_id_type=MESH,
        )

    def down(slot):
        return pltpu.make_async_remote_copy(
            src_ref=pack_lo.at[slot], dst_ref=recv_hi.at[slot], send_sem=row_send.at[0], recv_sem=row_recv.at[slot, 0],
            device_id=(below_gx, gy), device_id_type=MESH,
        )

    def up(slot):
        return pltpu.make_async_remote_copy(
            src_ref=pack_hi.at[slot], dst_ref=recv_lo.at[slot], send_sem=row_send.at[1], recv_sem=row_recv.at[slot, 1],
            device_id=(above_gx, gy), device_id_type=MESH,
        )

    def start_far(slot):
        @pl.when(at_end)
        def _():
            for i in far_order:
                to_far(slot, 0, i).start()

    def start_ahead(slot):
        @pl.when(at_end)
        def _():
            for i in range(1, gyn):
                to_near(slot, i).start()
            for i in far_order:
                to_far(slot, 1, i).start()

    def start_rows(slot):
        @pl.when(not_low)
        def _():
            down(slot).start()

        @pl.when(not_high)
        def _():
            up(slot).start()

    def finish_sends(slot):
        @pl.when(at_end)
        def _():
            for group in range(2):
                for g in range(gyn):
                    to_far(slot, group, g).wait_send()
            for i in range(1, gyn):
                to_near(slot, i).wait_send()

        @pl.when(not_low)
        def _():
            down(slot).wait_send()

        @pl.when(not_high)
        def _():
            up(slot).wait_send()

    to_west = pltpu.make_async_remote_copy(
        src_ref=block.at[:, :, :, 0:128], dst_ref=col_r, send_sem=col_send.at[0], recv_sem=col_recv.at[0],
        device_id=(gx, west), device_id_type=MESH,
    )
    to_east = pltpu.make_async_remote_copy(
        src_ref=block.at[:, :, :, 128:256], dst_ref=col_l, send_sem=col_send.at[1], recv_sem=col_recv.at[1],
        device_id=(gx, east), device_id_type=MESH,
    )

    def interleaved(x, start, stop):
        flat = x.reshape(7 * OWN * 8, stop - start)
        out = jnp.dot(
            flat, permutation[start:stop], precision=lax.Precision.HIGHEST, preferred_element_type=jnp.float32
        )
        return out.reshape(7, OWN, 8, LANES)

    own_columns = interleaved(block[...], 0, 256)
    U[:, 0:OWN] = own_columns
    edges_of_block(0)
    fold_edge(0)
    pl.semaphore_wait(barrier, jnp.where(at_end, 2 * gyn, 4))

    start_far(0)
    to_west.start()
    to_east.start()
    start_ahead(0)
    to_west.wait()
    to_east.wait()

    near = lane_iota((7, OWN, 8, 128)) < 64
    halo = interleaved(jnp.where(near, col_r[...], col_l[...]), 256, 384)
    U[:, 0:OWN] = U[:, 0:OWN] + halo
    for field in range(7):
        for k in (ABOVE, BELOW) + AHEAD:
            U[field, k] = U[field, 0]
    edges_of_block(0)
    start_rows(0)

    def ghosts_of_neighbours(slot):
        @pl.when(not_high)
        def _():
            outer = unpacked(load_pack(recv_hi, slot, 0), 0)
            inner = unpacked(load_pack(recv_hi, slot, 1), 3)
            for f in range(7):
                U[f, ABOVE] = jnp.where(rows8 < 3, outer[f], inner[f])

        @pl.when(not_low)
        def _():
            outer = unpacked(load_pack(recv_lo, slot, 0), 5)
            inner = unpacked(load_pack(recv_lo, slot, 1), 2)
            for f in range(7):
                U[f, BELOW] = jnp.where(rows8 >= 5, outer[f], inner[f])

    wrapped = jnp.where(columns < 320, columns, columns - LANES)

    def window(ring, moved):
        origin = lax.rem(gy * 256 + moved + 512 * gyn, 256 * gyn)
        first_block = lax.div(origin, 256)
        offset = lax.rem(origin, 256)
        sources = []
        for i in (0, 1, jnp.where(offset < 128, -1, 2)):
            ahead = offset - 256 * i
            whole = lax.div(ahead + 2 * LANES, 3)
            phase = lax.rem(ahead + 2 * LANES, 3)
            place = lax.rem(first_block + i + gyn, gyn)
            turns = []
            for j in range(3):
                turns.append(lax.rem(4 * 128 - whole - lax.div(phase + j, 3), 128))
            at = wrapped + ahead
            sources.append((place, phase, turns, jnp.logical_and(at >= 0, at < 256)))
        out = []
        for part in range(3):
            spans = []
            for place, phase, turns, _ in sources:
                one, two = ring[place, 0, part], ring[place, 1, part]
                three = jnp.where(lane < 42, roll(one, -86, 1), roll(two, -43, 1))
                vectors = (one, two, three)
                picked = [
                    jnp.where(phase == 0, vectors[j], jnp.where(phase == 1, vectors[(j + 1) % 3], vectors[(j + 2) % 3]))
                    for j in range(3)
                ]
                spans.append(jnp.concatenate([pltpu.roll(x, turn, 1) for x, turn in zip(picked, turns)], axis=1))
            out.append(jnp.where(sources[0][3], spans[0], jnp.where(sources[1][3], spans[1], spans[2])))
        return out

    def blended(x, fraction, towards):
        return (1.0 - fraction) * x + fraction * (lane_after(x) if towards == 1 else lane_before(x))

    def low_ghosts(f, raw, fraction):
        ghost = blended(raw, fraction, -1)
        far_rows = roll(raw, 1, 0)
        own = roll(blended(U[f, 0], fraction, 1), 1, 0)
        U[f, BELOW] = jnp.where(rows8 >= 5, ghost, jnp.where(first_row, far_rows, own))
        U[f, ABOVE] = jnp.where(rows8 >= 6, far_rows, U[f, ABOVE])

    def high_ghosts(f, raw, fraction):
        ghost = blended(raw, fraction, 1)
        far_rows = roll(raw, 6, 0)
        own = roll(blended(U[f, OWN - 1], fraction, -1), -2, 0)
        U[f, ABOVE] = jnp.where(rows8 < 3, ghost, jnp.where(rows8 < 6, own, far_rows))
        U[f, BELOW] = jnp.where(rows8 < 2, far_rows, U[f, BELOW])

    def ghosts_of_far_end(slot, n):
        shift = shift_ref[n]
        fraction = frac_ref[n]

        @pl.when(at_end)
        def _():
            for g in range(gyn):
                from_far(slot, 0, g).wait_recv()
            ring_far[0] = circ_far[slot, 0]

        @pl.when(at_low)
        def _():
            for f, raw in enumerate(unpacked(window(ring_far.at[0], -shift), 5)):
                low_ghosts(f, raw, fraction)

        @pl.when(at_high)
        def _():
            for f, raw in enumerate(unpacked(window(ring_far.at[0], shift), 0)):
                high_ghosts(f, raw, fraction)

    def rows_ahead(slot, n):
        shift, shift_next = shift_ref[n], shift_ref[n + 1]
        fraction = frac_ref[n]
        left, right = AHEAD

        @pl.when(at_end)
        def _():
            for i in range(1, gyn):
                from_near(slot, i).wait_recv()
            for g in range(gyn):
                from_far(slot, 1, g).wait_recv()
            ring_far[1] = circ_far[slot, 1]
            ring_near[...] = circ_near[slot]

        @pl.when(at_low)
        def _():
            ring_near[gy] = fold[slot, 0]
            outer = window(ring_far.at[0], -shift_next)
            inner = unpacked(window(ring_far.at[1], -shift_next), 2)
            beyond = window(ring_near, shift - shift_next)
            rows_a = unpacked(outer, 5)
            ghost = unpacked([blended(x, fraction, 1) for x in beyond], 0)
            mirror = unpacked([blended(x, fraction, -1) for x in outer], 3)
            raw = unpacked(beyond, 6)
            for f in range(7):
                U[f, left] = jnp.where(first_row, raw[f], jnp.where(rows8 < 5, inner[f], rows_a[f]))
                U[f, right] = jnp.where(rows8 < 3, ghost[f], jnp.where(rows8 < 6, mirror[f], raw[f]))

        @pl.when(at_high)
        def _():
            ring_near[gy] = fold[slot, 0]
            outer = window(ring_far.at[0], shift_next)
            inner = unpacked(window(ring_far.at[1], shift_next), 3)
            beyond = window(ring_near, shift_next - shift)
            rows_a = unpacked(outer, 0)
            ghost = unpacked([blended(x, fraction, -1) for x in beyond], 5)
            mirror = unpacked([blended(x, fraction, 1) for x in outer], 2)
            raw = unpacked(beyond, 7)
            for f in range(7):
                U[f, left] = jnp.where(rows8 < 2, raw[f], jnp.where(rows8 < 5, mirror[f], ghost[f]))
                U[f, right] = jnp.where(rows8 < 3, rows_a[f], jnp.where(last_row, raw[f], inner[f]))

    def ghosts_from_ahead(n):
        fraction = frac_ref[n]

        @pl.when(at_low)
        def _():
            for f in range(7):
                low_ghosts(f, U[f, AHEAD[0]], fraction)

        @pl.when(at_high)
        def _():
            for f in range(7):
                high_ghosts(f, U[f, AHEAD[1]], fraction)

    def minmod(a, b):
        return jnp.maximum(jnp.minimum(a, b), 0.0) + jnp.minimum(jnp.maximum(a, b), 0.0)

    def signal(density, speed, squared):
        total = density + squared
        return jnp.abs(speed) + jnp.abs(total) * lax.rsqrt(total * density)

    def riemann(left, right, normal, wanted):
        dl, vnl, vtl, vsl, btl, bsl = left
        dr, vnr, vtr, vsr, btr, bsr = right
        n2 = normal * normal
        tl = btl * btl + bsl * bsl
        tr = btr * btr + bsr * bsr
        fastest = jnp.maximum(signal(dl, vnl, n2 + tl), signal(dr, vnr, n2 + tr))
        ul = vnl + fastest
        ur = vnr - fastest
        out = {}
        if wanted != (4,):
            al = dl * ul
            ar = dr * ur
        if 0 in wanted:
            out[0] = al + ar
        if 1 in wanted:
            out[1] = (al * vnl + ar * vnr) + ((dl + dr) + (0.5 * (tl + tr) - n2))
        if 2 in wanted:
            out[2] = (al * vtl + ar * vtr) - normal * (btl + btr)
        if 3 in wanted:
            out[3] = (al * vsl + ar * vsr) - normal * (bsl + bsr)
        if 4 in wanted:
            out[4] = (btl * ul + btr * ur) - normal * (vtl + vtr)
        if 5 in wanted:
            out[5] = (bsl * ul + bsr * ur) - normal * (vsl + vsr)
        return out

    def primitives(k, density, mx, my, mz, bz, bx, bx_after, by):
        inverse = 1.0 / density
        Q[0, k] = density
        Q[VX, k] = mx * inverse
        Q[VY, k] = my * inverse
        Q[VZ, k] = mz * inverse
        Q[CX, k] = 0.5 * (bx + row_after(bx, bx_after))
        Q[CY, k] = 0.5 * (by + lane_after(by))
        Q[QBZ, k] = bz

    def initial_primitives(k):
        primitives(k, *(U[f, k] for f in (D, MX, MY, MZ, BZ, BX)), U[BX, following(k)], U[BY, k])

    X_STATE = (0, VX, VY, VZ, CY, QBZ)
    Y_STATE = (0, VY, VX, VZ, CX, QBZ)

    def finish_fluxes(k, fx, fy, stride, mx, my, cells):
        half = 0.5 * stride
        if 0 in fx:
            for spot, part in enumerate((0, 1, 2, 3, 5)):
                FX[spot, k] = fx[part]
        FY4[k] = fy[4]
        SX4[k] = fx[4] + lane_before(fx[4])
        if cells:
            for spot, (field, px, py) in enumerate(((D, 0, 0), (MX, 1, 2), (MY, 2, 1), (MZ, 3, 3), (BZ, 5, 5))):
                value = U[field, k] - half * ((lane_after(fy[py]) - fy[py]) - fx[px])
                if field == MX:
                    value += (stride * 2.0 * OMEGA) * my
                if field == MY:
                    value -= (stride * (2.0 - QSHEAR) * OMEGA) * mx
                PART[spot, k] = value

    ALL = (0, 1, 2, 3, 4, 5)

    def first_order(k, stride):
        left = [row_before(Q[i, previous(k)], Q[i, k]) for i in X_STATE]
        fx = riemann(left, [Q[i, k] for i in X_STATE], U[BX, k], ALL)
        right = [Q[i, k] for i in Y_STATE]
        fy = riemann([lane_before(q) for q in right], right, U[BY, k], ALL)
        finish_fluxes(k, fx, fy, stride, U[MX, k], U[MY, k], True)

    def slopes(k):
        for spot, i in enumerate(X_STATE):
            here = Q[i, k]
            gradient = 0.5 * minmod(here - row_before(Q[i, previous(k)], here), row_after(here, Q[i, following(k)]) - here)
            QL[spot, k] = here + gradient
            QR[spot, k] = here - gradient

    def second_order(k, stride, last):
        cells = k < OWN or not last
        x_wanted = ALL if cells or k == ABOVE else (4,)
        y_wanted = ALL if cells else (4,)
        left = [row_before(QL[i, previous(k)], QL[i, k]) for i in range(6)]
        fx = riemann(left, [QR[i, k] for i in range(6)], NBX[k], x_wanted)
        left, right = [], []
        for i in Y_STATE:
            here = Q[i, k]
            behind = here - lane_before(here)
            gradient = 0.5 * minmod(behind, lane_after(behind))
            left.append(lane_before(here + gradient))
            right.append(here - gradient)
        fy = riemann(left, right, NBY[k], y_wanted)
        finish_fluxes(k, fx, fy, stride, M[0, k], M[1, k], cells)

    def corner(k):
        return 0.125 * (FY4[k] + row_before(FY4[previous(k)], FY4[k]) - SX4[k])

    def face_x(k, emf, stride):
        EZ[k] = emf
        return U[BX, k] - stride * (lane_after(emf) - emf)

    def face_y(k, stride):
        emf = EZ[k]
        return U[BY, k] + stride * (row_after(emf, EZ[following(k)]) - emf)

    def cells_of(k, stride):
        return [PART[i, k] - (0.5 * stride) * row_after(FX[i, k], FX[i, following(k)]) for i in range(5)]

    def advance(n, last, ring, ready_primitives=(), ready_fluxes=(), send_edges=None):
        fraction = frac_ref[n]

        def tiles(run):
            for k in ring:
                run(k)

        stride = 0.5 * TIMESTEP
        for k in ring:
            if k not in ready_primitives:
                initial_primitives(k)
        for k in ring:
            if k not in ready_fluxes:
                first_order(k, stride)

        def predicted_x(k):
            NBX[k] = face_x(k, corner(k), stride)

        tiles(predicted_x)

        def predicted_cells(k):
            density, mx, my, mz, bz = cells_of(k, stride)
            by = face_y(k, stride)
            NBY[k] = by
            M[0, k] = mx
            M[1, k] = my
            primitives(k, density, mx, my, mz, bz, NBX[k], NBX[following(k)], by)

        tiles(predicted_cells)

        tiles(slopes)
        if not last:
            tiles(lambda k: second_order(k, TIMESTEP, False))
        def new_cells(k):
            for field, value in zip((D, MX, MY, MZ, BZ), cells_of(k, TIMESTEP)):
                U[field, k] = value
            U[BY, k] = face_y(k, TIMESTEP)

        if ring == AHEAD:
            left, right = AHEAD
            emf_l, emf_r = corner(left), corner(right)
            from_low = blended(roll(emf_r, -6, 0), fraction, 1)
            from_high = blended(roll(emf_l, -2, 0), fraction, -1)
            remote = jnp.where(at_low, from_low, from_high)
            emf_r = jnp.where(first_row, 0.5 * (emf_r + remote), emf_r)
            U[BX, left] = face_x(left, emf_l, TIMESTEP)
            U[BX, right] = face_x(right, emf_r, TIMESTEP)
            tiles(new_cells)
            return
        kept = range(OWN) if last else ring

        def mended(emf, remote_row, towards, ours):
            remote = blended(remote_row, fraction, towards)
            return jnp.where(jnp.logical_and(first_row, ours), 0.5 * (emf + remote), emf)

        def fixed_corners(ks):
            emfs = {k: corner(k) for k in ks}
            if 0 in ks:
                emfs[0] = mended(emfs[0], roll(emfs[BELOW], -1, 0), -1, at_low)
                emfs[ABOVE] = mended(emfs[ABOVE], roll(emfs[ABOVE], -6, 0), 1, at_high)
            return emfs

        if not last:
            emfs = fixed_corners(ring)
        else:
            early, late = (0, OWN - 1, ABOVE, BELOW), range(1, OWN - 1)
            for k in early:
                second_order(k, TIMESTEP, True)
            emfs = fixed_corners(early)
            new_bx = {k: face_x(k, emfs[k], TIMESTEP) for k in early}

            def edge_tiles(k):
                density, mx, my, mz, bz = cells_of(k, TIMESTEP)
                return [density, mx, my, mz, new_bx[k], face_y(k, TIMESTEP), bz]

            send_edges(edge_tiles)
            for k in late:
                second_order(k, TIMESTEP, True)
            emfs.update({k: corner(k) for k in (*late, OWN - 1)})
        for k in kept:
            U[BX, k] = face_x(k, emfs[k], TIMESTEP)
        for k in ring:
            if k not in kept:
                EZ[k] = emfs[k]
        for k in kept:
            new_cells(k)

    rounds = STEPS // 2

    def two_steps(r, carry):
        slot = lax.rem(r, 2)

        for k in range(OWN - 1):
            initial_primitives(k)
        for k in range(1, OWN - 1):
            first_order(k, 0.5 * TIMESTEP)

        @pl.when(not_high)
        def _():
            down(slot).wait_recv()

        @pl.when(not_low)
        def _():
            up(slot).wait_recv()

        ghosts_of_neighbours(slot)
        ghosts_of_far_end(slot, 2 * r)
        advance(2 * r, False, MAIN, tuple(range(OWN - 1)), tuple(range(1, OWN - 1)))
        rows_ahead(slot, 2 * r)

        @pl.when(at_end)
        def _():
            advance(2 * r, False, AHEAD)

        ghosts_from_ahead(2 * r + 1)
        finish_sends(slot)

        def send_edges(edge_tiles):
            @pl.when(r < rounds - 1)
            def _():
                pack_edges(1 - slot, edge_tiles(0), edge_tiles(OWN - 1))
                fold_edge(1 - slot)
                start_far(1 - slot)
                start_rows(1 - slot)
                start_ahead(1 - slot)

        advance(2 * r + 1, True, MAIN, send_edges=send_edges)
        return carry

    lax.fori_loop(0, rounds, two_steps, 0)

    flat = U[:, 0:OWN].reshape(7 * OWN * 8, LANES)
    out = lax.dot_general(
        flat, permutation[0:256], (((1,), (1,)), ((), ())),
        precision=lax.Precision.HIGHEST, preferred_element_type=jnp.float32,
    ).reshape(7, 8 * OWN, 256)
    den_out[...] = out[D]
    mom_out[...] = out[MX : MZ + 1]
    mag_out[...] = out[BX : BZ + 1]


def store_kernel(den, mom, mag, den_out, mom_out, mag_out, sem):
    copies = [pltpu.make_async_copy(a, b, sem.at[i]) for i, (a, b) in enumerate(((den, den_out), (mom, mom_out), (mag, mag_out)))]
    for copy in copies:
        copy.start()
    for copy in copies:
        copy.wait()


def scratch(gyn):
    tile = (TILES, 8, LANES)
    f32 = jnp.float32
    vmem = lambda *shape: pltpu.VMEM(shape, f32)
    dma = pltpu.SemaphoreType.DMA
    return [
        vmem(7, *tile), vmem(7, *tile), vmem(2, *tile), vmem(6, *tile), vmem(6, *tile), vmem(5, *tile), vmem(5, *tile),
        vmem(*tile), vmem(*tile), vmem(*tile), vmem(*tile), vmem(*tile),
        *(vmem(2, GROUPS, 3, 3, 8, 128) for _ in range(4)), vmem(2, GROUPS, 2, 3, 8, 128),
        vmem(7, OWN, 8, 256), vmem(2, GROUPS, gyn, 2, 3, 8, 128), vmem(2, gyn, 2, 3, 8, 128),
        vmem(GROUPS, gyn, 2, 3, 8, 128), vmem(gyn, 2, 3, 8, 128), vmem(7, OWN, 8, 128), vmem(7, OWN, 8, 128),
        pltpu.SMEM((STEPS,), jnp.int32), pltpu.SMEM((STEPS,), f32), dma((5,)),
        dma((2,)), dma((2,)), dma((2,)), dma((2, 2)),
        dma((GROUPS, gyn)), dma((2, GROUPS, gyn)), dma((gyn,)), dma((2, gyn)),
    ]


def solution(mesh):
    gxn, gyn = mesh.shape["gx"], mesh.shape["gy"]

    def per_device(density, momentum, magnetic, shear_shift, shear_frac):
        state = pl.pallas_call(
            functools.partial(kernel, gxn, gyn),
            name="shearing_box",
            out_shape=tuple(jax.ShapeDtypeStruct(a.shape, jnp.float32) for a in (density, momentum, magnetic)),
            in_specs=[pl.BlockSpec(memory_space=pl.ANY)] * 5,
            out_specs=tuple(pl.BlockSpec(memory_space=pltpu.VMEM) for _ in range(3)),
            scratch_shapes=scratch(gyn),
            compiler_params=pltpu.CompilerParams(
                collective_id=0, has_side_effects=True, vmem_limit_bytes=48 * 1024 * 1024
            ),
        )(
            shear_shift,
            shear_frac,
            density.reshape(OWN, 8, 256),
            momentum.reshape(3, OWN, 8, 256),
            magnetic.reshape(3, OWN, 8, 256),
        )
        return pl.pallas_call(
            store_kernel,
            name="store",
            out_shape=tuple(jax.ShapeDtypeStruct(a.shape, jnp.float32) for a in (density, momentum, magnetic)),
            in_specs=[pl.BlockSpec(memory_space=pltpu.VMEM)] * 3,
            out_specs=tuple(pl.BlockSpec(memory_space=pl.ANY) for _ in range(3)),
            scratch_shapes=[pltpu.SemaphoreType.DMA((3,))],
            compiler_params=pltpu.CompilerParams(vmem_limit_bytes=48 * 1024 * 1024),
        )(*state)

    return jax.shard_map(
        per_device,
        mesh=mesh,
        in_specs=(P("gx", "gy"), P(None, "gx", "gy"), P(None, "gx", "gy"), P(), P()),
        out_specs=(P("gx", "gy"), P(None, "gx", "gy"), P(None, "gx", "gy")),
        check_vma=False,
    )
```

```python
import functools

import jax
import jax.numpy as jnp
from jax import lax
from jax.experimental import pallas as pl
from jax.experimental.pallas import tpu as pltpu
from jax.sharding import PartitionSpec as P

STEPS = 8
OMEGA = 0.5
QSHEAR = 1.5
TIMESTEP = 0.1
MESH = pl.DeviceIdType.MESH

D, MX, MY, MZ, BX, BY, BZ = range(7)
VX, VY, VZ, CY, CX, QBZ = 1, 2, 3, 4, 5, 6
OWN = 4
ABOVE, BELOW = OWN, OWN + 1
RING = OWN + 2
AHEAD = (RING, RING + 1)
MAIN = tuple(range(RING))
TILES = RING + 2
LANES = 384
GROUPS = 2


def roll(x, shift, axis):
    return pltpu.roll(x, shift % x.shape[axis], axis)


def row_iota(shape):
    return lax.broadcasted_iota(jnp.int32, shape, len(shape) - 2)


def lane_iota(shape):
    return lax.broadcasted_iota(jnp.int32, shape, len(shape) - 1)


def kernel(
    gxn, gyn, shift_in, frac_in, den, mom, mag, den_out, mom_out, mag_out,
    U, Q, M, QL, QR, FX, PART, FY4, SX4, EZ, NBX, NBY,
    pack, recv, fold, block, circ_far, circ_near, ring_far, ring_near, col_out, col_r, col_l, halo_columns,
    shift_ref, frac_ref, load_sem,
    col_send, col_recv, row_send, row_recv, far_send, far_recv, near_send, near_recv,
):
    gx = lax.axis_index("gx")
    gy = lax.axis_index("gy")
    at_low = gx == 0
    at_high = gx == gxn - 1
    at_end = jnp.logical_or(at_low, at_high)
    not_end = jnp.logical_not(at_end)
    not_low = gx > 0
    not_high = gx < gxn - 1
    below_gx = lax.max(gx - 1, 0)
    above_gx = lax.min(gx + 1, gxn - 1)
    other_end = gxn - 1 - gx
    east = lax.rem(gy + 1, gyn)
    west = lax.rem(gy + gyn - 1, gyn)
    far_order = sorted(range(gyn), key=lambda i: -min(i, gyn - i))

    rows8 = row_iota((8, LANES))
    first_row = rows8 == 0
    last_row = rows8 == 7
    near = lane_iota((8, 128)) < 64

    def previous(k):
        return sum(AHEAD) - k if k in AHEAD else (k + RING - 1) % RING

    def following(k):
        return sum(AHEAD) - k if k in AHEAD else (k + 1) % RING

    def row_before(before, here):
        return roll(jnp.where(last_row, before, here), 1, 0)

    def row_after(here, after):
        return roll(jnp.where(first_row, after, here), -1, 0)

    def lane_before(x):
        return jnp.concatenate([roll(x[:, 256:384], 1, 1), x[:, 0:128], x[:, 128:256]], axis=1)

    def lane_after(x):
        return jnp.concatenate([x[:, 128:256], x[:, 256:384], roll(x[:, 0:128], -1, 1)], axis=1)

    spots = lane_iota((8, LANES))
    columns = 3 * (spots & 127) + (spots >> 7)
    spot_of_row = lane_iota((LANES, LANES))
    permutation = jnp.where(row_iota((LANES, LANES)) == 3 * (spot_of_row & 127) + (spot_of_row >> 7), 1.0, 0.0)

    loads = [
        pltpu.make_async_copy(den, block.at[D], load_sem.at[0]),
        pltpu.make_async_copy(mom, block.at[MX : MZ + 1], load_sem.at[1]),
        pltpu.make_async_copy(mag, block.at[BX : BZ + 1], load_sem.at[2]),
        pltpu.make_async_copy(shift_in, shift_ref, load_sem.at[3]),
        pltpu.make_async_copy(frac_in, frac_ref, load_sem.at[4]),
    ]
    for load in loads:
        load.start()

    barrier = pltpu.get_barrier_semaphore()

    def greet(to_gx, to_gy):
        pl.semaphore_signal(barrier, inc=1, device_id=(to_gx, to_gy), device_id_type=MESH)

    @pl.when(at_end)
    def _():
        for i in far_order:
            greet(other_end, lax.rem(gy + i, gyn))
        for i in range(1, gyn):
            greet(gx, lax.rem(gy + i, gyn))

    @pl.when(jnp.logical_not(at_end))
    def _():
        greet(gx, east)
        greet(gx, west)

    @pl.when(not_low)
    def _():
        greet(below_gx, gy)

    @pl.when(not_high)
    def _():
        greet(above_gx, gy)

    for load in loads:
        load.wait()

    def packed(tiles, first):
        def at(field, row):
            return tiles[field] if row == first else roll(tiles[field], row - first, 0)

        return [
            jnp.where(rows8 < 3, at(0, 0), jnp.where(rows8 < 6, at(1, 3), at(6, 6))),
            jnp.where(rows8 < 3, at(2, 0), jnp.where(rows8 < 6, at(3, 3), at(6, 4))),
            jnp.where(rows8 < 3, at(4, 0), at(5, 3)),
        ]

    def turned_rows(x, amount):
        return pltpu.roll(x, amount & 7, 0)

    def unpacked(tiles, first):
        def move(x, row):
            return turned_rows(x, first + 8 - row)

        sixth = jnp.where(((rows8 + 8 - first) & 7) < 2, move(tiles[0], 6), move(tiles[1], 4))
        return (
            move(tiles[0], 0), move(tiles[0], 3), move(tiles[1], 0), move(tiles[1], 3),
            move(tiles[2], 0), move(tiles[2], 3), sixth,
        )

    def by_end(low, high):
        return jnp.where(at_low, low, high)

    def pack_edge(side, slot, tiles, outer, inner):
        for group, first in enumerate((outer, inner)):
            for part, tile in enumerate(packed(tiles, first)):
                for lane in range(3):
                    pack[side, slot, group, lane, part] = tile[:, 128 * lane : 128 * (lane + 1)]

    def load_pack(side, slot, group):
        return [jnp.concatenate([recv[side, slot, group, lane, part] for lane in range(3)], axis=1) for part in range(3)]

    def pack_edges(slot, low_tiles, high_tiles):
        pack_edge(0, slot, low_tiles, 0, 3)
        pack_edge(1, slot, high_tiles, 5, 2)

    def edges_of_block(slot):
        pack_edges(slot, [U[f, 0] for f in range(7)], [U[f, OWN - 1] for f in range(7)])

    lane = lane_iota((8, 128))

    end_side = by_end(0, 1)
    inner_side = 1 - end_side

    def fold_edge(slot):
        for group in range(GROUPS):
            for part in range(3):
                first, second, third = (pack[end_side, slot, group, j, part] for j in range(3))
                fold[slot, group, 0, part] = jnp.where(lane < 86, first, roll(third, 86, 1))
                fold[slot, group, 1, part] = jnp.where(lane < 85, second, roll(third, 43, 1))

    def to_far(slot, group, i):
        return pltpu.make_async_remote_copy(
            src_ref=fold.at[slot, group], dst_ref=circ_far.at[slot, group, gy],
            send_sem=far_send.at[group, i], recv_sem=far_recv.at[slot, group, gy],
            device_id=(other_end, lax.rem(gy + i, gyn)), device_id_type=MESH,
        )

    def from_far(slot, group, g):
        return pltpu.make_async_remote_copy(
            src_ref=fold.at[slot, group], dst_ref=circ_far.at[slot, group, g],
            send_sem=far_send.at[group, g], recv_sem=far_recv.at[slot, group, g],
            device_id=(other_end, g), device_id_type=MESH,
        )

    def to_near(slot, i):
        return pltpu.make_async_remote_copy(
            src_ref=fold.at[slot, 0], dst_ref=circ_near.at[slot, gy],
            send_sem=near_send.at[i], recv_sem=near_recv.at[slot, i],
            device_id=(gx, lax.rem(gy + i, gyn)), device_id_type=MESH,
        )

    def from_near(slot, i):
        sender = lax.rem(gy + gyn - i, gyn)
        return pltpu.make_async_remote_copy(
            src_ref=fold.at[slot, 0], dst_ref=circ_near.at[slot, sender],
            send_sem=near_send.at[i], recv_sem=near_recv.at[slot, i],
            device_id=(gx, sender), device_id_type=MESH,
        )

    def to_row(slot, side):
        to_gx = jnp.where(side == 0, below_gx, above_gx)
        return pltpu.make_async_remote_copy(
            src_ref=pack.at[side, slot], dst_ref=recv.at[side, slot],
            send_sem=row_send.at[side], recv_sem=row_recv.at[slot, side],
            device_id=(to_gx, gy), device_id_type=MESH,
        )

    def start_exchange(slot, rows, between=lambda: None):
        @pl.when(at_end)
        def _():
            fold_edge(slot)
            for i in far_order:
                to_far(slot, 0, i).start()
            if rows:
                to_row(slot, inner_side).start()
            between()
            for i in range(1, gyn):
                to_near(slot, i).start()
            for i in far_order:
                to_far(slot, 1, i).start()

        @pl.when(not_end)
        def _():
            if rows:
                to_row(slot, 0).start()
                to_row(slot, 1).start()
            between()

    def rows_arrived(slot):
        to_row(slot, jnp.where(at_high, 1, 0)).wait_recv()

        @pl.when(not_end)
        def _():
            to_row(slot, 1).wait_recv()

    def rows_sent(slot):
        to_row(slot, jnp.where(at_low, 1, 0)).wait_send()

        @pl.when(not_end)
        def _():
            to_row(slot, 1).wait_send()

    def far_sent(slot):
        for group in range(GROUPS):
            for g in range(gyn):
                to_far(slot, group, g).wait_send()
        for i in range(1, gyn):
            to_near(slot, i).wait_send()

    to_west = pltpu.make_async_remote_copy(
        src_ref=col_out.at[0], dst_ref=col_r, send_sem=col_send.at[0], recv_sem=col_recv.at[0],
        device_id=(gx, west), device_id_type=MESH,
    )
    to_east = pltpu.make_async_remote_copy(
        src_ref=col_out.at[1], dst_ref=col_l, send_sem=col_send.at[1], recv_sem=col_recv.at[1],
        device_id=(gx, east), device_id_type=MESH,
    )

    def interleaved(x, start, stop):
        flat = x.reshape(7 * OWN * 8, stop - start)
        out = jnp.dot(
            flat, permutation[start:stop], precision=lax.Precision.HIGHEST, preferred_element_type=jnp.float32
        )
        return out.reshape(7, OWN, 8, LANES)

    own_columns = interleaved(block[...], 0, 256)
    U[:, 0:OWN] = own_columns
    near = lane < 64
    for pair in range(4):
        one, two = 2 * pair, min(2 * pair + 1, 6)
        for k in range(OWN):
            col_out[0, pair, k] = jnp.where(near, block[one, k, :, 0:128], roll(block[two, k, :, 0:128], 64, 1))
            col_out[1, pair, k] = jnp.where(near, roll(block[one, k, :, 128:256], 64, 1), block[two, k, :, 128:256])
    edges_of_block(0)
    pl.semaphore_wait(barrier, jnp.where(at_end, 2 * gyn, 4))

    def start_columns():
        to_west.start()
        to_east.start()

    start_exchange(0, False, start_columns)
    to_west.wait()
    to_east.wait()

    for field in range(7):
        for k in range(OWN):
            right, left = col_r[field // 2, k], col_l[field // 2, k]
            if field % 2:
                halo_columns[field, k] = jnp.where(near, roll(right, 64, 1), left)
            else:
                halo_columns[field, k] = jnp.where(near, right, roll(left, 64, 1))
    halo = interleaved(halo_columns[...], 256, 384)
    U[:, 0:OWN] = U[:, 0:OWN] + halo
    for field in range(7):
        for k in (ABOVE, BELOW) + AHEAD:
            U[field, k] = U[field, 0]
    edges_of_block(0)
    to_row(0, jnp.where(at_low, 1, 0)).start()

    @pl.when(not_end)
    def _():
        to_row(0, 1).start()


    def ghosts_of_neighbours(slot):
        for side, k, outer_first, inner_first, mask in ((0, ABOVE, 0, 3, rows8 < 3), (1, BELOW, 5, 2, rows8 >= 5)):
            outer = unpacked(load_pack(side, slot, 0), outer_first)
            inner = unpacked(load_pack(side, slot, 1), inner_first)
            for f in range(7):
                U[f, k] = jnp.where(mask, outer[f], inner[f])

    wrapped = jnp.where(columns < 320, columns, columns - LANES)

    def window(ring, moved):
        origin = lax.rem(gy * 256 + moved + 512 * gyn, 256 * gyn)
        first_block = lax.div(origin, 256)
        offset = lax.rem(origin, 256)
        sources = []
        for i in (0, 1, jnp.where(offset < 128, -1, 2)):
            ahead = offset - 256 * i
            whole = lax.div(ahead + 2 * LANES, 3)
            phase = lax.rem(ahead + 2 * LANES, 3)
            place = lax.rem(first_block + i + gyn, gyn)
            turns = []
            for j in range(3):
                turns.append(lax.rem(4 * 128 - whole - lax.div(phase + j, 3), 128))
            at = wrapped + ahead
            sources.append((place, phase, turns, jnp.logical_and(at >= 0, at < 256)))
        out = []
        for part in range(3):
            spans = []
            for place, phase, turns, _ in sources:
                one, two = ring[place, 0, part], ring[place, 1, part]
                three = jnp.where(lane < 42, roll(one, -86, 1), roll(two, -43, 1))
                vectors = (one, two, three)
                picked = [
                    jnp.where(phase == 0, vectors[j], jnp.where(phase == 1, vectors[(j + 1) % 3], vectors[(j + 2) % 3]))
                    for j in range(3)
                ]
                spans.append(jnp.concatenate([pltpu.roll(x, turn, 1) for x, turn in zip(picked, turns)], axis=1))
            out.append(jnp.where(sources[0][3], spans[0], jnp.where(sources[1][3], spans[1], spans[2])))
        return out

    def blended(x, fraction, towards):
        return (1.0 - fraction) * x + fraction * (lane_after(x) if towards == 1 else lane_before(x))

    def blended_out(x, fraction):
        return (1.0 - fraction) * x + fraction * by_end(lane_before(x), lane_after(x))

    def blended_back(x, fraction):
        return (1.0 - fraction) * x + fraction * by_end(lane_after(x), lane_before(x))

    ghost_first = by_end(5, 0)
    ghost_above = jnp.logical_and(at_high, rows8 < 3)
    own_above = jnp.logical_and(at_high, jnp.logical_and(rows8 >= 3, rows8 < 6))
    ghost_below = jnp.logical_and(at_low, rows8 >= 5)
    own_below = jnp.logical_and(at_low, jnp.logical_and(rows8 >= 1, rows8 < 5))
    far_below = rows8 < by_end(1, 2)

    def end_ghosts(f, raw, fraction):
        ghost = blended_out(raw, fraction)
        far_rows = turned_rows(raw, by_end(1, 6))
        own = turned_rows(blended_back(by_end(U[f, 0], U[f, OWN - 1]), fraction), by_end(1, 6))
        U[f, ABOVE] = jnp.where(
            ghost_above, ghost, jnp.where(own_above, own, jnp.where(rows8 >= 6, far_rows, U[f, ABOVE]))
        )
        U[f, BELOW] = jnp.where(
            ghost_below, ghost, jnp.where(own_below, own, jnp.where(far_below, far_rows, U[f, BELOW]))
        )

    def ghosts_of_far_end(slot, n):
        for g in range(gyn):
            from_far(slot, 0, g).wait_recv()
        ring_far[0] = circ_far[slot, 0]
        shift = shift_ref[n]
        for f, raw in enumerate(unpacked(window(ring_far.at[0], by_end(-shift, shift)), ghost_first)):
            end_ghosts(f, raw, frac_ref[n])

    def rows_ahead(slot, n):
        for i in range(1, gyn):
            from_near(slot, i).wait_recv()
        for g in range(gyn):
            from_far(slot, 1, g).wait_recv()
        ring_far[1] = circ_far[slot, 1]
        ring_near[...] = circ_near[slot]
        ring_near[gy] = fold[slot, 0]
        shift, shift_next = shift_ref[n], shift_ref[n + 1]
        fraction = frac_ref[n]
        left, right = AHEAD
        ahead = by_end(-shift_next, shift_next)
        outer = window(ring_far.at[0], ahead)
        beyond = window(ring_near, ahead + by_end(shift, -shift))
        inner = unpacked(window(ring_far.at[1], ahead), by_end(2, 3))
        rows_a = unpacked(outer, ghost_first)
        ghost = unpacked([blended_back(x, fraction) for x in beyond], by_end(0, 5))
        mirror = unpacked([blended_out(x, fraction) for x in outer], by_end(3, 2))
        raw = unpacked(beyond, by_end(6, 7))
        raw_left, raw_right = rows8 < by_end(1, 2), rows8 >= by_end(6, 7)
        for f in range(7):
            middle = jnp.where(rows8 < 5, by_end(inner[f], mirror[f]), by_end(rows_a[f], ghost[f]))
            U[f, left] = jnp.where(raw_left, raw[f], middle)
            middle = jnp.where(rows8 < 3, by_end(ghost[f], rows_a[f]), by_end(mirror[f], inner[f]))
            U[f, right] = jnp.where(raw_right, raw[f], middle)

    def ghosts_from_ahead(n):
        for f in range(7):
            end_ghosts(f, by_end(U[f, AHEAD[0]], U[f, AHEAD[1]]), frac_ref[n])

    def minmod(a, b):
        return jnp.maximum(jnp.minimum(a, b), 0.0) + jnp.minimum(jnp.maximum(a, b), 0.0)

    def signal(density, speed, squared):
        total = density + squared
        return jnp.abs(speed) + jnp.abs(total) * lax.rsqrt(total * density)

    def riemann(left, right, normal, wanted):
        dl, vnl, vtl, vsl, btl, bsl = left
        dr, vnr, vtr, vsr, btr, bsr = right
        n2 = normal * normal
        tl = btl * btl + bsl * bsl
        tr = btr * btr + bsr * bsr
        fastest = jnp.maximum(signal(dl, vnl, n2 + tl), signal(dr, vnr, n2 + tr))
        ul = vnl + fastest
        ur = vnr - fastest
        out = {}
        if wanted != (4,):
            al = dl * ul
            ar = dr * ur
        if 0 in wanted:
            out[0] = al + ar
        if 1 in wanted:
            out[1] = (al * vnl + ar * vnr) + ((dl + dr) + (0.5 * (tl + tr) - n2))
        if 2 in wanted:
            out[2] = (al * vtl + ar * vtr) - normal * (btl + btr)
        if 3 in wanted:
            out[3] = (al * vsl + ar * vsr) - normal * (bsl + bsr)
        if 4 in wanted:
            out[4] = (btl * ul + btr * ur) - normal * (vtl + vtr)
        if 5 in wanted:
            out[5] = (bsl * ul + bsr * ur) - normal * (vsl + vsr)
        return out

    def primitives(k, density, mx, my, mz, bz, bx, bx_after, by):
        inverse = 1.0 / density
        Q[0, k] = density
        Q[VX, k] = mx * inverse
        Q[VY, k] = my * inverse
        Q[VZ, k] = mz * inverse
        Q[CX, k] = 0.5 * (bx + row_after(bx, bx_after))
        Q[CY, k] = 0.5 * (by + lane_after(by))
        Q[QBZ, k] = bz

    def initial_primitives(k):
        primitives(k, *(U[f, k] for f in (D, MX, MY, MZ, BZ, BX)), U[BX, following(k)], U[BY, k])

    X_STATE = (0, VX, VY, VZ, CY, QBZ)
    Y_STATE = (0, VY, VX, VZ, CX, QBZ)

    def finish_fluxes(k, fx, fy, stride, mx, my, cells):
        half = 0.5 * stride
        if 0 in fx:
            for spot, part in enumerate((0, 1, 2, 3, 5)):
                FX[spot, k] = fx[part]
        FY4[k] = fy[4]
        SX4[k] = fx[4] + lane_before(fx[4])
        if cells:
            for spot, (field, px, py) in enumerate(((D, 0, 0), (MX, 1, 2), (MY, 2, 1), (MZ, 3, 3), (BZ, 5, 5))):
                value = U[field, k] - half * ((lane_after(fy[py]) - fy[py]) - fx[px])
                if field == MX:
                    value += (stride * 2.0 * OMEGA) * my
                if field == MY:
                    value -= (stride * (2.0 - QSHEAR) * OMEGA) * mx
                PART[spot, k] = value

    ALL = (0, 1, 2, 3, 4, 5)

    def first_order(k, stride):
        left = [row_before(Q[i, previous(k)], Q[i, k]) for i in X_STATE]
        fx = riemann(left, [Q[i, k] for i in X_STATE], U[BX, k], ALL)
        right = [Q[i, k] for i in Y_STATE]
        fy = riemann([lane_before(q) for q in right], right, U[BY, k], ALL)
        finish_fluxes(k, fx, fy, stride, U[MX, k], U[MY, k], True)

    def slopes(k):
        for spot, i in enumerate(X_STATE):
            here = Q[i, k]
            gradient = 0.5 * minmod(here - row_before(Q[i, previous(k)], here), row_after(here, Q[i, following(k)]) - here)
            QL[spot, k] = here + gradient
            QR[spot, k] = here - gradient

    def second_order(k, stride, last):
        cells = k < OWN or not last
        x_wanted = ALL if cells or k == ABOVE else (4,)
        y_wanted = ALL if cells else (4,)
        left = [row_before(QL[i, previous(k)], QL[i, k]) for i in range(6)]
        fx = riemann(left, [QR[i, k] for i in range(6)], NBX[k], x_wanted)
        left, right = [], []
        for i in Y_STATE:
            here = Q[i, k]
            behind = here - lane_before(here)
            gradient = 0.5 * minmod(behind, lane_after(behind))
            left.append(lane_before(here + gradient))
            right.append(here - gradient)
        fy = riemann(left, right, NBY[k], y_wanted)
        finish_fluxes(k, fx, fy, stride, M[0, k], M[1, k], cells)

    def corner(k):
        return 0.125 * (FY4[k] + row_before(FY4[previous(k)], FY4[k]) - SX4[k])

    def face_x(k, emf, stride):
        EZ[k] = emf
        return U[BX, k] - stride * (lane_after(emf) - emf)

    def face_y(k, stride):
        emf = EZ[k]
        return U[BY, k] + stride * (row_after(emf, EZ[following(k)]) - emf)

    def cells_of(k, stride):
        return [PART[i, k] - (0.5 * stride) * row_after(FX[i, k], FX[i, following(k)]) for i in range(5)]

    def advance(n, last, ring, ready_primitives=(), ready_fluxes=(), send_edges=None):
        fraction = frac_ref[n]

        def tiles(run):
            for k in ring:
                run(k)

        stride = 0.5 * TIMESTEP
        for k in ring:
            if k not in ready_primitives:
                initial_primitives(k)
        for k in ring:
            if k not in ready_fluxes:
                first_order(k, stride)

        def predicted_x(k):
            NBX[k] = face_x(k, corner(k), stride)

        tiles(predicted_x)

        def predicted_cells(k):
            density, mx, my, mz, bz = cells_of(k, stride)
            by = face_y(k, stride)
            NBY[k] = by
            M[0, k] = mx
            M[1, k] = my
            primitives(k, density, mx, my, mz, bz, NBX[k], NBX[following(k)], by)

        tiles(predicted_cells)

        tiles(slopes)
        if not last:
            tiles(lambda k: second_order(k, TIMESTEP, False))
        def new_cells(k):
            for field, value in zip((D, MX, MY, MZ, BZ), cells_of(k, TIMESTEP)):
                U[field, k] = value
            U[BY, k] = face_y(k, TIMESTEP)

        if ring == AHEAD:
            left, right = AHEAD
            emf_l, emf_r = corner(left), corner(right)
            from_low = blended(roll(emf_r, -6, 0), fraction, 1)
            from_high = blended(roll(emf_l, -2, 0), fraction, -1)
            remote = jnp.where(at_low, from_low, from_high)
            emf_r = jnp.where(first_row, 0.5 * (emf_r + remote), emf_r)
            U[BX, left] = face_x(left, emf_l, TIMESTEP)
            U[BX, right] = face_x(right, emf_r, TIMESTEP)
            tiles(new_cells)
            return
        kept = range(OWN) if last else ring

        def mended(emf, remote_row, towards, ours):
            remote = blended(remote_row, fraction, towards)
            return jnp.where(jnp.logical_and(first_row, ours), 0.5 * (emf + remote), emf)

        def fixed_corners(ks):
            emfs = {k: corner(k) for k in ks}
            if 0 in ks:
                emfs[0] = mended(emfs[0], roll(emfs[BELOW], -1, 0), -1, at_low)
                emfs[ABOVE] = mended(emfs[ABOVE], roll(emfs[ABOVE], -6, 0), 1, at_high)
            return emfs

        if not last:
            emfs = fixed_corners(ring)
        else:
            early, late = (0, OWN - 1, ABOVE, BELOW), range(1, OWN - 1)
            for k in early:
                second_order(k, TIMESTEP, True)
            emfs = fixed_corners(early)
            new_bx = {k: face_x(k, emfs[k], TIMESTEP) for k in early}

            def edge_tiles(k):
                density, mx, my, mz, bz = cells_of(k, TIMESTEP)
                return [density, mx, my, mz, new_bx[k], face_y(k, TIMESTEP), bz]

            send_edges(edge_tiles)
            for k in late:
                second_order(k, TIMESTEP, True)
            emfs.update({k: corner(k) for k in (*late, OWN - 1)})
        for k in kept:
            U[BX, k] = face_x(k, emfs[k], TIMESTEP)
        for k in ring:
            if k not in kept:
                EZ[k] = emfs[k]
        for k in kept:
            new_cells(k)

    rounds = STEPS // 2

    def two_steps(r, carry):
        slot = lax.rem(r, 2)

        for k in range(OWN - 1):
            initial_primitives(k)
        for k in range(1, OWN - 1):
            first_order(k, 0.5 * TIMESTEP)

        rows_arrived(slot)
        ghosts_of_neighbours(slot)

        @pl.when(at_end)
        def _():
            ghosts_of_far_end(slot, 2 * r)

        advance(2 * r, False, MAIN, tuple(range(OWN - 1)), tuple(range(1, OWN - 1)))

        @pl.when(at_end)
        def _():
            rows_ahead(slot, 2 * r)
            advance(2 * r, False, AHEAD)
            ghosts_from_ahead(2 * r + 1)
            far_sent(slot)

        rows_sent(slot)

        def send_edges(edge_tiles):
            @pl.when(r < rounds - 1)
            def _():
                pack_edges(1 - slot, edge_tiles(0), edge_tiles(OWN - 1))
                start_exchange(1 - slot, True)

        advance(2 * r + 1, True, MAIN, send_edges=send_edges)
        return carry

    lax.fori_loop(0, rounds, two_steps, 0)

    flat = U[:, 0:OWN].reshape(7 * OWN * 8, LANES)
    out = lax.dot_general(
        flat, permutation[0:256], (((1,), (1,)), ((), ())),
        precision=lax.Precision.HIGHEST, preferred_element_type=jnp.float32,
    ).reshape(7, 8 * OWN, 256)
    den_out[...] = out[D]
    mom_out[...] = out[MX : MZ + 1]
    mag_out[...] = out[BX : BZ + 1]


def store_kernel(den, mom, mag, den_out, mom_out, mag_out, sem):
    copies = [pltpu.make_async_copy(a, b, sem.at[i]) for i, (a, b) in enumerate(((den, den_out), (mom, mom_out), (mag, mag_out)))]
    for copy in copies:
        copy.start()
    for copy in copies:
        copy.wait()


def scratch(gyn):
    tile = (TILES, 8, LANES)
    f32 = jnp.float32
    vmem = lambda *shape: pltpu.VMEM(shape, f32)
    dma = pltpu.SemaphoreType.DMA
    return [
        vmem(7, *tile), vmem(7, *tile), vmem(2, *tile), vmem(6, *tile), vmem(6, *tile), vmem(5, *tile), vmem(5, *tile),
        vmem(*tile), vmem(*tile), vmem(*tile), vmem(*tile), vmem(*tile),
        vmem(2, 2, GROUPS, 3, 3, 8, 128), vmem(2, 2, GROUPS, 3, 3, 8, 128), vmem(2, GROUPS, 2, 3, 8, 128),
        vmem(7, OWN, 8, 256), vmem(2, GROUPS, gyn, 2, 3, 8, 128), vmem(2, gyn, 2, 3, 8, 128),
        vmem(GROUPS, gyn, 2, 3, 8, 128), vmem(gyn, 2, 3, 8, 128), vmem(2, 4, OWN, 8, 128), vmem(4, OWN, 8, 128), vmem(4, OWN, 8, 128), vmem(7, OWN, 8, 128),
        pltpu.SMEM((STEPS,), jnp.int32), pltpu.SMEM((STEPS,), f32), dma((5,)),
        dma((2,)), dma((2,)), dma((2,)), dma((2, 2)),
        dma((GROUPS, gyn)), dma((2, GROUPS, gyn)), dma((gyn,)), dma((2, gyn)),
    ]


def solution(mesh):
    gxn, gyn = mesh.shape["gx"], mesh.shape["gy"]

    def per_device(density, momentum, magnetic, shear_shift, shear_frac):
        state = pl.pallas_call(
            functools.partial(kernel, gxn, gyn),
            name="shearing_box",
            out_shape=tuple(jax.ShapeDtypeStruct(a.shape, jnp.float32) for a in (density, momentum, magnetic)),
            in_specs=[pl.BlockSpec(memory_space=pl.ANY)] * 5,
            out_specs=tuple(pl.BlockSpec(memory_space=pltpu.VMEM) for _ in range(3)),
            scratch_shapes=scratch(gyn),
            compiler_params=pltpu.CompilerParams(
                collective_id=0, has_side_effects=True, vmem_limit_bytes=48 * 1024 * 1024
            ),
        )(
            shear_shift,
            shear_frac,
            density.reshape(OWN, 8, 256),
            momentum.reshape(3, OWN, 8, 256),
            magnetic.reshape(3, OWN, 8, 256),
        )
        return pl.pallas_call(
            store_kernel,
            name="store",
            out_shape=tuple(jax.ShapeDtypeStruct(a.shape, jnp.float32) for a in (density, momentum, magnetic)),
            in_specs=[pl.BlockSpec(memory_space=pltpu.VMEM)] * 3,
            out_specs=tuple(pl.BlockSpec(memory_space=pl.ANY) for _ in range(3)),
            scratch_shapes=[pltpu.SemaphoreType.DMA((3,))],
            compiler_params=pltpu.CompilerParams(vmem_limit_bytes=48 * 1024 * 1024),
        )(*state)

    return jax.shard_map(
        per_device,
        mesh=mesh,
        in_specs=(P("gx", "gy"), P(None, "gx", "gy"), P(None, "gx", "gy"), P(), P()),
        out_specs=(P("gx", "gy"), P(None, "gx", "gy"), P(None, "gx", "gy")),
        check_vma=False,
    )
```

```python
import functools

import jax
import jax.numpy as jnp
from jax import lax
from jax.experimental import pallas as pl
from jax.experimental.pallas import tpu as pltpu
from jax.sharding import PartitionSpec as P

STEPS = 8
OMEGA = 0.5
QSHEAR = 1.5
TIMESTEP = 0.1
MESH = pl.DeviceIdType.MESH

D, MX, MY, MZ, BX, BY, BZ = range(7)
VX, VY, VZ, CY, CX, QBZ = 1, 2, 3, 4, 5, 6
OWN = 4
ABOVE, BELOW = OWN, OWN + 1
RING = OWN + 2
AHEAD = (RING, RING + 1)
MAIN = tuple(range(RING))
TILES = RING + 2
LANES = 384
GROUPS = 2


def roll(x, shift, axis):
    return pltpu.roll(x, shift % x.shape[axis], axis)


def row_iota(shape):
    return lax.broadcasted_iota(jnp.int32, shape, len(shape) - 2)


def lane_iota(shape):
    return lax.broadcasted_iota(jnp.int32, shape, len(shape) - 1)


def kernel(
    gxn, gyn, shift_in, frac_in, den, mom, mag, den_out, mom_out, mag_out,
    U, Q, M, QL, QR, FX, PART, FY4, SX4, EZ, NBX, NBY,
    pack, recv, fold, block, circ_far, circ_near, ring_far, ring_near, col_out, col_r, col_l, halo_columns,
    shift_ref, frac_ref, load_sem,
    col_send, col_recv, row_send, row_recv, far_send, far_recv, near_send, near_recv,
):
    gx = lax.axis_index("gx")
    gy = lax.axis_index("gy")
    at_low = gx == 0
    at_high = gx == gxn - 1
    at_end = jnp.logical_or(at_low, at_high)
    not_end = jnp.logical_not(at_end)
    not_low = gx > 0
    not_high = gx < gxn - 1
    below_gx = lax.max(gx - 1, 0)
    above_gx = lax.min(gx + 1, gxn - 1)
    other_end = gxn - 1 - gx
    east = lax.rem(gy + 1, gyn)
    west = lax.rem(gy + gyn - 1, gyn)
    far_order = sorted(range(gyn), key=lambda i: -min(i, gyn - i))

    rows8 = row_iota((8, LANES))
    first_row = rows8 == 0
    last_row = rows8 == 7
    near = lane_iota((8, 128)) < 64

    def previous(k):
        return sum(AHEAD) - k if k in AHEAD else (k + RING - 1) % RING

    def following(k):
        return sum(AHEAD) - k if k in AHEAD else (k + 1) % RING

    def row_before(before, here):
        return roll(jnp.where(last_row, before, here), 1, 0)

    def row_after(here, after):
        return roll(jnp.where(first_row, after, here), -1, 0)

    def lane_before(x):
        return jnp.concatenate([roll(x[:, 256:384], 1, 1), x[:, 0:128], x[:, 128:256]], axis=1)

    def lane_after(x):
        return jnp.concatenate([x[:, 128:256], x[:, 256:384], roll(x[:, 0:128], -1, 1)], axis=1)

    spots = lane_iota((8, LANES))
    columns = 3 * (spots & 127) + (spots >> 7)
    spot_of_row = lane_iota((LANES, LANES))
    permutation = jnp.where(row_iota((LANES, LANES)) == 3 * (spot_of_row & 127) + (spot_of_row >> 7), 1.0, 0.0)

    loads = [
        pltpu.make_async_copy(den, block.at[D], load_sem.at[0]),
        pltpu.make_async_copy(mom, block.at[MX : MZ + 1], load_sem.at[1]),
        pltpu.make_async_copy(mag, block.at[BX : BZ + 1], load_sem.at[2]),
        pltpu.make_async_copy(shift_in, shift_ref, load_sem.at[3]),
        pltpu.make_async_copy(frac_in, frac_ref, load_sem.at[4]),
    ]
    for load in loads:
        load.start()

    barrier = pltpu.get_barrier_semaphore()

    def greet(to_gx, to_gy):
        pl.semaphore_signal(barrier, inc=1, device_id=(to_gx, to_gy), device_id_type=MESH)

    @pl.when(at_end)
    def _():
        for i in far_order:
            greet(other_end, lax.rem(gy + i, gyn))
        for i in range(1, gyn):
            greet(gx, lax.rem(gy + i, gyn))

    @pl.when(jnp.logical_not(at_end))
    def _():
        greet(gx, east)
        greet(gx, west)

    @pl.when(not_low)
    def _():
        greet(below_gx, gy)

    @pl.when(not_high)
    def _():
        greet(above_gx, gy)

    for load in loads:
        load.wait()

    def packed(tiles, first):
        def at(field, row):
            return tiles[field] if row == first else roll(tiles[field], row - first, 0)

        return [
            jnp.where(rows8 < 3, at(0, 0), jnp.where(rows8 < 6, at(1, 3), at(6, 6))),
            jnp.where(rows8 < 3, at(2, 0), jnp.where(rows8 < 6, at(3, 3), at(6, 4))),
            jnp.where(rows8 < 3, at(4, 0), at(5, 3)),
        ]

    def turned_rows(x, amount):
        return pltpu.roll(x, amount & 7, 0)

    def unpacked(tiles, first):
        def move(x, row):
            return turned_rows(x, first + 8 - row)

        sixth = jnp.where(((rows8 + 8 - first) & 7) < 2, move(tiles[0], 6), move(tiles[1], 4))
        return (
            move(tiles[0], 0), move(tiles[0], 3), move(tiles[1], 0), move(tiles[1], 3),
            move(tiles[2], 0), move(tiles[2], 3), sixth,
        )

    def by_end(low, high):
        return jnp.where(at_low, low, high)

    def pack_edge(side, slot, tiles, outer, inner):
        for group, first in enumerate((outer, inner)):
            for part, tile in enumerate(packed(tiles, first)):
                for lane in range(3):
                    pack[side, slot, group, lane, part] = tile[:, 128 * lane : 128 * (lane + 1)]

    def load_pack(side, slot, group):
        return [jnp.concatenate([recv[side, slot, group, lane, part] for lane in range(3)], axis=1) for part in range(3)]

    def pack_edges(slot, low_tiles, high_tiles):
        pack_edge(0, slot, low_tiles, 0, 3)
        pack_edge(1, slot, high_tiles, 5, 2)

    def edges_of_block(slot):
        pack_edges(slot, [U[f, 0] for f in range(7)], [U[f, OWN - 1] for f in range(7)])

    lane = lane_iota((8, 128))

    end_side = by_end(0, 1)
    inner_side = 1 - end_side

    def fold_edge(slot):
        for group in range(GROUPS):
            for part in range(3):
                first, second, third = (pack[end_side, slot, group, j, part] for j in range(3))
                fold[slot, group, 0, part] = jnp.where(lane < 86, first, roll(third, 86, 1))
                fold[slot, group, 1, part] = jnp.where(lane < 85, second, roll(third, 43, 1))

    def to_far(slot, group, i):
        return pltpu.make_async_remote_copy(
            src_ref=fold.at[slot, group], dst_ref=circ_far.at[slot, group, gy],
            send_sem=far_send.at[group, i], recv_sem=far_recv.at[slot, group, gy],
            device_id=(other_end, lax.rem(gy + i, gyn)), device_id_type=MESH,
        )

    def from_far(slot, group, g):
        return pltpu.make_async_remote_copy(
            src_ref=fold.at[slot, group], dst_ref=circ_far.at[slot, group, g],
            send_sem=far_send.at[group, g], recv_sem=far_recv.at[slot, group, g],
            device_id=(other_end, g), device_id_type=MESH,
        )

    def to_near(slot, i):
        return pltpu.make_async_remote_copy(
            src_ref=fold.at[slot, 0], dst_ref=circ_near.at[slot, gy],
            send_sem=near_send.at[i], recv_sem=near_recv.at[slot, i],
            device_id=(gx, lax.rem(gy + i, gyn)), device_id_type=MESH,
        )

    def from_near(slot, i):
        sender = lax.rem(gy + gyn - i, gyn)
        return pltpu.make_async_remote_copy(
            src_ref=fold.at[slot, 0], dst_ref=circ_near.at[slot, sender],
            send_sem=near_send.at[i], recv_sem=near_recv.at[slot, i],
            device_id=(gx, sender), device_id_type=MESH,
        )

    def to_row(slot, side):
        to_gx = jnp.where(side == 0, below_gx, above_gx)
        return pltpu.make_async_remote_copy(
            src_ref=pack.at[side, slot], dst_ref=recv.at[side, slot],
            send_sem=row_send.at[side], recv_sem=row_recv.at[slot, side],
            device_id=(to_gx, gy), device_id_type=MESH,
        )

    def start_exchange(slot, rows, between=lambda: None):
        @pl.when(at_end)
        def _():
            fold_edge(slot)
            for i in far_order:
                to_far(slot, 0, i).start()
            if rows:
                to_row(slot, inner_side).start()
            between()
            for i in range(1, gyn):
                to_near(slot, i).start()
            for i in far_order:
                to_far(slot, 1, i).start()

        @pl.when(not_end)
        def _():
            if rows:
                to_row(slot, 0).start()
                to_row(slot, 1).start()
            between()

    def rows_arrived(slot):
        to_row(slot, jnp.where(at_high, 1, 0)).wait_recv()

        @pl.when(not_end)
        def _():
            to_row(slot, 1).wait_recv()

    def rows_sent(slot):
        to_row(slot, jnp.where(at_low, 1, 0)).wait_send()

        @pl.when(not_end)
        def _():
            to_row(slot, 1).wait_send()

    def far_sent(slot):
        for group in range(GROUPS):
            for g in range(gyn):
                to_far(slot, group, g).wait_send()
        for i in range(1, gyn):
            to_near(slot, i).wait_send()

    to_west = pltpu.make_async_remote_copy(
        src_ref=col_out.at[0], dst_ref=col_r, send_sem=col_send.at[0], recv_sem=col_recv.at[0],
        device_id=(gx, west), device_id_type=MESH,
    )
    to_east = pltpu.make_async_remote_copy(
        src_ref=col_out.at[1], dst_ref=col_l, send_sem=col_send.at[1], recv_sem=col_recv.at[1],
        device_id=(gx, east), device_id_type=MESH,
    )

    def permuted(x, one_hot, dim):
        picks = one_hot.astype(jnp.bfloat16)
        total = None
        for _ in range(3):
            term = x.astype(jnp.bfloat16)
            x = x - term.astype(jnp.float32)
            moved = lax.dot_general(term, picks, (((1,), (dim,)), ((), ())), preferred_element_type=jnp.float32)
            total = moved if total is None else total + moved
        return total

    def interleaved(x, start, stop):
        flat = x.reshape(7 * OWN * 8, stop - start)
        out = permuted(flat, permutation[start:stop], 0)
        return out.reshape(7, OWN, 8, LANES)

    own_columns = interleaved(block[...], 0, 256)
    U[:, 0:OWN] = own_columns
    near = lane < 64
    for pair in range(4):
        one, two = 2 * pair, min(2 * pair + 1, 6)
        for k in range(OWN):
            col_out[0, pair, k] = jnp.where(near, block[one, k, :, 0:128], roll(block[two, k, :, 0:128], 64, 1))
            col_out[1, pair, k] = jnp.where(near, roll(block[one, k, :, 128:256], 64, 1), block[two, k, :, 128:256])
    edges_of_block(0)
    pl.semaphore_wait(barrier, jnp.where(at_end, 2 * gyn, 4))

    def start_columns():
        to_west.start()
        to_east.start()

    start_exchange(0, False, start_columns)
    to_west.wait()
    to_east.wait()

    for field in range(7):
        for k in range(OWN):
            right, left = col_r[field // 2, k], col_l[field // 2, k]
            if field % 2:
                halo_columns[field, k] = jnp.where(near, roll(right, 64, 1), left)
            else:
                halo_columns[field, k] = jnp.where(near, right, roll(left, 64, 1))
    halo = interleaved(halo_columns[...], 256, 384)
    U[:, 0:OWN] = U[:, 0:OWN] + halo
    for field in range(7):
        for k in (ABOVE, BELOW) + AHEAD:
            U[field, k] = U[field, 0]
    edges_of_block(0)
    to_row(0, jnp.where(at_low, 1, 0)).start()

    @pl.when(not_end)
    def _():
        to_row(0, 1).start()


    def ghosts_of_neighbours(slot):
        for side, k, outer_first, inner_first, mask in ((0, ABOVE, 0, 3, rows8 < 3), (1, BELOW, 5, 2, rows8 >= 5)):
            outer = unpacked(load_pack(side, slot, 0), outer_first)
            inner = unpacked(load_pack(side, slot, 1), inner_first)
            for f in range(7):
                U[f, k] = jnp.where(mask, outer[f], inner[f])

    wrapped = jnp.where(columns < 320, columns, columns - LANES)

    def window(ring, moved):
        origin = lax.rem(gy * 256 + moved + 512 * gyn, 256 * gyn)
        first_block = lax.div(origin, 256)
        offset = lax.rem(origin, 256)
        sources = []
        for i in (0, 1, jnp.where(offset < 128, -1, 2)):
            ahead = offset - 256 * i
            whole = lax.div(ahead + 2 * LANES, 3)
            phase = lax.rem(ahead + 2 * LANES, 3)
            place = lax.rem(first_block + i + gyn, gyn)
            turns = []
            for j in range(3):
                turns.append(lax.rem(4 * 128 - whole - lax.div(phase + j, 3), 128))
            at = wrapped + ahead
            sources.append((place, phase, turns, jnp.logical_and(at >= 0, at < 256)))
        out = []
        for part in range(3):
            spans = []
            for place, phase, turns, _ in sources:
                one, two = ring[place, 0, part], ring[place, 1, part]
                three = jnp.where(lane < 42, roll(one, -86, 1), roll(two, -43, 1))
                vectors = (one, two, three)
                picked = [
                    jnp.where(phase == 0, vectors[j], jnp.where(phase == 1, vectors[(j + 1) % 3], vectors[(j + 2) % 3]))
                    for j in range(3)
                ]
                spans.append(jnp.concatenate([pltpu.roll(x, turn, 1) for x, turn in zip(picked, turns)], axis=1))
            out.append(jnp.where(sources[0][3], spans[0], jnp.where(sources[1][3], spans[1], spans[2])))
        return out

    def blended(x, fraction, towards):
        return (1.0 - fraction) * x + fraction * (lane_after(x) if towards == 1 else lane_before(x))

    def blended_out(x, fraction):
        return (1.0 - fraction) * x + fraction * by_end(lane_before(x), lane_after(x))

    def blended_back(x, fraction):
        return (1.0 - fraction) * x + fraction * by_end(lane_after(x), lane_before(x))

    ghost_first = by_end(5, 0)
    ghost_above = jnp.logical_and(at_high, rows8 < 3)
    own_above = jnp.logical_and(at_high, jnp.logical_and(rows8 >= 3, rows8 < 6))
    ghost_below = jnp.logical_and(at_low, rows8 >= 5)
    own_below = jnp.logical_and(at_low, jnp.logical_and(rows8 >= 1, rows8 < 5))
    far_below = rows8 < by_end(1, 2)

    def end_ghosts(f, raw, fraction):
        ghost = blended_out(raw, fraction)
        far_rows = turned_rows(raw, by_end(1, 6))
        own = turned_rows(blended_back(by_end(U[f, 0], U[f, OWN - 1]), fraction), by_end(1, 6))
        U[f, ABOVE] = jnp.where(
            ghost_above, ghost, jnp.where(own_above, own, jnp.where(rows8 >= 6, far_rows, U[f, ABOVE]))
        )
        U[f, BELOW] = jnp.where(
            ghost_below, ghost, jnp.where(own_below, own, jnp.where(far_below, far_rows, U[f, BELOW]))
        )

    def ghosts_of_far_end(slot, n):
        for g in range(gyn):
            from_far(slot, 0, g).wait_recv()
        ring_far[0] = circ_far[slot, 0]
        shift = shift_ref[n]
        for f, raw in enumerate(unpacked(window(ring_far.at[0], by_end(-shift, shift)), ghost_first)):
            end_ghosts(f, raw, frac_ref[n])

    def rows_ahead(slot, n):
        for i in range(1, gyn):
            from_near(slot, i).wait_recv()
        for g in range(gyn):
            from_far(slot, 1, g).wait_recv()
        ring_far[1] = circ_far[slot, 1]
        ring_near[...] = circ_near[slot]
        ring_near[gy] = fold[slot, 0]
        shift, shift_next = shift_ref[n], shift_ref[n + 1]
        fraction = frac_ref[n]
        left, right = AHEAD
        ahead = by_end(-shift_next, shift_next)
        outer = window(ring_far.at[0], ahead)
        beyond = window(ring_near, ahead + by_end(shift, -shift))
        inner = unpacked(window(ring_far.at[1], ahead), by_end(2, 3))
        rows_a = unpacked(outer, ghost_first)
        ghost = unpacked([blended_back(x, fraction) for x in beyond], by_end(0, 5))
        mirror = unpacked([blended_out(x, fraction) for x in outer], by_end(3, 2))
        raw = unpacked(beyond, by_end(6, 7))
        raw_left, raw_right = rows8 < by_end(1, 2), rows8 >= by_end(6, 7)
        for f in range(7):
            middle = jnp.where(rows8 < 5, by_end(inner[f], mirror[f]), by_end(rows_a[f], ghost[f]))
            U[f, left] = jnp.where(raw_left, raw[f], middle)
            middle = jnp.where(rows8 < 3, by_end(ghost[f], rows_a[f]), by_end(mirror[f], inner[f]))
            U[f, right] = jnp.where(raw_right, raw[f], middle)

    def ghosts_from_ahead(n):
        for f in range(7):
            end_ghosts(f, by_end(U[f, AHEAD[0]], U[f, AHEAD[1]]), frac_ref[n])

    def minmod(a, b):
        return jnp.maximum(jnp.minimum(a, b), 0.0) + jnp.minimum(jnp.maximum(a, b), 0.0)

    def signal(density, speed, squared):
        total = density + squared
        return jnp.abs(speed) + jnp.abs(total) * lax.rsqrt(total * density)

    def riemann(left, right, normal, wanted):
        dl, vnl, vtl, vsl, btl, bsl = left
        dr, vnr, vtr, vsr, btr, bsr = right
        n2 = normal * normal
        tl = btl * btl + bsl * bsl
        tr = btr * btr + bsr * bsr
        fastest = jnp.maximum(signal(dl, vnl, n2 + tl), signal(dr, vnr, n2 + tr))
        ul = vnl + fastest
        ur = vnr - fastest
        out = {}
        if wanted != (4,):
            al = dl * ul
            ar = dr * ur
        if 0 in wanted:
            out[0] = al + ar
        if 1 in wanted:
            out[1] = (al * vnl + ar * vnr) + ((dl + dr) + (0.5 * (tl + tr) - n2))
        if 2 in wanted:
            out[2] = (al * vtl + ar * vtr) - normal * (btl + btr)
        if 3 in wanted:
            out[3] = (al * vsl + ar * vsr) - normal * (bsl + bsr)
        if 4 in wanted:
            out[4] = (btl * ul + btr * ur) - normal * (vtl + vtr)
        if 5 in wanted:
            out[5] = (bsl * ul + bsr * ur) - normal * (vsl + vsr)
        return out

    def primitives(k, density, mx, my, mz, bz, bx, bx_after, by):
        inverse = 1.0 / density
        Q[0, k] = density
        Q[VX, k] = mx * inverse
        Q[VY, k] = my * inverse
        Q[VZ, k] = mz * inverse
        Q[CX, k] = 0.5 * (bx + row_after(bx, bx_after))
        Q[CY, k] = 0.5 * (by + lane_after(by))
        Q[QBZ, k] = bz

    def initial_primitives(k):
        primitives(k, *(U[f, k] for f in (D, MX, MY, MZ, BZ, BX)), U[BX, following(k)], U[BY, k])

    X_STATE = (0, VX, VY, VZ, CY, QBZ)
    Y_STATE = (0, VY, VX, VZ, CX, QBZ)

    def finish_fluxes(k, fx, fy, stride, mx, my, cells):
        half = 0.5 * stride
        if 0 in fx:
            for spot, part in enumerate((0, 1, 2, 3, 5)):
                FX[spot, k] = fx[part]
        FY4[k] = fy[4]
        SX4[k] = fx[4] + lane_before(fx[4])
        if cells:
            for spot, (field, px, py) in enumerate(((D, 0, 0), (MX, 1, 2), (MY, 2, 1), (MZ, 3, 3), (BZ, 5, 5))):
                value = U[field, k] - half * ((lane_after(fy[py]) - fy[py]) - fx[px])
                if field == MX:
                    value += (stride * 2.0 * OMEGA) * my
                if field == MY:
                    value -= (stride * (2.0 - QSHEAR) * OMEGA) * mx
                PART[spot, k] = value

    ALL = (0, 1, 2, 3, 4, 5)

    def first_order(k, stride):
        left = [row_before(Q[i, previous(k)], Q[i, k]) for i in X_STATE]
        fx = riemann(left, [Q[i, k] for i in X_STATE], U[BX, k], ALL)
        right = [Q[i, k] for i in Y_STATE]
        fy = riemann([lane_before(q) for q in right], right, U[BY, k], ALL)
        finish_fluxes(k, fx, fy, stride, U[MX, k], U[MY, k], True)

    def slopes(k):
        for spot, i in enumerate(X_STATE):
            here = Q[i, k]
            gradient = 0.5 * minmod(here - row_before(Q[i, previous(k)], here), row_after(here, Q[i, following(k)]) - here)
            QL[spot, k] = here + gradient
            QR[spot, k] = here - gradient

    def second_order(k, stride, last):
        cells = k < OWN or not last
        x_wanted = ALL if cells or k == ABOVE else (4,)
        y_wanted = ALL if cells else (4,)
        left = [row_before(QL[i, previous(k)], QL[i, k]) for i in range(6)]
        fx = riemann(left, [QR[i, k] for i in range(6)], NBX[k], x_wanted)
        left, right = [], []
        for i in Y_STATE:
            here = Q[i, k]
            behind = here - lane_before(here)
            gradient = 0.5 * minmod(behind, lane_after(behind))
            left.append(lane_before(here + gradient))
            right.append(here - gradient)
        fy = riemann(left, right, NBY[k], y_wanted)
        finish_fluxes(k, fx, fy, stride, M[0, k], M[1, k], cells)

    def corner(k):
        return 0.125 * (FY4[k] + row_before(FY4[previous(k)], FY4[k]) - SX4[k])

    def face_x(k, emf, stride):
        EZ[k] = emf
        return U[BX, k] - stride * (lane_after(emf) - emf)

    def face_y(k, stride):
        emf = EZ[k]
        return U[BY, k] + stride * (row_after(emf, EZ[following(k)]) - emf)

    def cells_of(k, stride):
        return [PART[i, k] - (0.5 * stride) * row_after(FX[i, k], FX[i, following(k)]) for i in range(5)]

    def advance(n, last, ring, ready_primitives=(), ready_fluxes=(), send_edges=None):
        fraction = frac_ref[n]

        def tiles(run):
            for k in ring:
                run(k)

        stride = 0.5 * TIMESTEP
        for k in ring:
            if k not in ready_primitives:
                initial_primitives(k)
        for k in ring:
            if k not in ready_fluxes:
                first_order(k, stride)

        def predicted_x(k):
            NBX[k] = face_x(k, corner(k), stride)

        tiles(predicted_x)

        def predicted_cells(k):
            density, mx, my, mz, bz = cells_of(k, stride)
            by = face_y(k, stride)
            NBY[k] = by
            M[0, k] = mx
            M[1, k] = my
            primitives(k, density, mx, my, mz, bz, NBX[k], NBX[following(k)], by)

        tiles(predicted_cells)

        tiles(slopes)
        if not last:
            tiles(lambda k: second_order(k, TIMESTEP, False))
        def new_cells(k):
            for field, value in zip((D, MX, MY, MZ, BZ), cells_of(k, TIMESTEP)):
                U[field, k] = value
            U[BY, k] = face_y(k, TIMESTEP)

        if ring == AHEAD:
            left, right = AHEAD
            emf_l, emf_r = corner(left), corner(right)
            from_low = blended(roll(emf_r, -6, 0), fraction, 1)
            from_high = blended(roll(emf_l, -2, 0), fraction, -1)
            remote = jnp.where(at_low, from_low, from_high)
            emf_r = jnp.where(first_row, 0.5 * (emf_r + remote), emf_r)
            U[BX, left] = face_x(left, emf_l, TIMESTEP)
            U[BX, right] = face_x(right, emf_r, TIMESTEP)
            tiles(new_cells)
            return
        kept = range(OWN) if last else ring

        def mended(emf, remote_row, towards, ours):
            remote = blended(remote_row, fraction, towards)
            return jnp.where(jnp.logical_and(first_row, ours), 0.5 * (emf + remote), emf)

        def fixed_corners(ks):
            emfs = {k: corner(k) for k in ks}
            if 0 in ks:
                emfs[0] = mended(emfs[0], roll(emfs[BELOW], -1, 0), -1, at_low)
                emfs[ABOVE] = mended(emfs[ABOVE], roll(emfs[ABOVE], -6, 0), 1, at_high)
            return emfs

        if not last:
            emfs = fixed_corners(ring)
        else:
            early, late = (0, OWN - 1, ABOVE, BELOW), range(1, OWN - 1)
            for k in early:
                second_order(k, TIMESTEP, True)
            emfs = fixed_corners(early)
            new_bx = {k: face_x(k, emfs[k], TIMESTEP) for k in early}

            def edge_tiles(k):
                density, mx, my, mz, bz = cells_of(k, TIMESTEP)
                return [density, mx, my, mz, new_bx[k], face_y(k, TIMESTEP), bz]

            send_edges(edge_tiles)
            for k in late:
                second_order(k, TIMESTEP, True)
            emfs.update({k: corner(k) for k in (*late, OWN - 1)})
        for k in kept:
            U[BX, k] = face_x(k, emfs[k], TIMESTEP)
        for k in ring:
            if k not in kept:
                EZ[k] = emfs[k]
        for k in kept:
            new_cells(k)

    rounds = STEPS // 2

    def two_steps(r, carry):
        slot = lax.rem(r, 2)

        for k in range(OWN - 1):
            initial_primitives(k)
        for k in range(1, OWN - 1):
            first_order(k, 0.5 * TIMESTEP)

        rows_arrived(slot)
        ghosts_of_neighbours(slot)

        @pl.when(at_end)
        def _():
            ghosts_of_far_end(slot, 2 * r)

        advance(2 * r, False, MAIN, tuple(range(OWN - 1)), tuple(range(1, OWN - 1)))

        @pl.when(at_end)
        def _():
            rows_ahead(slot, 2 * r)
            advance(2 * r, False, AHEAD)
            ghosts_from_ahead(2 * r + 1)
            far_sent(slot)

        rows_sent(slot)

        def send_edges(edge_tiles):
            @pl.when(r < rounds - 1)
            def _():
                pack_edges(1 - slot, edge_tiles(0), edge_tiles(OWN - 1))
                start_exchange(1 - slot, True)

        advance(2 * r + 1, True, MAIN, send_edges=send_edges)
        return carry

    lax.fori_loop(0, rounds, two_steps, 0)

    flat = U[:, 0:OWN].reshape(7 * OWN * 8, LANES)
    out = permuted(flat, permutation[0:256], 1).reshape(7, 8 * OWN, 256)
    den_out[...] = out[D]
    mom_out[...] = out[MX : MZ + 1]
    mag_out[...] = out[BX : BZ + 1]


def store_kernel(den, mom, mag, den_out, mom_out, mag_out, sem):
    copies = [pltpu.make_async_copy(a, b, sem.at[i]) for i, (a, b) in enumerate(((den, den_out), (mom, mom_out), (mag, mag_out)))]
    for copy in copies:
        copy.start()
    for copy in copies:
        copy.wait()


def scratch(gyn):
    tile = (TILES, 8, LANES)
    f32 = jnp.float32
    vmem = lambda *shape: pltpu.VMEM(shape, f32)
    dma = pltpu.SemaphoreType.DMA
    return [
        vmem(7, *tile), vmem(7, *tile), vmem(2, *tile), vmem(6, *tile), vmem(6, *tile), vmem(5, *tile), vmem(5, *tile),
        vmem(*tile), vmem(*tile), vmem(*tile), vmem(*tile), vmem(*tile),
        vmem(2, 2, GROUPS, 3, 3, 8, 128), vmem(2, 2, GROUPS, 3, 3, 8, 128), vmem(2, GROUPS, 2, 3, 8, 128),
        vmem(7, OWN, 8, 256), vmem(2, GROUPS, gyn, 2, 3, 8, 128), vmem(2, gyn, 2, 3, 8, 128),
        vmem(GROUPS, gyn, 2, 3, 8, 128), vmem(gyn, 2, 3, 8, 128), vmem(2, 4, OWN, 8, 128), vmem(4, OWN, 8, 128), vmem(4, OWN, 8, 128), vmem(7, OWN, 8, 128),
        pltpu.SMEM((STEPS,), jnp.int32), pltpu.SMEM((STEPS,), f32), dma((5,)),
        dma((2,)), dma((2,)), dma((2,)), dma((2, 2)),
        dma((GROUPS, gyn)), dma((2, GROUPS, gyn)), dma((gyn,)), dma((2, gyn)),
    ]


def solution(mesh):
    gxn, gyn = mesh.shape["gx"], mesh.shape["gy"]

    def per_device(density, momentum, magnetic, shear_shift, shear_frac):
        state = pl.pallas_call(
            functools.partial(kernel, gxn, gyn),
            name="shearing_box",
            out_shape=tuple(jax.ShapeDtypeStruct(a.shape, jnp.float32) for a in (density, momentum, magnetic)),
            in_specs=[pl.BlockSpec(memory_space=pl.ANY)] * 5,
            out_specs=tuple(pl.BlockSpec(memory_space=pltpu.VMEM) for _ in range(3)),
            scratch_shapes=scratch(gyn),
            compiler_params=pltpu.CompilerParams(
                collective_id=0, has_side_effects=True, vmem_limit_bytes=48 * 1024 * 1024
            ),
        )(
            shear_shift,
            shear_frac,
            density.reshape(OWN, 8, 256),
            momentum.reshape(3, OWN, 8, 256),
            magnetic.reshape(3, OWN, 8, 256),
        )
        return pl.pallas_call(
            store_kernel,
            name="store",
            out_shape=tuple(jax.ShapeDtypeStruct(a.shape, jnp.float32) for a in (density, momentum, magnetic)),
            in_specs=[pl.BlockSpec(memory_space=pltpu.VMEM)] * 3,
            out_specs=tuple(pl.BlockSpec(memory_space=pl.ANY) for _ in range(3)),
            scratch_shapes=[pltpu.SemaphoreType.DMA((3,))],
            compiler_params=pltpu.CompilerParams(vmem_limit_bytes=48 * 1024 * 1024),
        )(*state)

    return jax.shard_map(
        per_device,
        mesh=mesh,
        in_specs=(P("gx", "gy"), P(None, "gx", "gy"), P(None, "gx", "gy"), P(), P()),
        out_specs=(P("gx", "gy"), P(None, "gx", "gy"), P(None, "gx", "gy")),
        check_vma=False,
    )
```
